32 devices in a mesh: dp: 2 (over x), fsdp: 16 (over z, y, core).
Axes of the slice: x: 2, y: 2, z: 4, core: 2. Of those that a mesh axis runs over, the one named last changes fastest.
Arguments:
- tokens: bfloat16 [16384, 768], P(('dp', 'fsdp')), may hold values from -6 to 6
- cotangent: bfloat16 [16384, 768], P(('dp', 'fsdp')), may hold values from -6 to 6
- image_ids: int32 [16384], P(('dp', 'fsdp')), may hold values from 0 to 2, as said below
- in_weight: float32 [768, 5376], P('fsdp'), may hold values from -0.21875 to 0.21875
- out_weight: float32 [3840, 768], P('fsdp'), may hold values from -1.5 to 1.5
- vectors: float32 [4, 768], P(None, 'fsdp'), may hold values from -1.5 to 1.5
- in_moment: float32 [768, 5376], P('fsdp'), may hold values from -0.66 to 0.66
- out_moment: float32 [3840, 768], P('fsdp'), may hold values from -0.66 to 0.66
- vec_moment: float32 [4, 768], P(None, 'fsdp'), may hold values from -0.66 to 0.66
- in_second: float32 [768, 5376], P('fsdp'), may hold values from 0.01 to 0.1
- out_second: float32 [3840, 768], P('fsdp'), may hold values from 0.01 to 0.1
- vec_second: float32 [4, 768], P(None, 'fsdp'), may hold values from 0.01 to 0.1
Outputs:
- activations: bfloat16 [16384, 768], P(('dp', 'fsdp'))
- input_grad: float32 [16384, 768], P(('dp', 'fsdp'))
- in_grad: float32 [768, 5376], P('fsdp')
- out_grad: float32 [3840, 768], P('fsdp')
- vec_grad: float32 [4, 768], P(None, 'fsdp')
- grad_norm: float32 [], replicated
- in_update: float32 [768, 5376], P('fsdp')
- out_update: float32 [3840, 768], P('fsdp')
- vec_update: float32 [4, 768], P(None, 'fsdp')
- in_mean: float32 [768, 5376], P('fsdp')
- out_mean: float32 [3840, 768], P('fsdp')
- vec_mean: float32 [4, 768], P(None, 'fsdp')
- in_square: float32 [768, 5376], P('fsdp')
- out_square: float32 [3840, 768], P('fsdp')
- vec_square: float32 [4, 768], P(None, 'fsdp')
The draws below stay inside these ranges and needn't reach their ends.
Inputs may be any that keep to these rules, and one draw needn't show every extreme that they name: `image_ids`: tokens of one image all lie within one device's 512 rows, and ids never decrease along a device's rows. One eighth of the devices each hold a single image of 512 tokens with id 0; every other device holds images of 196 tokens numbered 0, 1, 2, ... followed by one shorter image.
All inputs are finite; a program needn't handle non-finite values.
Results may differ from the reference program's by a relative error of at most 0.02.
Values may be sent and summed in bfloat16 or wider, within the bound.
No kernel may reach another device: no remote copies, remote signals or barrier semaphores. Data moves between devices by JAX's collectives and lax.ppermute only.
A program may use at most 128 MiB of HBM per device.

```python
import math
import jax
import jax.numpy as jnp
from jax import lax

D = 768
H = 12
HD = 64
FF = 3072
TOK_DEV = 512
SMALL_LEN = 196
ADAM_STEP = 10
TOKENS = 16384
PARAMS = 7080960
N_DP = 2
N_FSDP = 16


def draw_image_ids(key, part):
    device_count = N_DP * N_FSDP
    order = jax.random.permutation(key, device_count)
    single = order < max(1, device_count // 8)
    position = jnp.arange(TOK_DEV, dtype=jnp.int32)
    local = position // SMALL_LEN
    return jnp.where(single[:, None], 0, local[None, :]).astype(jnp.int32).reshape(-1)


def draw_out_weight(key, part):
    noise = jnp.clip(jax.random.normal(key, (D + FF, D), jnp.float32), -6.0, 6.0)
    row_index = jnp.arange(D + FF)[:, None]
    factor = jnp.where(row_index < D, 0.25, FF ** (-0.5))
    return noise * factor


def draw_vectors(key, part):
    gains = jax.random.uniform(key, (3, D), jnp.float32, 0.5, 1.5)
    offset = 0.5 * jax.random.normal(jax.random.fold_in(key, 7), (1, D), jnp.float32)
    return jnp.concatenate([gains, jnp.clip(offset, -1.5, 1.5)], axis=0)


def block_scale(own_key, shape, split, low, top_value):
    level = 1.0
    for dim, parts in split:
        draws = jax.random.uniform(jax.random.fold_in(jax.random.fold_in(own_key, 6), dim), (parts,), jnp.float32, low / len(split), top_value / len(split))
        level = level * jnp.repeat(jnp.exp(draws), shape[dim] // parts).reshape((-1,) + (1,) * (len(shape) - 1 - dim))
    return level


def gaussian(key, extent, scale, bound, shards=(), kind=jnp.bfloat16):
    values = scale * jax.random.normal(key, extent, jnp.float32)
    if shards:
        values = values * block_scale(key, extent, shards, -0.22, 0.18)
    return jnp.clip(values, -bound, bound).astype(kind)


def setup_inputs(seed: int = 0) -> dict:
    keys = jax.random.split(jax.random.key(seed), 13)
    tokens = gaussian(keys[0], (TOKENS, D), 1.0, 6.0, ((0, 32),))
    cotangent = gaussian(keys[1], (TOKENS, D), 1.0, 6.0, ((0, 32),))
    image_ids = draw_image_ids(jax.random.fold_in(keys[12], 71), 0)
    in_weight = gaussian(keys[3], (D, 3 * D + FF), D ** -0.5, 0.21875, ((0, 16),), jnp.float32)
    out_weight = draw_out_weight(jax.random.fold_in(keys[12], 71), 0)
    vectors = draw_vectors(jax.random.fold_in(keys[12], 71), 0)
    in_moment = gaussian(keys[6], (D, 3 * D + FF), 0.11, 0.66, ((0, 16),), jnp.float32)
    out_moment = gaussian(keys[7], (D + FF, D), 0.11, 0.66, ((0, 16),), jnp.float32)
    vec_moment = gaussian(keys[8], (4, D), 0.11, 0.66, ((1, 16),), jnp.float32)
    in_second = jnp.clip(jnp.exp(math.log(0.1) - 2.3025851 * jax.random.uniform(keys[9], (D, 3 * D + FF), jnp.float32) ** block_scale(keys[9], (D, 3 * D + FF), ((0, 16),), -0.2, 0.2)), 0.01, 0.1)
    out_second = jnp.clip(jnp.exp(math.log(0.1) - 2.3025851 * jax.random.uniform(keys[10], (D + FF, D), jnp.float32) ** block_scale(keys[10], (D + FF, D), ((0, 16),), -0.2, 0.2)), 0.01, 0.1)
    vec_second = jnp.clip(jnp.exp(math.log(0.1) - 2.3025851 * jax.random.uniform(keys[11], (4, D), jnp.float32) ** block_scale(keys[11], (4, D), ((1, 16),), -0.2, 0.2)), 0.01, 0.1)
    return {"tokens": tokens, "cotangent": cotangent, "image_ids": image_ids, "in_weight": in_weight, "out_weight": out_weight, "vectors": vectors, "in_moment": in_moment, "out_moment": out_moment, "vec_moment": vec_moment, "in_second": in_second, "out_second": out_second, "vec_second": vec_second}


highest = lax.Precision.HIGHEST
beta_one = 0.9
beta_two = 0.95
learning = 0.03
decay_rate = 0.1
epsilon = 1e-08
norm_eps = 1e-06
masked = -1e+30

@jax.custom_vjp
def low(v):
    return lax.optimization_barrier(v.astype(jnp.bfloat16)).astype(jnp.float32)

@jax.custom_vjp
def low_back(v):
    return v

def low_keep(v):
    return (low(v), None)

def low_pass(kept, grad):
    return (grad,)

def back_keep(v):
    return (v, None)

def back_low(kept, grad):
    return (low(grad),)
low.defvjp(low_keep, low_pass)
low_back.defvjp(back_keep, back_low)

def row_norm(values):
    centre = values - lax.optimization_barrier(jnp.mean(values, axis=-1, keepdims=True))
    spread = lax.optimization_barrier(jnp.mean(centre * centre, axis=-1, keepdims=True))
    return centre * lax.rsqrt(spread + norm_eps)

def head_norm(raw, gain, factor):
    heads = raw.reshape(raw.shape[0], H, HD)
    return row_norm(heads) * gain.reshape(H, HD) * factor

def device_block(weights, rows, id_rows):
    in_low, out_low, vec_low = weights
    scaled = low(row_norm(rows) * vec_low[0])
    hidden = low_back(jnp.dot(scaled, in_low, precision=highest))
    query = low(head_norm(hidden[:, :D], vec_low[1], HD ** (-0.5)))
    keyed = low(head_norm(hidden[:, D:2 * D], vec_low[2], 1.0))
    values = low(hidden[:, 2 * D:3 * D]).reshape(-1, H, HD)
    inner = hidden[:, 3 * D:]
    scores = low_back(jnp.einsum('qhd,khd->hqk', query, keyed, precision=highest))
    same = (id_rows[:, None] == id_rows[None, :])[None]
    scores = jnp.where(same, scores, masked)
    probs = low(jax.nn.softmax(scores, axis=-1))
    attended = jnp.einsum('hqk,khd->qhd', probs, values, precision=highest).reshape(-1, D)
    mixed = jnp.concatenate([attended, jax.nn.gelu(inner, approximate=True)], axis=1)
    mixed = low(low_back(mixed))
    return rows + jnp.dot(mixed, out_low, precision=highest) + vec_low[3]

def adamw(master, first, second, grad, factor):
    clipped = grad * factor
    first_new = beta_one * first + (1.0 - beta_one) * clipped
    second_new = beta_two * second + (1.0 - beta_two) * clipped * clipped
    first_hat = first_new / (1.0 - beta_one ** ADAM_STEP)
    second_hat = second_new / (1.0 - beta_two ** ADAM_STEP)
    update = -learning * (first_hat / (jnp.sqrt(second_hat) + epsilon) + decay_rate * master)
    return (update, first_new, second_new)

def reference(tokens, cotangent, image_ids, in_weight, out_weight, vectors, in_moment, out_moment, vec_moment, in_second, out_second, vec_second):
    rows = tokens.astype(jnp.float32)
    groups = rows.shape[0] // TOK_DEV
    id_groups = image_ids.reshape(groups, TOK_DEV)

    def forward(weights, inputs):
        rounded = (low(weights[0]), low(weights[1]), low(weights[2]))

        def per_group(pair):
            return device_block(rounded, pair[0], pair[1])
        outputs = lax.map(jax.checkpoint(per_group), (inputs.reshape(groups, TOK_DEV, D), id_groups))
        return outputs.reshape(-1, D)
    result, pullback = jax.vjp(forward, (in_weight, out_weight, vectors), rows)
    weight_grads, input_grad = pullback(cotangent.astype(jnp.float32))
    in_grad, out_grad, vec_grad = weight_grads
    total = jnp.sum(in_grad * in_grad) + jnp.sum(out_grad * out_grad) + jnp.sum(vec_grad * vec_grad)
    grad_norm = jnp.sqrt(total)
    factor = jnp.minimum(1.0, math.sqrt(PARAMS) / grad_norm)
    in_update, in_mean, in_square = adamw(in_weight, in_moment, in_second, in_grad, factor)
    out_update, out_mean, out_square = adamw(out_weight, out_moment, out_second, out_grad, factor)
    vec_update, vec_mean, vec_square = adamw(vectors, vec_moment, vec_second, vec_grad, factor)
    return (result.astype(jnp.bfloat16), input_grad, in_grad, out_grad, vec_grad, grad_norm, in_update, out_update, vec_update, in_mean, out_mean, vec_mean, in_square, out_square, vec_square)
```

```python
import math

import jax
import jax.numpy as jnp
from jax import lax
from jax.experimental import pallas as pl
from jax.experimental.pallas import tpu as pltpu
from jax.sharding import PartitionSpec as P

D = 768
H = 12
HD = 64
FF = 3072
ADAM_STEP = 10
PARAMS = 7080960

beta_one = 0.9
beta_two = 0.95
learning = 0.03
decay_rate = 0.1
epsilon = 1e-08
norm_eps = 1e-06

F32 = jnp.float32
BF16 = jnp.bfloat16
DH = D // 2
FH = FF // 2
PAIR = 128
PAIRS = DH // PAIR
QKV = 3 * PAIR
QW = PAIRS * QKV
VEC = 128
GELU_C = math.sqrt(2.0 / math.pi)
MIB = 1 << 20

NT = (((1,), (1,)), ((), ()))
TN = (((0,), (0,)), ((), ()))


def mm(a, b, dims=(((1,), (0,)), ((), ()))):
    return lax.dot_general(a, b, dims, preferred_element_type=F32)


class Plan:
    def __init__(self, n_fsdp, n_dp):
        chips = n_fsdp // 2
        self.n, self.n_dp, self.chips = n_fsdp, n_dp, chips
        self.zs = 4 if chips % 4 == 0 else chips
        self.ys = chips // self.zs
        index = lax.axis_index("fsdp")
        self.core = index % 2
        self.y = (index // 2) % self.ys
        self.z = index // (2 * self.ys)
        self.pos = jnp.stack([self.z, self.y, self.core]).astype(jnp.int32)
        self.order = [(t, s) for t in range(self.ys) for s in range(self.zs)]

    def index(self, z, y, core):
        return ((z % self.zs) * self.ys + y % self.ys) * 2 + core

    def all(self):
        return [
            (z, y, c) for z in range(self.zs) for y in range(self.ys) for c in range(2)
        ]

    def from_z(self, a, s):
        pairs = [(self.index(z + s, y, c), self.index(z, y, c)) for z, y, c in self.all()]
        return lax.ppermute(a, "fsdp", pairs)

    def from_y(self, a, t):
        pairs = [(self.index(z, y + t, c), self.index(z, y, c)) for z, y, c in self.all()]
        return lax.ppermute(a, "fsdp", pairs)

    def swap_core(self, a):
        pairs = [(self.index(z, y, c), self.index(z, y, 1 - c)) for z, y, c in self.all()]
        return lax.ppermute(a, "fsdp", pairs)

    def gather(self, piece):
        column = [piece] + [self.from_z(piece, s) for s in range(1, self.zs)]
        out = list(column)
        for t in range(1, self.ys):
            out += [self.from_y(a, t) for a in column]
        return out

    def scatter(self, pieces):
        column = []
        for s in range(self.zs):
            total = pieces[s].astype(F32)
            for t in range(1, self.ys):
                total = total + self.from_y(pieces[t * self.zs + s], -t).astype(F32)
            column.append(total)
        total = column[0]
        for s in range(1, self.zs):
            total = total + self.from_z(column[s].astype(BF16), -s).astype(F32)
        return total

    def over_dp(self, a):
        if self.n_dp == 2:
            other = lax.ppermute(a, "dp", [(0, 1), (1, 0)])
            return a.astype(F32) + other.astype(F32)
        return lax.psum(a.astype(F32), "dp")

    def total(self, a):
        m = 1
        while m < self.n:
            a = a + lax.ppermute(a, "fsdp", [(i, i ^ m) for i in range(self.n)])
            m *= 2
        return a

    def row(self, pos_ref, t, s, rows):
        z = lax.rem(pos_ref[0] + s, self.zs)
        y = lax.rem(pos_ref[1] + t, self.ys)
        return pl.multiple_of((z * self.ys + y) * rows, 16)


def smem():
    return pl.BlockSpec(memory_space=pltpu.SMEM)


def whole(shape):
    return pl.BlockSpec(shape, lambda *_: (0,) * len(shape))


def params(mib):
    return pltpu.CompilerParams(
        dimension_semantics=("arbitrary",), vmem_limit_bytes=mib * MIB
    )


def cost(flops, nbytes, exps=0):
    return pl.CostEstimate(flops=int(flops), bytes_accessed=int(nbytes), transcendentals=int(exps))


def place(plan, pos_ref, refs, rows, out_ref):
    for (t, s), ref in zip(plan.order, refs):
        out_ref[pl.ds(plan.row(pos_ref, t, s, rows), rows), :] = ref[...]


def mlp_forward(plan, x_own, xc_other, pieces):
    tok = x_own.shape[0]
    rows = pieces[0].shape[0]
    tile = 512
    n = len(pieces)

    def kernel(pos_ref, xo_ref, xp_ref, *rest):
        refs, (mix_ref, slope_ref, w_ref) = rest[:n], rest[n:]
        place(plan, pos_ref, refs, rows, w_ref)
        for half, x_ref in enumerate((xo_ref, xp_ref)):
            v = mm(x_ref[...], w_ref[...])
            v2 = v * v
            t = jnp.tanh(v * (GELU_C + (GELU_C * 0.044715) * v2))
            h = 0.5 + 0.5 * t
            g = v * h
            slope = h + 2.0 * g * (1.0 - h) * (GELU_C + (3.0 * GELU_C * 0.044715) * v2)
            mix_ref[half] = g.astype(BF16)
            slope_ref[half] = slope.astype(BF16)

    block = pl.BlockSpec((2, tok, tile), lambda j: (0, 0, j))
    return pl.pallas_call(
        kernel,
        grid=(FH // tile,),
        in_specs=[
            smem(),
            whole((tok, D)),
            pl.BlockSpec((tok, D), lambda j: (0, 0)),
        ]
        + [pl.BlockSpec((rows, tile), lambda j: (0, j))] * n,
        out_specs=[block, block],
        out_shape=[jax.ShapeDtypeStruct((2, tok, FH), BF16)] * 2,
        scratch_shapes=[pltpu.VMEM((D, tile), BF16)],
        compiler_params=params(40),
        cost_estimate=cost(4 * tok * D * FH, 12 * tok * FH, 2 * tok * FH),
        name="mlp_forward",
    )(plan.pos, x_own, xc_other, *pieces)


def head_means(a, block_ref):
    high = a.astype(BF16)
    low = (a - high.astype(F32)).astype(BF16)
    return mm(high, block_ref[...]) + mm(low, block_ref[...])


def attention_forward(plan, x_own, xc_other, pieces, id_row, id_col, block):
    tok = x_own.shape[0]
    rows = pieces[0].shape[0]
    n = len(pieces)

    def kernel(pos_ref, xo_ref, xp_ref, idr_ref, idc_ref, block_ref, *rest):
        refs, vec_refs = rest[:n], rest[n : 2 * n]
        (
            q_ref, k_ref, v_ref, nq_ref, nk_ref, rq_ref, rk_ref, att_ref, p_ref, gain_ref,
            w_ref, vs_ref,
        ) = rest[2 * n :]
        step = pl.program_id(0)

        @pl.when(step == 0)
        def _():
            place(plan, pos_ref, vec_refs, rows, vs_ref)
            gain_ref[...] = vs_ref[...].astype(F32).T[:8]

        place(plan, pos_ref, refs, rows, w_ref)
        column = pl.ds(pl.multiple_of(pos_ref[2] * DH + step * PAIR, PAIR), PAIR)
        q_gain = gain_ref[0:1, column] * (HD ** (-0.5))
        k_gain = gain_ref[1:2, column]
        lane = lax.broadcasted_iota(jnp.int32, (tok, PAIR), 1)
        first = lane < HD
        for half, x_ref in enumerate((xo_ref, xp_ref)):
            raw = mm(x_ref[...], w_ref[...])

            def normed(a, gain, n_ref, r_ref, out_ref):
                centre = a - head_means(a, block_ref)
                r = lax.rsqrt(head_means(centre * centre, block_ref) + norm_eps)
                normal = centre * r
                n_ref[half] = normal.astype(BF16)
                r_ref[half] = r.astype(BF16)
                low = (normal * gain).astype(BF16)
                out_ref[half] = low
                return low

            q = normed(raw[:, :PAIR], q_gain, nq_ref, rq_ref, q_ref)
            k = normed(raw[:, PAIR : 2 * PAIR], k_gain, nk_ref, rk_ref, k_ref)
            v = raw[:, 2 * PAIR :].astype(BF16)
            v_ref[half] = v
            same = idc_ref[half] == idr_ref[half]
            att = []
            zero = jnp.zeros_like(q)
            for head in range(2):
                qh = jnp.where(first, q, zero) if head == 0 else jnp.where(first, zero, q)
                e = jnp.where(same, jnp.exp(mm(qh, k, NT)), 0.0)
                p = (e * (1.0 / jnp.sum(e, axis=1, keepdims=True))).astype(BF16)
                p_ref[half, head] = p
                att.append(mm(p, v))
            att_ref[half] = jnp.where(first, att[0], att[1]).astype(BF16)

    pair = pl.BlockSpec((2, tok, PAIR), lambda j: (0, 0, j))
    small = jax.ShapeDtypeStruct((2, tok, DH), BF16)
    return pl.pallas_call(
        kernel,
        grid=(PAIRS,),
        in_specs=[
            smem(),
            whole((tok, D)),
            pl.BlockSpec((tok, D), lambda j: (0, 0)),
            whole((2, 1, tok)),
            whole((2, tok, 1)),
            whole((PAIR, PAIR)),
        ]
        + [pl.BlockSpec((rows, QKV), lambda j: (0, j))] * n
        + [pl.BlockSpec((rows, VEC), lambda j: (0, QW // VEC))] * n,
        out_specs=[pair] * 8
        + [pl.BlockSpec((2, 2, tok, tok), lambda j: (0, j, 0, 0)), whole((8, D))],
        out_shape=[small] * 8
        + [
            jax.ShapeDtypeStruct((2, 2 * PAIRS, tok, tok), BF16),
            jax.ShapeDtypeStruct((8, D), F32),
        ],
        scratch_shapes=[pltpu.VMEM((D, QKV), BF16), pltpu.VMEM((D, VEC), BF16)],
        compiler_params=params(48),
        cost_estimate=cost(4 * tok * D * QW, 20 * MIB, 12 * tok * tok),
        name="attention_forward",
    )(plan.pos, x_own, xc_other, id_row, id_col, block, *pieces, *pieces)


def output_step(plan, att, mixed, slope, cot_own, xc_other, w_own, w_other):
    tok = cot_own.shape[0]
    rows = w_own.shape[0] // plan.chips
    tile = DH
    steps = 1 + FH // tile

    def kernel(
        pos_ref, att_ref, mix_ref, slope_ref, co_ref, cp_ref, wo_ref, wp_ref,
        out_own_ref, out_other_ref, d_att_ref, d_in_ref, g_own_ref, g_other_ref,
        w_ref, acc_ref, cot_ref,
    ):
        step = pl.program_id(0)
        core = pos_ref[2]
        own = pl.ds(pl.multiple_of(core * DH, DH), DH)
        other = pl.ds(pl.multiple_of((1 - core) * DH, DH), DH)

        @pl.when(step == 0)
        def _():
            for i, (t, s) in enumerate(plan.order):
                at = pl.ds(plan.row(pos_ref, t, s, rows), rows)
                w_ref[at, own] = wo_ref[i * rows : (i + 1) * rows, :]
                w_ref[at, other] = wp_ref[i * rows : (i + 1) * rows, :]
            acc_ref[...] = jnp.zeros_like(acc_ref)
            cot_ref[:tok] = co_ref[...]
            cot_ref[tok:] = cp_ref[...]

        start = jnp.where(step == 0, core * DH, D + core * FH + (step - 1) * tile)
        w = w_ref[pl.ds(pl.multiple_of(start, tile), tile), :]
        m = jnp.where(step == 0, att_ref[...], mix_ref[...]).reshape(2 * tok, tile)
        cot = cot_ref[...]
        acc_ref[...] += mm(m, w)
        d = mm(cot, w, NT)

        @pl.when(step == 0)
        def _():
            d_att_ref[...] = d.astype(BF16).reshape(2, tok, tile)

        slopes = slope_ref[...].reshape(2 * tok, tile).astype(F32)
        d_in_ref[...] = (d * slopes).astype(BF16).reshape(2, tok, tile)
        g_own_ref[...] = mm(m, cot_ref[:, own], TN).astype(BF16)
        g_other_ref[...] = mm(m, cot_ref[:, other], TN).astype(BF16)

        @pl.when(step == steps - 1)
        def _():
            out_own_ref[...] = acc_ref[:tok]
            out_other_ref[...] = acc_ref[tok:].astype(BF16)

    hidden = pl.BlockSpec((2, tok, tile), lambda j: (0, 0, jnp.maximum(j - 1, 0)))
    grad = pl.BlockSpec((tile, DH), lambda j: (j, 0))
    return pl.pallas_call(
        kernel,
        grid=(steps,),
        in_specs=[
            smem(),
            whole((2, tok, tile)),
            hidden,
            hidden,
            whole((tok, D)),
            pl.BlockSpec((tok, D), lambda j: (0, 1)),
            whole(w_own.shape),
            whole(w_other.shape),
        ],
        out_specs=[whole((tok, D)), whole((tok, D)), whole((2, tok, tile)), hidden, grad, grad],
        out_shape=[
            jax.ShapeDtypeStruct((tok, D), F32),
            jax.ShapeDtypeStruct((tok, D), BF16),
            jax.ShapeDtypeStruct((2, tok, DH), BF16),
            jax.ShapeDtypeStruct((2, tok, FH), BF16),
            jax.ShapeDtypeStruct((steps * tile, DH), BF16),
            jax.ShapeDtypeStruct((steps * tile, DH), BF16),
        ],
        scratch_shapes=[
            pltpu.VMEM((D + FF, D), BF16),
            pltpu.VMEM((2 * tok, D), F32),
            pltpu.VMEM((2 * tok, D), BF16),
        ],
        compiler_params=params(56),
        cost_estimate=cost(6 * 2 * tok * steps * tile * D, 30 * MIB),
        name="output_step",
    )(plan.pos, att, mixed, slope, cot_own, xc_other, w_own, w_other)


def turned(plan, pos_ref, xt_ref, xs_ref, rows):
    for i, (t, s) in enumerate(plan.order):
        xs_ref[i * rows : (i + 1) * rows, :] = xt_ref[
            pl.ds(plan.row(pos_ref, t, s, rows), rows), :
        ]


def mlp_backward(plan, xt, d_inner, pieces):
    tok = d_inner.shape[1]
    rows = pieces[0].shape[0]
    n = len(pieces)
    tile = 512
    steps = FH // tile

    def kernel(pos_ref, xt_ref, d_ref, *rest):
        refs, grads = rest[:n], rest[n : 2 * n]
        e_own_ref, e_other_ref, w_ref, xs_ref, acc_ref = rest[2 * n :]
        step = pl.program_id(0)

        @pl.when(step == 0)
        def _():
            turned(plan, pos_ref, xt_ref, xs_ref, rows)
            acc_ref[...] = jnp.zeros_like(acc_ref)

        place(plan, pos_ref, refs, rows, w_ref)
        d = d_ref[...].reshape(2 * tok, tile)
        g = mm(xs_ref[...], d).astype(BF16)
        for i, ref in enumerate(grads):
            ref[...] = g[i * rows : (i + 1) * rows]
        acc_ref[...] += mm(d, w_ref[...], NT)

        @pl.when(step == steps - 1)
        def _():
            e_own_ref[...] = acc_ref[:tok]
            e_other_ref[...] = acc_ref[tok:]

    piece = pl.BlockSpec((rows, tile), lambda j: (0, j))
    out = pl.pallas_call(
        kernel,
        grid=(steps,),
        in_specs=[
            smem(),
            whole((D, 2 * tok)),
            pl.BlockSpec((2, tok, tile), lambda j: (0, 0, j)),
        ]
        + [piece] * n,
        out_specs=[piece] * n + [whole((tok, D))] * 2,
        out_shape=[jax.ShapeDtypeStruct((rows, FH), BF16)] * n
        + [jax.ShapeDtypeStruct((tok, D), F32)] * 2,
        scratch_shapes=[
            pltpu.VMEM((D, tile), BF16),
            pltpu.VMEM((D, 2 * tok), BF16),
            pltpu.VMEM((2 * tok, D), F32),
        ],
        compiler_params=params(48),
        cost_estimate=cost(8 * tok * D * FH, 20 * MIB),
        name="mlp_backward",
    )(plan.pos, xt, d_inner, *pieces)
    return out[:n], out[n], out[n + 1]


def attention_backward(plan, xt, saved, d_att, block, gains, pieces, e_own, e_other):
    q, k, v, nq, nk, rq, rk, probs = saved
    tok = d_att.shape[1]
    rows = pieces[0].shape[0]
    n = len(pieces)

    def kernel(pos_ref, xt_ref, q_ref, k_ref, v_ref, nq_ref, nk_ref, rq_ref, rk_ref, p_ref,
               da_ref, block_ref, gain_ref, ein_own_ref, ein_other_ref, *rest):
        refs, grads = rest[:n], rest[n : 2 * n]
        e_own_ref, e_other_ref, gg_ref, w_ref, xs_ref, d_ref = rest[2 * n :]
        step = pl.program_id(0)

        @pl.when(step == 0)
        def _():
            turned(plan, pos_ref, xt_ref, xs_ref, rows)
            e_own_ref[...] = ein_own_ref[...]
            e_other_ref[...] = ein_other_ref[...]

        place(plan, pos_ref, refs, rows, w_ref)
        column = pl.ds(pl.multiple_of(pos_ref[2] * DH + step * PAIR, PAIR), PAIR)
        q_gain = gain_ref[0:1, column]
        k_gain = gain_ref[1:2, column]
        first = lax.broadcasted_iota(jnp.int32, (tok, PAIR), 1) < HD
        sums = [jnp.zeros((1, PAIR), F32), jnp.zeros((1, PAIR), F32)]
        for half in range(2):
            qb, kb, vb, da = q_ref[half], k_ref[half], v_ref[half], da_ref[half]
            q_t, da_t = qb.T, da.T
            zero = jnp.zeros_like(da)
            dq, dk_t, dv_t = [], [], []
            for head in range(2):
                at = slice(head * HD, (head + 1) * HD)
                dah = jnp.where(first, da, zero) if head == 0 else jnp.where(first, zero, da)
                p_low = p_ref[half, head]
                p = p_low.astype(F32)
                t = p * mm(dah, vb, NT)
                ds = (t - p * jnp.sum(t, axis=1, keepdims=True)).astype(BF16)
                dv_t.append(mm(da_t[at], p_low))
                dk_t.append(mm(q_t[at], ds))
                dq.append(mm(ds, kb))
            d_query = jnp.where(first, dq[0], dq[1])
            d_key = jnp.concatenate(dk_t, axis=0).T
            d_value = jnp.concatenate(dv_t, axis=0).T

            def back(d, gain, n_ref, r_ref, which, factor):
                normal = n_ref[half].astype(F32)
                d = d * factor
                sums[which] = sums[which] + jnp.sum(d * normal, axis=0, keepdims=True)
                e = d * gain
                mean = head_means(e, block_ref)
                along = head_means(e * normal, block_ref)
                return (r_ref[half].astype(F32) * (e - mean - normal * along)).astype(BF16)

            at = slice(half * tok, (half + 1) * tok)
            d_ref[at, :PAIR] = back(d_query, q_gain, nq_ref, rq_ref, 0, HD ** (-0.5))
            d_ref[at, PAIR : 2 * PAIR] = back(d_key, k_gain, nk_ref, rk_ref, 1, 1.0)
            d_ref[at, 2 * PAIR :] = d_value.astype(BF16)
        gg_ref[...] = jnp.concatenate(sums + [jnp.zeros((6, PAIR), F32)], axis=0)
        g = mm(xs_ref[...], d_ref[...]).astype(BF16)
        for i, ref in enumerate(grads):
            ref[...] = g[i * rows : (i + 1) * rows]
        e_own_ref[...] += mm(d_ref[:tok], w_ref[...], NT)
        e_other_ref[...] += mm(d_ref[tok:], w_ref[...], NT)

    piece = pl.BlockSpec((rows, QKV), lambda j: (0, j))
    pair = pl.BlockSpec((2, tok, PAIR), lambda j: (0, 0, j))
    out = pl.pallas_call(
        kernel,
        grid=(PAIRS,),
        in_specs=[smem(), whole((D, 2 * tok))]
        + [pair] * 7
        + [
            pl.BlockSpec((2, 2, tok, tok), lambda j: (0, j, 0, 0)),
            pair,
            whole((PAIR, PAIR)),
            whole((8, D)),
            whole((tok, D)),
            whole((tok, D)),
        ]
        + [piece] * n,
        out_specs=[piece] * n
        + [whole((tok, D))] * 2
        + [pl.BlockSpec((8, PAIR), lambda j: (0, j))],
        out_shape=[jax.ShapeDtypeStruct((rows, QW), BF16)] * n
        + [jax.ShapeDtypeStruct((tok, D), F32)] * 2
        + [jax.ShapeDtypeStruct((8, DH), F32)],
        scratch_shapes=[
            pltpu.VMEM((D, QKV), BF16),
            pltpu.VMEM((D, 2 * tok), BF16),
            pltpu.VMEM((2 * tok, QKV), BF16),
        ],
        compiler_params=params(56),
        cost_estimate=cost(8 * tok * D * QW, 20 * MIB),
        name="attention_backward",
    )(plan.pos, xt, q, k, v, nq, nk, rq, rk, probs, d_att, block, gains, e_own, e_other, *pieces)
    return out[:n], out[n], out[n + 1], out[n + 2]


def row_stats(rows):
    centre = rows - jnp.mean(rows, axis=-1, keepdims=True)
    r = lax.rsqrt(jnp.mean(centre * centre, axis=-1, keepdims=True) + norm_eps)
    return centre * r, r


def adamw(master, first, second, grad, factor):
    clipped = grad * factor
    first_new = beta_one * first + (1.0 - beta_one) * clipped
    second_new = beta_two * second + (1.0 - beta_two) * clipped * clipped
    first_hat = first_new / (1.0 - beta_one**ADAM_STEP)
    second_hat = second_new / (1.0 - beta_two**ADAM_STEP)
    update = -learning * (first_hat / (jnp.sqrt(second_hat) + epsilon) + decay_rate * master)
    return (update, first_new, second_new)


def pick(a, index, axis):
    return lax.dynamic_index_in_dim(a, index, axis, keepdims=False)


def both(core, own, other, axis):
    return jnp.concatenate(
        [jnp.where(core == 0, own, other), jnp.where(core == 0, other, own)], axis=axis
    )


def local(
    tokens,
    cotangent,
    image_ids,
    in_weight,
    out_weight,
    vectors,
    in_moment,
    out_moment,
    vec_moment,
    in_second,
    out_second,
    vec_second,
):
    plan = Plan(lax.axis_size("fsdp"), lax.axis_size("dp"))
    core = plan.core
    tok = tokens.shape[0]
    rows = in_weight.shape[0]
    out_rows = out_weight.shape[0]

    low_in = in_weight.astype(BF16)
    low_out = out_weight.astype(BF16)
    low_vec = vectors.astype(BF16)
    gain = low_vec[0].astype(F32)[:, None]
    scaled_in = (low_in.astype(F32) * gain).astype(BF16)
    qkv_all = scaled_in[:, : 3 * D].reshape(rows, 3, 2, PAIRS, PAIR)
    mlp_all = scaled_in[:, 3 * D :].reshape(rows, 2, FH)
    vec_cols = jnp.pad(low_vec[1:].T, ((0, 0), (0, VEC - 3)))

    def qkv_of(c):
        part = pick(qkv_all, c, 2).transpose(0, 2, 1, 3).reshape(rows, QW)
        return jnp.concatenate([part, vec_cols], axis=1)

    def joined(own, other_wants):
        return both(core, own, plan.swap_core(other_wants), 0)

    mlp_piece = joined(pick(mlp_all, core, 1), pick(mlp_all, 1 - core, 1))
    qkv_piece = joined(qkv_of(core), qkv_of(1 - core))
    out_all = low_out.reshape(out_rows, 2, DH)
    out_piece = joined(pick(out_all, core, 1), pick(out_all, 1 - core, 1))

    normal, _ = row_stats(tokens.astype(F32))
    x_own = normal.astype(BF16)
    xc_other = plan.swap_core(jnp.concatenate([x_own, cotangent], axis=1))
    ids_other = plan.swap_core(image_ids)
    ids = jnp.stack([image_ids, ids_other])
    xt = jnp.concatenate([x_own, xc_other[:, :D]], axis=0).T
    lane = jnp.arange(PAIR) // HD
    block = jnp.where(lane[:, None] == lane[None, :], 1.0 / HD, 0.0).astype(BF16)

    mlp_pieces = plan.gather(mlp_piece)
    qkv_pieces = plan.gather(qkv_piece)
    out_pieces = plan.gather(out_piece)

    mixed, slope = mlp_forward(plan, x_own, xc_other, mlp_pieces)
    *saved, att, probs, gains = attention_forward(
        plan, x_own, xc_other, qkv_pieces, ids[:, None, :], ids[:, :, None], block
    )
    w_own = jnp.concatenate(out_pieces, axis=0)
    w_other = plan.swap_core(w_own)
    out_own, out_other, d_att, d_inner, g_own, g_other = output_step(
        plan, att, mixed, slope, cotangent, xc_other, w_own, w_other
    )
    out_recv = plan.swap_core(out_other)
    result = (
        tokens.astype(F32) + out_own + out_recv.astype(F32) + gains[2][None, :]
    ).astype(BF16)

    g_recv = plan.swap_core(g_other)
    full = jnp.concatenate(
        [both(core, g_own[:DH], g_recv[:DH], 0), both(core, g_own[DH:], g_recv[DH:], 0)], axis=0
    ).reshape(plan.zs, plan.ys, 2 * out_rows, DH)
    parts = [
        lax.dynamic_slice(
            full,
            ((plan.z + s) % plan.zs, (plan.y + t) % plan.ys, 0, 0),
            (1, 1, 2 * out_rows, DH),
        )[0, 0]
        for t, s in plan.order
    ]
    out_sum = plan.scatter(parts)

    mlp_grads, e_own, e_other = mlp_backward(plan, xt, d_inner, mlp_pieces)
    mlp_sum = plan.scatter(mlp_grads)
    qkv_grads, e_own, e_other, gain_grads = attention_backward(
        plan, xt, tuple(saved) + (probs,), d_att, block, gains, qkv_pieces, e_own, e_other
    )
    half = jnp.zeros((2, DH), F32)
    cot_sum = jnp.sum(cotangent.astype(F32), axis=0)
    head_rows = jnp.zeros((2, D), F32)
    head_rows = lax.dynamic_update_slice(head_rows, gain_grads[:2], (0, core * DH))
    vec_rows = jnp.concatenate([head_rows, cot_sum[None]], axis=0)
    vec_local = jnp.pad(vec_rows.T, ((0, 0), (0, VEC - 3))).astype(BF16)
    vec_local = vec_local.reshape(plan.zs, plan.ys, 2 * rows, VEC)
    vec_parts = [
        lax.dynamic_slice(
            vec_local,
            ((plan.z + s) % plan.zs, (plan.y + t) % plan.ys, 0, 0),
            (1, 1, 2 * rows, VEC),
        )[0, 0]
        for t, s in plan.order
    ]
    qkv_sum = plan.scatter(
        [jnp.concatenate([a, b], axis=1) for a, b in zip(qkv_grads, vec_parts)]
    )

    e_recv = plan.swap_core(e_other.astype(BF16))
    e = e_own + e_recv.astype(F32)
    normal, r = row_stats(tokens.astype(F32))
    mean = jnp.mean(e, axis=-1, keepdims=True)
    along = jnp.mean(e * normal, axis=-1, keepdims=True)
    input_grad = cotangent.astype(F32) + r * (e - mean - normal * along)

    def finish(total, count):
        total = total.astype(BF16)
        own = lax.dynamic_slice_in_dim(total, core * count, count, 0)
        other = plan.swap_core(lax.dynamic_slice_in_dim(total, (1 - core) * count, count, 0))
        return plan.over_dp(own), plan.over_dp(other)

    out_grad = both(core, *finish(out_sum, out_rows), 1)
    mlp_hat = both(core, *finish(mlp_sum, rows), 1)
    qkv_own, qkv_other = finish(qkv_sum, rows)
    qkv_hat = jnp.stack(
        [
            jnp.where(core == 0, qkv_own[:, :QW], qkv_other[:, :QW]),
            jnp.where(core == 0, qkv_other[:, :QW], qkv_own[:, :QW]),
        ],
        axis=1,
    )
    qkv_hat = (
        qkv_hat.reshape(rows, 2, PAIRS, 3, PAIR).transpose(0, 3, 1, 2, 4).reshape(rows, 3 * D)
    )
    hat = jnp.concatenate([qkv_hat, mlp_hat], axis=1)
    in_grad = hat * gain
    gain_grad = jnp.sum(hat * low_in.astype(F32), axis=1)
    vec_tail = (qkv_own[:, QW:] + qkv_other[:, QW:])[:, :3].T
    vec_grad = jnp.concatenate([gain_grad[None], vec_tail], axis=0)

    square = (
        jnp.sum(in_grad * in_grad) + jnp.sum(out_grad * out_grad) + jnp.sum(vec_grad * vec_grad)
    )
    total = plan.total(jnp.full((8, 128), square, F32))[0, 0]
    grad_norm = jnp.sqrt(total)
    factor = jnp.minimum(1.0, math.sqrt(PARAMS) / grad_norm)
    in_update, in_mean, in_square = adamw(in_weight, in_moment, in_second, in_grad, factor)
    out_update, out_mean, out_square = adamw(out_weight, out_moment, out_second, out_grad, factor)
    vec_update, vec_mean, vec_square = adamw(vectors, vec_moment, vec_second, vec_grad, factor)
    return (
        result,
        input_grad,
        in_grad,
        out_grad,
        vec_grad,
        grad_norm,
        in_update,
        out_update,
        vec_update,
        in_mean,
        out_mean,
        vec_mean,
        in_square,
        out_square,
        vec_square,
    )


def solution(mesh):
    in_specs = (
        P(("dp", "fsdp"), None),
        P(("dp", "fsdp"), None),
        P(("dp", "fsdp")),
        P("fsdp", None),
        P("fsdp", None),
        P(None, "fsdp"),
        P("fsdp", None),
        P("fsdp", None),
        P(None, "fsdp"),
        P("fsdp", None),
        P("fsdp", None),
        P(None, "fsdp"),
    )
    out_specs = (
        P(("dp", "fsdp"), None),
        P(("dp", "fsdp"), None),
        P("fsdp", None),
        P("fsdp", None),
        P(None, "fsdp"),
        P(),
        P("fsdp", None),
        P("fsdp", None),
        P(None, "fsdp"),
        P("fsdp", None),
        P("fsdp", None),
        P(None, "fsdp"),
        P("fsdp", None),
        P("fsdp", None),
        P(None, "fsdp"),
    )
    return jax.shard_map(local, mesh=mesh, in_specs=in_specs, out_specs=out_specs, check_vma=False)
```

```python
import math

import jax
import jax.numpy as jnp
from jax import lax
from jax.experimental import pallas as pl
from jax.experimental.pallas import tpu as pltpu
from jax.sharding import PartitionSpec as P

D = 768
H = 12
HD = 64
FF = 3072
ADAM_STEP = 10
PARAMS = 7080960

beta_one = 0.9
beta_two = 0.95
learning = 0.03
decay_rate = 0.1
epsilon = 1e-08
norm_eps = 1e-06

F32 = jnp.float32
BF16 = jnp.bfloat16
DH = D // 2
FH = FF // 2
PAIR = 128
PAIRS = DH // PAIR
QKV = 3 * PAIR
QW = PAIRS * QKV
VEC = 128
GELU_C = math.sqrt(2.0 / math.pi)
MIB = 1 << 20

NT = (((1,), (1,)), ((), ()))
TN = (((0,), (0,)), ((), ()))


def mm(a, b, dims=(((1,), (0,)), ((), ()))):
    return lax.dot_general(a, b, dims, preferred_element_type=F32)


def fence(*arrays):
    return lax.optimization_barrier(arrays)


class Plan:
    def __init__(self, n_fsdp, n_dp):
        chips = n_fsdp // 2
        self.n, self.n_dp, self.chips = n_fsdp, n_dp, chips
        self.zs = 4 if chips % 4 == 0 else chips
        self.ys = chips // self.zs
        index = lax.axis_index("fsdp")
        self.core = index % 2
        self.y = (index // 2) % self.ys
        self.z = index // (2 * self.ys)
        self.plane = lax.axis_index("dp") % 2
        self.pos = jnp.stack([self.z, self.y, self.core, self.plane]).astype(jnp.int32)
        self.order = [
            (c, t, s) for c in range(2) for t in range(self.ys) for s in range(self.zs)
        ]

    def index(self, z, y, core):
        return ((z % self.zs) * self.ys + y % self.ys) * 2 + core

    def all(self):
        return [
            (z, y, c) for z in range(self.zs) for y in range(self.ys) for c in range(2)
        ]

    def from_z(self, a, s):
        pairs = [(self.index(z + s, y, c), self.index(z, y, c)) for z, y, c in self.all()]
        return lax.ppermute(a, "fsdp", pairs)

    def from_y(self, a, t):
        pairs = [(self.index(z, y + t, c), self.index(z, y, c)) for z, y, c in self.all()]
        return lax.ppermute(a, "fsdp", pairs)

    def swap_core(self, a):
        pairs = [(self.index(z, y, c), self.index(z, y, 1 - c)) for z, y, c in self.all()]
        return lax.ppermute(a, "fsdp", pairs)

    def swap_plane(self, a):
        return lax.ppermute(a, "dp", [(i, i ^ 1) for i in range(self.n_dp)])

    def over_pairs(self, a):
        if self.n_dp == 2:
            return a
        groups = [list(range(p, self.n_dp, 2)) for p in range(2)]
        return lax.psum(a.astype(F32), "dp", axis_index_groups=groups)

    def total(self, a):
        m = 1
        while m < self.n:
            a = a + lax.ppermute(a, "fsdp", [(i, i ^ m) for i in range(self.n)])
            m *= 2
        return a

    def row(self, pos_ref, piece, rows):
        c, t, s = piece
        z = lax.rem(pos_ref[0] + s, self.zs)
        y = lax.rem(pos_ref[1] + t, self.ys)
        core = lax.rem(pos_ref[2] + c, 2)
        at = ((z * self.ys + y) * 2 + core) * rows
        return pl.multiple_of(at, math.gcd(rows, 16))


class Scatter:
    def __init__(self, plan, own, other):
        self.plan, self.own, self.other = plan, own, other
        self.rows = own.shape[0] // plan.chips

    def by_core(self):
        self.recv = self.plan.swap_core(self.other)

    def sums(self, begin, end, arrays):
        total = self.own[begin:end].astype(F32) + self.recv[begin:end].astype(F32)
        for a in arrays:
            total = total + a.astype(F32)
        return total

    def by_y(self):
        size = self.plan.zs * self.rows
        self.y_got = [
            self.plan.from_y(self.sums(t * size, (t + 1) * size, ()).astype(BF16), -t)
            for t in range(1, self.plan.ys)
        ]

    def part(self, s):
        at = slice(s * self.rows, (s + 1) * self.rows)
        return self.sums(at.start, at.stop, [a[at] for a in self.y_got])

    def by_z(self):
        parts = [self.part(s).astype(BF16) for s in range(1, self.plan.zs)]
        self.z_got = [self.plan.from_z(a, -s - 1) for s, a in enumerate(parts)]

    def total(self):
        total = self.part(0)
        for a in self.z_got:
            total = total + a.astype(F32)
        return total.astype(BF16)


def smem():
    return pl.BlockSpec(memory_space=pltpu.SMEM)


def whole(shape):
    return pl.BlockSpec(shape, lambda *_: (0,) * len(shape))


def params(mib=58):
    return pltpu.CompilerParams(
        dimension_semantics=("arbitrary",), vmem_limit_bytes=mib * MIB
    )


def cost(flops, nbytes, exps=0):
    return pl.CostEstimate(flops=int(flops), bytes_accessed=int(nbytes), transcendentals=int(exps))


def row_type(rows):
    return BF16 if rows % 16 == 0 else F32


def place(plan, pos_ref, refs, rows, out_ref):
    for piece, ref in zip(plan.order, refs):
        out_ref[pl.ds(plan.row(pos_ref, piece, rows), rows), :] = ref[...].astype(out_ref.dtype)


def turn(plan, pos_ref, from_ref, rows, put):
    for i, piece in enumerate(plan.order):
        put(i * rows, from_ref[pl.ds(plan.row(pos_ref, piece, rows), rows), :])


def pack_in(plan, in_weight, vec_t):
    rows = in_weight.shape[0]

    def kernel(pos_ref, w_ref, vec_ref, mlp_ref, qkv_ref):
        plane = pos_ref[3]
        gain = vec_ref[:, :1]

        def take(source, width):
            at = pl.ds(pl.multiple_of(source, PAIR), width)
            low = w_ref[:, at].astype(BF16).astype(F32)
            return (low * gain).astype(BF16)

        mlp_ref[...] = take(3 * D + plane * FH, FH)
        for pair in range(PAIRS):
            for which in range(3):
                to = pair * QKV + which * PAIR
                source = which * D + plane * DH + pair * PAIR
                qkv_ref[:, to : to + PAIR] = take(source, PAIR)
        qkv_ref[:, QW:] = vec_ref[...].astype(BF16)

    return pl.pallas_call(
        kernel,
        grid=(1,),
        in_specs=[smem(), whole(in_weight.shape), whole((rows, VEC))],
        out_specs=[whole((rows, FH)), whole((rows, QW + VEC))],
        out_shape=[
            jax.ShapeDtypeStruct((rows, FH), BF16),
            jax.ShapeDtypeStruct((rows, QW + VEC), BF16),
        ],
        compiler_params=params(16),
        cost_estimate=cost(2 * rows * 3 * D, 6 * rows * 7 * D),
        name="pack_in",
    )(plan.pos, in_weight, vec_t)


def pack_out(plan, blocks):
    n, rows, width = blocks.shape

    def kernel(pos_ref, in_ref, out_ref, full_ref):
        plane = pos_ref[3]
        for i in range(n):
            full_ref[:, i * width : (i + 1) * width] = in_ref[i].astype(F32)
        mlp = full_ref[:, pl.ds(pl.multiple_of(D + plane * FH, PAIR), FH)]
        out_ref[:, :FH] = mlp.astype(BF16)
        heads = full_ref[:, pl.ds(pl.multiple_of(plane * DH, PAIR), DH)]
        out_ref[:, FH:] = heads.astype(BF16)

    return pl.pallas_call(
        kernel,
        grid=(1,),
        in_specs=[smem(), whole(blocks.shape)],
        out_specs=whole((rows, FH + DH)),
        out_shape=jax.ShapeDtypeStruct((rows, FH + DH), BF16),
        scratch_shapes=[pltpu.VMEM((rows, D + FF), F32)],
        compiler_params=params(16),
        cost_estimate=cost(rows * (D + FF), 6 * rows * D),
        name="pack_out",
    )(plan.pos, blocks)


def unpack_out(plan, own, swap, own_heads, swap_heads):
    rows = own.shape[0]
    width = (D + FF) // plan.n

    def kernel(pos_ref, own_ref, swap_ref, own_h_ref, swap_h_ref, out_ref, full_ref):
        first = pos_ref[3] == 0
        pairs = ((own_h_ref, swap_h_ref, 0, DH), (own_ref, swap_ref, D, FH))
        for a_ref, b_ref, at, size in pairs:
            a, b = a_ref[...].astype(F32), b_ref[...].astype(F32)
            full_ref[:, at : at + size] = jnp.where(first, a, b)
            full_ref[:, at + size : at + 2 * size] = jnp.where(first, b, a)
        for i in range(plan.n):
            out_ref[i] = full_ref[:, i * width : (i + 1) * width].astype(BF16)

    return pl.pallas_call(
        kernel,
        grid=(1,),
        in_specs=[smem(), whole(own.shape), whole(own.shape)]
        + [pl.BlockSpec((rows, DH), lambda j: (0, FH // DH))] * 2,
        out_specs=whole((plan.n, rows, width)),
        out_shape=jax.ShapeDtypeStruct((plan.n, rows, width), BF16),
        scratch_shapes=[pltpu.VMEM((rows, D + FF), F32)],
        compiler_params=params(16),
        cost_estimate=cost(rows * (D + FF), 6 * rows * D),
        name="unpack_out",
    )(plan.pos, own, swap, own_heads, swap_heads)


def fold(a):
    total = a[:, :PAIR]
    for i in range(1, a.shape[1] // PAIR):
        total = total + a[:, i * PAIR : (i + 1) * PAIR]
    return total


def finish_out(blocks):
    n, rows, width = blocks.shape

    def kernel(in_ref, out_ref, sq_ref):
        grad = in_ref[...].reshape(n * rows, width).astype(F32).T
        out_ref[...] = grad
        sq_ref[...] = jnp.broadcast_to(
            jnp.sum(fold(grad * grad), axis=0, keepdims=True) * 0.125, (8, PAIR)
        )

    return pl.pallas_call(
        kernel,
        grid=(1,),
        in_specs=[whole(blocks.shape)],
        out_specs=[whole((width, D)), whole((8, PAIR))],
        out_shape=[
            jax.ShapeDtypeStruct((width, D), F32),
            jax.ShapeDtypeStruct((8, PAIR), F32),
        ],
        compiler_params=params(16),
        cost_estimate=cost(4 * width * D, 6 * width * D),
        name="finish_out",
    )(blocks)


def finish_mlp(plan, own, swap, in_weight, vec_t):
    rows = in_weight.shape[0]

    def kernel(pos_ref, own_ref, swap_ref, w_ref, vec_ref, grad_ref, sq_ref, dot_ref):
        step = pl.program_id(0)

        @pl.when(step == 0)
        def _():
            sq_ref[...] = jnp.zeros_like(sq_ref)
            dot_ref[...] = jnp.zeros_like(dot_ref)

        mine = step // 2 == pos_ref[3]
        hat = jnp.where(mine, own_ref[...].astype(F32), swap_ref[...].astype(F32))
        grad = hat * vec_ref[:, :1]
        grad_ref[...] = grad
        sq_ref[...] += fold(grad * grad)
        dot_ref[...] += fold(w_ref[...].astype(BF16).astype(F32) * hat)

    part = pl.BlockSpec((rows, D), lambda j: (0, j % 2))
    columns = pl.BlockSpec((rows, D), lambda j: (0, 3 + j))
    small = jax.ShapeDtypeStruct((rows, VEC), F32)
    return pl.pallas_call(
        kernel,
        grid=(FF // D,),
        in_specs=[smem(), part, part, columns, whole((rows, VEC))],
        out_specs=[columns, whole((rows, VEC)), whole((rows, VEC))],
        out_shape=[jax.ShapeDtypeStruct(in_weight.shape, F32), small, small],
        compiler_params=params(16),
        cost_estimate=cost(8 * rows * FF, 12 * rows * FF),
        name="finish_mlp",
    )(plan.pos, own, swap, in_weight, vec_t)


def finish_qkv(plan, own, swap, in_weight, vec_t, grad, sq, dot, sq_out):
    rows = in_weight.shape[0]

    def kernel(
        pos_ref, own_ref, swap_ref, w_ref, vec_ref, _, sq_in_ref, dot_in_ref, sqo_ref,
        grad_ref, vg_ref, total_ref, sq_ref, dot_ref,
    ):
        step = pl.program_id(0)

        @pl.when(step == 0)
        def _():
            sq_ref[...] = sq_in_ref[...]
            dot_ref[...] = dot_in_ref[...]

        first = pos_ref[3] == 0
        parts = []
        for pair in range(PAIRS):
            at = pl.ds(pl.multiple_of(pair * QKV + step * PAIR, PAIR), PAIR)
            parts.append((own_ref[:, at].astype(F32), swap_ref[:, at].astype(F32)))
        low = [jnp.where(first, a, b) for a, b in parts]
        high = [jnp.where(first, b, a) for a, b in parts]
        hat = jnp.concatenate(low + high, axis=1)
        grad = hat * vec_ref[:, :1]
        grad_ref[...] = grad
        sq_ref[...] += fold(grad * grad)
        dot_ref[...] += fold(w_ref[...].astype(BF16).astype(F32) * hat)

        @pl.when(step == 2)
        def _():
            tail = own_ref[:, QW:].astype(F32) + swap_ref[:, QW:].astype(F32)
            gain = jnp.sum(dot_ref[...], axis=1, keepdims=True)
            lane = lax.broadcasted_iota(jnp.int32, tail.shape, 1)
            vec = jnp.where(lane == 0, gain, tail)
            vg_ref[...] = vec
            total = jnp.sum(sq_ref[...] + vec * vec, axis=0, keepdims=True)
            total_ref[...] = jnp.broadcast_to(total * 0.125, (8, PAIR)) + sqo_ref[...]

    columns = pl.BlockSpec((rows, D), lambda j: (0, j))
    small = whole((rows, VEC))
    return pl.pallas_call(
        kernel,
        grid=(3,),
        in_specs=[
            smem(), whole(own.shape), whole(own.shape), columns, small,
            pl.BlockSpec(memory_space=pl.ANY), small, small, whole((8, PAIR)),
        ],
        out_specs=[columns, small, whole((8, PAIR))],
        out_shape=[
            jax.ShapeDtypeStruct(in_weight.shape, F32),
            jax.ShapeDtypeStruct((rows, VEC), F32),
            jax.ShapeDtypeStruct((8, PAIR), F32),
        ],
        scratch_shapes=[pltpu.VMEM((rows, VEC), F32)] * 2,
        input_output_aliases={5: 0},
        compiler_params=params(16),
        cost_estimate=cost(24 * rows * D, 36 * rows * D),
        name="finish_qkv",
    )(plan.pos, own, swap, in_weight, vec_t, grad, sq, dot, sq_out)


def normalize(tokens, cotangent):
    tok = tokens.shape[0]

    def kernel(t_ref, c_ref, out_ref):
        rows = t_ref[...].astype(F32)
        centre = rows - jnp.mean(rows, axis=-1, keepdims=True)
        r = lax.rsqrt(jnp.mean(centre * centre, axis=-1, keepdims=True) + norm_eps)
        out_ref[:, :D] = (centre * r).astype(BF16)
        out_ref[:, D:] = c_ref[...]

    block = pl.BlockSpec((tok // 4, D), lambda j: (j, 0))
    return pl.pallas_call(
        kernel,
        grid=(4,),
        in_specs=[block, block],
        out_specs=pl.BlockSpec((tok // 4, 2 * D), lambda j: (j, 0)),
        out_shape=jax.ShapeDtypeStruct((tok, 2 * D), BF16),
        compiler_params=params(16),
        cost_estimate=cost(10 * tok * D, 8 * tok * D),
        name="normalize",
    )(tokens, cotangent)


def transposes(plan, xc_own, xc_other, rows):
    tok = xc_own.shape[0]
    kind = row_type(rows)

    def kernel(pos_ref, own_ref, other_ref, out_ref, sum_ref, t_ref):
        for half, ref in enumerate((own_ref, other_ref)):
            t_ref[...] = ref[...].astype(F32).T.astype(kind)

            def put(at, a):
                out_ref[0, at : at + rows, half * tok : (half + 1) * tok] = a.astype(BF16)

            turn(plan, pos_ref, t_ref, rows, put)
        total = jnp.sum(own_ref[...].astype(F32), axis=0, keepdims=True)
        sum_ref[0] = jnp.broadcast_to(total, (8, D))

    return pl.pallas_call(
        kernel,
        grid=(2,),
        in_specs=[smem()] + [pl.BlockSpec((tok, D), lambda j: (0, j))] * 2,
        out_specs=[
            pl.BlockSpec((1, D, 2 * tok), lambda j: (j, 0, 0)),
            pl.BlockSpec((1, 8, D), lambda j: (j, 0, 0)),
        ],
        out_shape=[
            jax.ShapeDtypeStruct((2, D, 2 * tok), BF16),
            jax.ShapeDtypeStruct((2, 8, D), F32),
        ],
        scratch_shapes=[pltpu.VMEM((D, tok), kind)],
        compiler_params=params(24),
        cost_estimate=cost(10 * tok * D, 16 * tok * D),
        name="transposes",
    )(plan.pos, xc_own, xc_other)


def mlp_forward(plan, xc_own, xc_other, turned, pieces):
    tok = xc_own.shape[0]
    rows = pieces[0].shape[0]
    tile = 512
    n = len(pieces)

    half_d = D // 2

    def kernel(pos_ref, xo_ref, xp_ref, ct_ref, *rest):
        refs, (mix_ref, slope_ref, g_own_ref, g_other_ref, w_ref) = rest[:n], rest[n:]
        place(plan, pos_ref, refs, rows, w_ref)
        w = w_ref[...].astype(BF16)
        for half, x_ref in enumerate((xo_ref, xp_ref)):
            v = mm(x_ref[...], w)
            v2 = v * v
            t = jnp.tanh(v * (GELU_C + (GELU_C * 0.044715) * v2))
            h = 0.5 + 0.5 * t
            g = v * h
            slope = h + 2.0 * g * (1.0 - h) * (GELU_C + (3.0 * GELU_C * 0.044715) * v2)
            mix_ref[half] = g.astype(BF16)
            slope_ref[half] = slope.astype(BF16)
        g = mm(ct_ref[0], mix_ref[...].reshape(2 * tok, tile)).astype(BF16)
        g_own_ref[...] = g[:half_d]
        g_other_ref[...] = g[half_d:]

    block = pl.BlockSpec((2, tok, tile), lambda j: (0, 0, j))
    grad = pl.BlockSpec((half_d, tile), lambda j: (0, j))
    return pl.pallas_call(
        kernel,
        grid=(FH // tile,),
        in_specs=[smem()]
        + [pl.BlockSpec((tok, D), lambda j: (0, 0))] * 2
        + [pl.BlockSpec((1, D, 2 * tok), lambda j: (1, 0, 0))]
        + [pl.BlockSpec((rows, tile), lambda j: (0, j))] * n,
        out_specs=[block, block, grad, grad],
        out_shape=[jax.ShapeDtypeStruct((2, tok, FH), BF16)] * 2
        + [jax.ShapeDtypeStruct((half_d, FH), BF16)] * 2,
        scratch_shapes=[pltpu.VMEM((D, tile), row_type(rows))],
        compiler_params=params(),
        cost_estimate=cost(8 * tok * D * FH, 12 * tok * FH, 2 * tok * FH),
        name="mlp_forward",
    )(plan.pos, xc_own, xc_other, turned, *pieces)


def head_means(a, block_ref):
    high = a.astype(BF16)
    low = (a - high.astype(F32)).astype(BF16)
    return mm(high, block_ref[...]) + mm(low, block_ref[...])


def attention_forward(plan, xc_own, xc_other, pieces, id_row, id_col, block, turned):
    tok = xc_own.shape[0]
    rows = pieces[0].shape[0]
    n = len(pieces)

    half_d = D // 2

    def kernel(pos_ref, xo_ref, xp_ref, idr_ref, idc_ref, block_ref, ct_ref, *rest):
        refs, vec_refs = rest[:n], rest[n : 2 * n]
        (
            q_ref, k_ref, v_ref, nq_ref, nk_ref, rq_ref, rk_ref, att_ref, p_ref, gain_ref,
            g_own_ref, g_other_ref, w_ref, vs_ref,
        ) = rest[2 * n :]
        step = pl.program_id(0)

        @pl.when(step == 0)
        def _():
            place(plan, pos_ref, vec_refs, rows, vs_ref)
            gain_ref[...] = vs_ref[...].astype(F32).T[:8]

        place(plan, pos_ref, refs, rows, w_ref)
        w = w_ref[...].astype(BF16)
        column = pl.ds(pl.multiple_of(pos_ref[3] * DH + step * PAIR, PAIR), PAIR)
        q_gain = gain_ref[1:2, column] * (HD ** (-0.5))
        k_gain = gain_ref[2:3, column]
        lane = lax.broadcasted_iota(jnp.int32, (tok, PAIR), 1)
        first = lane < HD
        for half, x_ref in enumerate((xo_ref, xp_ref)):
            raw = mm(x_ref[...], w)

            def normed(a, gain, n_ref, r_ref, out_ref):
                centre = a - head_means(a, block_ref)
                r = lax.rsqrt(head_means(centre * centre, block_ref) + norm_eps)
                normal = centre * r
                n_ref[half] = normal.astype(BF16)
                r_ref[half] = r.astype(BF16)
                low = (normal * gain).astype(BF16)
                out_ref[half] = low
                return low

            q = normed(raw[:, :PAIR], q_gain, nq_ref, rq_ref, q_ref)
            k = normed(raw[:, PAIR : 2 * PAIR], k_gain, nk_ref, rk_ref, k_ref)
            v = raw[:, 2 * PAIR :].astype(BF16)
            v_ref[half] = v
            same = idc_ref[half] == idr_ref[half]
            att = []
            zero = jnp.zeros_like(q)
            for head in range(2):
                qh = jnp.where(first, q, zero) if head == 0 else jnp.where(first, zero, q)
                e = jnp.where(same, jnp.exp(mm(qh, k, NT)), 0.0)
                p = (e * (1.0 / jnp.sum(e, axis=1, keepdims=True))).astype(BF16)
                p_ref[half, head] = p
                att.append(mm(p, v))
            att_ref[half] = jnp.where(first, att[0], att[1]).astype(BF16)
        g = mm(ct_ref[0], att_ref[...].reshape(2 * tok, PAIR)).astype(BF16)
        g_own_ref[...] = g[:half_d]
        g_other_ref[...] = g[half_d:]

    pair = pl.BlockSpec((2, tok, PAIR), lambda j: (0, 0, j))
    small = jax.ShapeDtypeStruct((2, tok, DH), BF16)
    return pl.pallas_call(
        kernel,
        grid=(PAIRS,),
        in_specs=[smem()]
        + [pl.BlockSpec((tok, D), lambda j: (0, 0))] * 2
        + [whole((2, 1, tok)), whole((2, tok, 1)), whole((PAIR, PAIR))]
        + [pl.BlockSpec((1, D, 2 * tok), lambda j: (1, 0, 0))]
        + [pl.BlockSpec((rows, QKV), lambda j: (0, j))] * n
        + [pl.BlockSpec((rows, VEC), lambda j: (0, QW // VEC))] * n,
        out_specs=[pair] * 8
        + [pl.BlockSpec((2, 2, tok, tok), lambda j: (0, j, 0, 0)), whole((8, D))]
        + [pl.BlockSpec((half_d, PAIR), lambda j: (0, FH // PAIR + j))] * 2,
        out_shape=[small] * 8
        + [
            jax.ShapeDtypeStruct((2, 2 * PAIRS, tok, tok), BF16),
            jax.ShapeDtypeStruct((8, D), F32),
            jax.ShapeDtypeStruct((half_d, FH + DH), BF16),
            jax.ShapeDtypeStruct((half_d, FH + DH), BF16),
        ],
        scratch_shapes=[
            pltpu.VMEM((D, QKV), row_type(rows)),
            pltpu.VMEM((D, VEC), row_type(rows)),
        ],
        compiler_params=params(),
        cost_estimate=cost(4 * tok * D * QW, 20 * MIB, 12 * tok * tok),
        name="attention_forward",
    )(
        plan.pos, xc_own, xc_other, id_row, id_col, block, turned,
        *pieces, *pieces,
    )


def output_step(plan, att, mixed, slope, xc_own, xc_other, pieces):
    tok = xc_own.shape[0]
    rows = pieces[0].shape[0]
    n = len(pieces)
    tile = DH
    steps = 1 + FH // tile

    def kernel(pos_ref, att_ref, mix_ref, slope_ref, co_ref, cp_ref, *rest):
        refs = rest[:n]
        out_own_ref, out_other_ref, d_att_ref, d_in_ref, w_ref, acc_ref = rest[n:]
        step = pl.program_id(0)

        place(plan, pos_ref, refs, rows, w_ref)
        w = w_ref[...].astype(BF16)

        @pl.when(step == 0)
        def _():
            for half, ref in enumerate((co_ref, cp_ref)):
                d_att_ref[half] = mm(ref[...], w).astype(BF16)
                acc_ref[half] = mm(att_ref[half], w, NT)

        @pl.when(step > 0)
        def _():
            for half, ref in enumerate((co_ref, cp_ref)):
                d = mm(ref[...], w)
                d_in_ref[half] = (d * slope_ref[half].astype(F32)).astype(BF16)
                acc_ref[half] += mm(mix_ref[half], w, NT)

        @pl.when(step == steps - 1)
        def _():
            out_own_ref[...] = acc_ref[0]
            out_other_ref[...] = acc_ref[1].astype(BF16)

    hidden = pl.BlockSpec((2, tok, tile), lambda j: (0, 0, jnp.maximum(j - 1, 0)))
    return pl.pallas_call(
        kernel,
        grid=(steps,),
        in_specs=[smem(), whole((2, tok, tile)), hidden, hidden]
        + [pl.BlockSpec((tok, D), lambda j: (0, 1))] * 2
        + [pl.BlockSpec((rows, tile), lambda j: (0, jnp.where(j == 0, steps - 1, j - 1)))] * n,
        out_specs=[whole((tok, D)), whole((tok, D)), whole((2, tok, tile)), hidden],
        out_shape=[
            jax.ShapeDtypeStruct((tok, D), F32),
            jax.ShapeDtypeStruct((tok, D), BF16),
            jax.ShapeDtypeStruct((2, tok, DH), BF16),
            jax.ShapeDtypeStruct((2, tok, FH), BF16),
        ],
        scratch_shapes=[
            pltpu.VMEM((D, tile), row_type(rows)),
            pltpu.VMEM((2, tok, D), F32),
        ],
        compiler_params=params(),
        cost_estimate=cost(4 * 2 * tok * steps * tile * D, 20 * MIB),
        name="output_step",
    )(plan.pos, att, mixed, slope, xc_own, xc_other, *pieces)


def mlp_backward(plan, turned, d_inner, pieces, g_own, g_other):
    tok = d_inner.shape[1]
    rows = pieces[0].shape[0]
    n = len(pieces)
    half_d = D // 2
    tile = 512
    steps = FH // tile

    def kernel(pos_ref, xt_ref, d_ref, *rest):
        refs = rest[:n]
        g_own_ref, g_other_ref, e_own_ref, e_other_ref, w_ref, acc_ref = rest[n + 2 :]
        step = pl.program_id(0)

        @pl.when(step == 0)
        def _():
            acc_ref[...] = jnp.zeros_like(acc_ref)

        place(plan, pos_ref, refs, rows, w_ref)
        d = d_ref[...].reshape(2 * tok, tile)
        g = mm(xt_ref[0], d).astype(BF16)
        g_own_ref[...] = g[:half_d]
        g_other_ref[...] = g[half_d:]
        acc_ref[...] += mm(d, w_ref[...].astype(BF16), NT)

        @pl.when(step == steps - 1)
        def _():
            e_own_ref[...] = acc_ref[:tok]
            e_other_ref[...] = acc_ref[tok:]

    grad = pl.BlockSpec((half_d, tile), lambda j: (0, j))
    return pl.pallas_call(
        kernel,
        grid=(steps,),
        in_specs=[
            smem(),
            pl.BlockSpec((1, D, 2 * tok), lambda j: (0, 0, 0)),
            pl.BlockSpec((2, tok, tile), lambda j: (0, 0, j)),
        ]
        + [pl.BlockSpec((rows, tile), lambda j: (0, j))] * n
        + [pl.BlockSpec(memory_space=pl.ANY)] * 2,
        out_specs=[grad, grad] + [whole((tok, D))] * 2,
        input_output_aliases={3 + n: 0, 4 + n: 1},
        out_shape=[jax.ShapeDtypeStruct((half_d, FH + DH), BF16)] * 2
        + [jax.ShapeDtypeStruct((tok, D), F32)] * 2,
        scratch_shapes=[
            pltpu.VMEM((D, tile), row_type(rows)),
            pltpu.VMEM((2 * tok, D), F32),
        ],
        compiler_params=params(),
        cost_estimate=cost(8 * tok * D * FH, 20 * MIB),
        name="mlp_backward",
    )(plan.pos, turned, d_inner, *pieces, g_own, g_other)


def attention_backward(
    plan, turned, saved, d_att, block, gains, cot_sum, pieces, e_own, e_other, before, begin, end
):
    q, k, v, nq, nk, rq, rk, probs = saved
    tok = d_att.shape[1]
    rows = pieces[0].shape[0]
    n = len(pieces)
    half_d = D // 2
    kind = row_type(rows)
    n_before = len(before)

    def kernel(pos_ref, xt_ref, q_ref, k_ref, v_ref, nq_ref, nk_ref, rq_ref, rk_ref, p_ref,
               da_ref, block_ref, gain_ref, cot_ref, ein_own_ref, ein_other_ref, *rest):
        refs, rest = rest[:n], rest[n:]
        befores, rest = rest[:n_before], rest[n_before:]
        (
            g_own_ref, g_other_ref, e_own_ref, e_other_ref, vec_ref, w_ref, d_ref, turn_ref,
        ) = rest
        step = pl.program_id(0) + begin

        @pl.when(step == begin)
        def _():
            e_own_ref[...] = ein_own_ref[...]
            e_other_ref[...] = ein_other_ref[...]
            if befores:
                before_own_ref, before_other_ref, before_vec_ref = befores
                vec_ref[...] = before_vec_ref[...]
                g_own_ref[:, : begin * QKV] = before_own_ref[...]
                g_other_ref[:, : begin * QKV] = before_other_ref[...]
            else:
                vec_ref[...] = jnp.zeros_like(vec_ref)
                vec_ref[3:4, :] = cot_ref[0, :1]

        place(plan, pos_ref, refs, rows, w_ref)
        w = w_ref[...].astype(BF16)
        column = pl.ds(pl.multiple_of(pos_ref[3] * DH + step * PAIR, PAIR), PAIR)
        q_gain = gain_ref[1:2, column]
        k_gain = gain_ref[2:3, column]
        first = lax.broadcasted_iota(jnp.int32, (tok, PAIR), 1) < HD
        for half in range(2):
            qb, kb, vb, da = q_ref[half], k_ref[half], v_ref[half], da_ref[half]
            q_t, da_t = qb.T, da.T
            zero = jnp.zeros_like(da)
            dq, dk_t, dv_t = [], [], []
            for head in range(2):
                at = slice(head * HD, (head + 1) * HD)
                dah = jnp.where(first, da, zero) if head == 0 else jnp.where(first, zero, da)
                p_low = p_ref[half, head]
                p = p_low.astype(F32)
                t = p * mm(dah, vb, NT)
                ds = (t - p * jnp.sum(t, axis=1, keepdims=True)).astype(BF16)
                dv_t.append(mm(da_t[at], p_low))
                dk_t.append(mm(q_t[at], ds))
                dq.append(mm(ds, kb))
            d_query = jnp.where(first, dq[0], dq[1])
            d_key = jnp.concatenate(dk_t, axis=0).T
            d_value = jnp.concatenate(dv_t, axis=0).T

            def back(d, gain, n_ref, r_ref, which, factor):
                normal = n_ref[half].astype(F32)
                d = d * factor
                vec_ref[which : which + 1, column] += jnp.sum(d * normal, axis=0, keepdims=True)
                e = d * gain
                mean = head_means(e, block_ref)
                along = head_means(e * normal, block_ref)
                return (r_ref[half].astype(F32) * (e - mean - normal * along)).astype(BF16)

            at = slice(half * tok, (half + 1) * tok)
            d_ref[at, :PAIR] = back(d_query, q_gain, nq_ref, rq_ref, 1, HD ** (-0.5))
            d_ref[at, PAIR : 2 * PAIR] = back(d_key, k_gain, nk_ref, rk_ref, 2, 1.0)
            d_ref[at, 2 * PAIR :] = d_value.astype(BF16)
        g = mm(xt_ref[0], d_ref[...]).astype(BF16)
        at = pl.ds(pl.multiple_of(step * QKV, QKV), QKV)
        g_own_ref[:, at] = g[:half_d]
        g_other_ref[:, at] = g[half_d:]
        e_own_ref[...] += mm(d_ref[:tok], w, NT)
        e_other_ref[...] += mm(d_ref[tok:], w, NT)

        if end < PAIRS:
            return

        @pl.when(step == PAIRS - 1)
        def _():
            turn_ref[...] = vec_ref[...].T.astype(kind)

            def put(at, a):
                ref = g_own_ref if at < half_d else g_other_ref
                ref[at % half_d : at % half_d + rows, QW:] = a.astype(BF16)

            turn(plan, pos_ref, turn_ref, rows, put)

    width = QW + VEC if end == PAIRS else end * QKV
    pair = pl.BlockSpec((2, tok, PAIR), lambda j: (0, 0, begin + j))
    return pl.pallas_call(
        kernel,
        grid=(end - begin,),
        in_specs=[smem(), pl.BlockSpec((1, D, 2 * tok), lambda j: (0, 0, 0))]
        + [pair] * 7
        + [
            pl.BlockSpec((2, 2, tok, tok), lambda j: (0, begin + j, 0, 0)),
            pair,
            whole((PAIR, PAIR)),
            whole((8, D)),
            pl.BlockSpec((1, 8, D), lambda j: (1, 0, 0)),
            whole((tok, D)),
            whole((tok, D)),
        ]
        + [pl.BlockSpec((rows, QKV), lambda j: (0, begin + j))] * n
        + [whole(a.shape) for a in before],
        out_specs=[whole((half_d, width))] * 2 + [whole((tok, D))] * 2 + [whole((VEC, D))],
        out_shape=[jax.ShapeDtypeStruct((half_d, width), BF16)] * 2
        + [jax.ShapeDtypeStruct((tok, D), F32)] * 2
        + [jax.ShapeDtypeStruct((VEC, D), F32)],
        scratch_shapes=[
            pltpu.VMEM((D, QKV), kind),
            pltpu.VMEM((2 * tok, QKV), BF16),
            pltpu.VMEM((D, VEC), kind),
        ],
        compiler_params=params(),
        cost_estimate=cost(20 * tok * D * QKV * (end - begin), 8 * MIB * (end - begin)),
        name="attention_backward",
    )(
        plan.pos, turned, q, k, v, nq, nk, rq, rk, probs, d_att, block, gains, cot_sum,
        e_own, e_other, *pieces, *before,
    )


def token_gradient(tokens, cotangent, e_own, e_recv):
    tok = tokens.shape[0]

    def kernel(t_ref, c_ref, own_ref, recv_ref, out_ref):
        rows = t_ref[...].astype(F32)
        centre = rows - jnp.mean(rows, axis=-1, keepdims=True)
        r = lax.rsqrt(jnp.mean(centre * centre, axis=-1, keepdims=True) + norm_eps)
        normal = centre * r
        e = own_ref[...] + recv_ref[...].astype(F32)
        mean = jnp.mean(e, axis=-1, keepdims=True)
        along = jnp.mean(e * normal, axis=-1, keepdims=True)
        out_ref[...] = c_ref[...].astype(F32) + r * (e - mean - normal * along)

    block = pl.BlockSpec((tok // 4, D), lambda j: (j, 0))
    return pl.pallas_call(
        kernel,
        grid=(4,),
        in_specs=[block] * 4,
        out_specs=block,
        out_shape=jax.ShapeDtypeStruct((tok, D), F32),
        compiler_params=params(16),
        cost_estimate=cost(20 * tok * D, 14 * tok * D),
        name="token_gradient",
    )(tokens, cotangent, e_own, e_recv)


def adamw(master, first, second, grad, factor):
    clipped = grad * factor
    first_new = beta_one * first + (1.0 - beta_one) * clipped
    second_new = beta_two * second + (1.0 - beta_two) * clipped * clipped
    first_hat = first_new / (1.0 - beta_one**ADAM_STEP)
    second_hat = second_new / (1.0 - beta_two**ADAM_STEP)
    update = -learning * (first_hat / (jnp.sqrt(second_hat) + epsilon) + decay_rate * master)
    return (update, first_new, second_new)


def local(
    tokens,
    cotangent,
    image_ids,
    in_weight,
    out_weight,
    vectors,
    in_moment,
    out_moment,
    vec_moment,
    in_second,
    out_second,
    vec_second,
):
    plan = Plan(lax.axis_size("fsdp"), lax.axis_size("dp"))
    rows = in_weight.shape[0]
    out_rows = out_weight.shape[0]

    low_vec = vectors.astype(BF16).astype(F32)
    vec_t = jnp.pad(low_vec.T, ((0, 0), (0, VEC - 4)))
    mlp_piece, qkv_piece = pack_in(plan, in_weight, vec_t)
    xc_own = normalize(tokens, cotangent)

    def z_all(piece):
        return [plan.from_z(piece, s) for s in range(1, plan.zs)]

    def y_all(pieces):
        return [[plan.from_y(a, t) for a in pieces] for t in range(1, plan.ys)]

    def join(y_first, y_rest):
        return [a for first, rest in zip(y_first, y_rest) for a in first + rest]

    def core_all(pieces):
        return [plan.swap_core(a) for a in pieces]

    def held(groups):
        flat = iter(fence(*[a for group in groups for a in group]))
        return [[next(flat) for _ in group] for group in groups]

    mlp_z = z_all(mlp_piece)
    mlp_y0 = y_all([mlp_piece])
    xc_other = plan.swap_plane(xc_own)
    ids_other = plan.swap_plane(image_ids)
    out_now, mlp_z[0] = fence(out_weight, mlp_z[0])
    blocks = out_now.astype(BF16).T.reshape(plan.n, rows, out_rows)
    blocks = lax.all_to_all(blocks, "fsdp", 0, 0)
    (qkv_piece,), mlp_z = held([[qkv_piece], mlp_z])
    mlp_col = [mlp_piece] + mlp_z
    mlp_y1 = y_all(mlp_z)
    qkv_z = z_all(qkv_piece)
    qkv_y0 = y_all([qkv_piece])
    mlp_core = core_all(mlp_col)
    out_piece = pack_out(plan, blocks)
    mlp_y = join(mlp_y0, mlp_y1)
    mlp_y, qkv_z, mlp_core, (out_piece,) = held([mlp_y, qkv_z, mlp_core, [out_piece]])
    qkv_col = [qkv_piece] + qkv_z
    mlp_core = mlp_core + core_all(mlp_y)
    mlp_pieces = mlp_col + mlp_y + mlp_core
    qkv_y1 = y_all(qkv_z)
    out_z = z_all(out_piece)
    out_y0 = y_all([out_piece])
    qkv_core = core_all(qkv_col)
    turned, cot_sum = transposes(plan, xc_own, xc_other, rows)
    mixed, slope, g_own, g_other = mlp_forward(plan, xc_own, xc_other, turned, mlp_pieces)
    qkv_y = join(qkv_y0, qkv_y1)
    qkv_y, out_z, qkv_core, (mixed, slope, g_own, g_other) = held(
        [qkv_y, out_z, qkv_core, [mixed, slope, g_own, g_other]]
    )
    s_out = Scatter(plan, g_own, g_other)
    s_out.by_core()
    out_col = [out_piece] + out_z
    qkv_core = qkv_core + core_all(qkv_y)
    qkv_pieces = qkv_col + qkv_y + qkv_core
    out_y1 = y_all(out_z)
    out_core = core_all(out_col)
    ids = jnp.stack([image_ids, ids_other])
    lane = jnp.arange(PAIR) // HD
    block = jnp.where(lane[:, None] == lane[None, :], 1.0 / HD, 0.0).astype(BF16)
    *saved, att, probs, gains, m_own, m_other = attention_forward(
        plan, xc_own, xc_other, qkv_pieces, ids[:, None, :], ids[:, :, None], block, turned
    )
    saved = tuple(saved) + (probs,)
    out_y = join(out_y0, out_y1)
    out_y, out_core, (att, s_out.recv) = held([out_y, out_core, [att, s_out.recv]])
    s_out.by_y()
    out_core = out_core + core_all(out_y)
    out_pieces = out_col + out_y + out_core
    out_mine, out_theirs, d_att, d_inner = output_step(
        plan, att, mixed, slope, xc_own, xc_other, out_pieces
    )
    s_out.y_got, (out_theirs, d_att, d_inner) = held([s_out.y_got, [out_theirs, d_att, d_inner]])
    s_out.by_z()
    out_recv = plan.swap_plane(out_theirs)
    g_own, g_other, e_own, e_other = mlp_backward(
        plan, turned, d_inner, mlp_pieces, m_own, m_other
    )
    s_out.z_got, (g_own, g_other, e_own, e_other) = held(
        [s_out.z_got, [g_own, g_other, e_own, e_other]]
    )
    s_mlp = Scatter(plan, g_own, g_other)
    s_mlp.by_core()
    out_sum = s_out.total()
    s_mlp.recv, e_own = fence(s_mlp.recv, e_own)
    s_mlp.by_y()
    out_swap = plan.swap_plane(out_sum)
    g_own, g_other, e_own, e_other, _ = attention_backward(
        plan, turned, saved, d_att, block, gains, cot_sum, qkv_pieces, e_own, e_other, (),
        0, PAIRS,
    )
    s_mlp.y_got, (g_own, g_other, e_own, e_other, out_swap, out_recv) = held(
        [s_mlp.y_got, [g_own, g_other, e_own, e_other, out_swap, out_recv]]
    )
    s_qkv = Scatter(plan, g_own, g_other)
    s_qkv.by_core()
    s_mlp.by_z()
    e_recv = plan.swap_plane(e_other.astype(BF16))
    result = (
        tokens.astype(F32) + out_mine + out_recv.astype(F32) + gains[3][None, :]
    ).astype(BF16)
    s_qkv.recv, result = fence(s_qkv.recv, result)
    s_qkv.by_y()
    s_mlp.z_got, s_qkv.y_got, (e_recv,) = held([s_mlp.z_got, s_qkv.y_got, [e_recv]])
    s_qkv.by_z()
    mlp_sum = s_mlp.total()
    mlp_swap = plan.swap_plane(mlp_sum)
    mlp_sum, mlp_swap = plan.over_pairs(mlp_sum), plan.over_pairs(mlp_swap)
    blocks = unpack_out(
        plan, plan.over_pairs(out_sum), plan.over_pairs(out_swap), mlp_sum, mlp_swap
    )
    blocks = lax.all_to_all(blocks, "fsdp", 0, 0)
    input_grad = token_gradient(tokens, cotangent, e_own, e_recv)
    in_grad, sq, dot = finish_mlp(plan, mlp_sum, mlp_swap, in_weight, vec_t)
    s_qkv.z_got, (input_grad, in_grad) = held([s_qkv.z_got, [input_grad, in_grad]])
    qkv_sum = s_qkv.total()
    qkv_swap = plan.swap_plane(qkv_sum)
    out_grad, sq_out = finish_out(blocks)
    in_grad, vec_cols, square = finish_qkv(
        plan, plan.over_pairs(qkv_sum), plan.over_pairs(qkv_swap), in_weight, vec_t, in_grad,
        sq, dot, sq_out,
    )
    vec_grad = vec_cols[:, :4].T
    total = jnp.sum(plan.total(square))
    grad_norm = jnp.sqrt(total)
    factor = jnp.minimum(1.0, math.sqrt(PARAMS) / grad_norm)
    in_update, in_mean, in_square = adamw(in_weight, in_moment, in_second, in_grad, factor)
    out_update, out_mean, out_square = adamw(out_weight, out_moment, out_second, out_grad, factor)
    vec_update, vec_mean, vec_square = adamw(vectors, vec_moment, vec_second, vec_grad, factor)
    return (
        result,
        input_grad,
        in_grad,
        out_grad,
        vec_grad,
        grad_norm,
        in_update,
        out_update,
        vec_update,
        in_mean,
        out_mean,
        vec_mean,
        in_square,
        out_square,
        vec_square,
    )


def solution(mesh):
    in_specs = (
        P(("dp", "fsdp"), None),
        P(("dp", "fsdp"), None),
        P(("dp", "fsdp")),
        P("fsdp", None),
        P("fsdp", None),
        P(None, "fsdp"),
        P("fsdp", None),
        P("fsdp", None),
        P(None, "fsdp"),
        P("fsdp", None),
        P("fsdp", None),
        P(None, "fsdp"),
    )
    out_specs = (
        P(("dp", "fsdp"), None),
        P(("dp", "fsdp"), None),
        P("fsdp", None),
        P("fsdp", None),
        P(None, "fsdp"),
        P(),
        P("fsdp", None),
        P("fsdp", None),
        P(None, "fsdp"),
        P("fsdp", None),
        P("fsdp", None),
        P(None, "fsdp"),
        P("fsdp", None),
        P("fsdp", None),
        P(None, "fsdp"),
    )
    return jax.shard_map(local, mesh=mesh, in_specs=in_specs, out_specs=out_specs, check_vma=False)
```

```python
import math

import jax
import jax.numpy as jnp
from jax import lax
from jax.experimental import pallas as pl
from jax.experimental.pallas import tpu as pltpu
from jax.sharding import PartitionSpec as P

D = 768
H = 12
HD = 64
FF = 3072
ADAM_STEP = 10
PARAMS = 7080960

beta_one = 0.9
beta_two = 0.95
learning = 0.03
decay_rate = 0.1
epsilon = 1e-08
norm_eps = 1e-06

F32 = jnp.float32
BF16 = jnp.bfloat16
DH = D // 2
FH = FF // 2
PAIR = 128
PAIRS = DH // PAIR
QKV = 3 * PAIR
QW = PAIRS * QKV
VEC = 128
GELU_C = math.sqrt(2.0 / math.pi)
MIB = 1 << 20

NT = (((1,), (1,)), ((), ()))
TN = (((0,), (0,)), ((), ()))


def mm(a, b, dims=(((1,), (0,)), ((), ()))):
    return lax.dot_general(a, b, dims, preferred_element_type=F32)


def fence(*arrays):
    return lax.optimization_barrier(arrays)


class Plan:
    def __init__(self, n_fsdp, n_dp):
        chips = n_fsdp // 2
        self.n, self.n_dp, self.chips = n_fsdp, n_dp, chips
        self.zs = 4 if chips % 4 == 0 else chips
        self.ys = chips // self.zs
        index = lax.axis_index("fsdp")
        self.core = index % 2
        self.y = (index // 2) % self.ys
        self.z = index // (2 * self.ys)
        self.plane = lax.axis_index("dp") % 2
        self.pos = jnp.stack([self.z, self.y, self.core, self.plane]).astype(jnp.int32)
        self.order = [
            (c, t, s) for c in range(2) for t in range(self.ys) for s in range(self.zs)
        ]

    def index(self, z, y, core):
        return ((z % self.zs) * self.ys + y % self.ys) * 2 + core

    def all(self):
        return [
            (z, y, c) for z in range(self.zs) for y in range(self.ys) for c in range(2)
        ]

    def from_z(self, a, s):
        pairs = [(self.index(z + s, y, c), self.index(z, y, c)) for z, y, c in self.all()]
        return lax.ppermute(a, "fsdp", pairs)

    def from_y(self, a, t):
        pairs = [(self.index(z, y + t, c), self.index(z, y, c)) for z, y, c in self.all()]
        return lax.ppermute(a, "fsdp", pairs)

    def swap_core(self, a):
        pairs = [(self.index(z, y, c), self.index(z, y, 1 - c)) for z, y, c in self.all()]
        return lax.ppermute(a, "fsdp", pairs)

    def swap_plane(self, a):
        return lax.ppermute(a, "dp", [(i, i ^ 1) for i in range(self.n_dp)])

    def over_pairs(self, a):
        if self.n_dp == 2:
            return a
        groups = [list(range(p, self.n_dp, 2)) for p in range(2)]
        return lax.psum(a.astype(F32), "dp", axis_index_groups=groups)

    def total(self, a):
        a = a + self.swap_core(a)
        for exchange, size in ((self.from_y, self.ys), (self.from_z, self.zs)):
            if size == 2:
                a = a + exchange(a, 1)
            elif size == 4:
                a = (a + exchange(a, 2)) + (exchange(a, 1) + exchange(a, 3))
            elif size > 1:
                a = sum([exchange(a, s) for s in range(1, size)], a)
        return a

    def row(self, pos_ref, piece, rows):
        c, t, s = piece
        z = lax.rem(pos_ref[0] + s, self.zs)
        y = lax.rem(pos_ref[1] + t, self.ys)
        core = lax.rem(pos_ref[2] + c, 2)
        at = ((z * self.ys + y) * 2 + core) * rows
        return pl.multiple_of(at, math.gcd(rows, 16))


class Scatter:
    def __init__(self, plan, own, other):
        self.plan, self.own, self.other = plan, own, other
        self.rows = own.shape[0] // plan.chips

    def by_core(self):
        self.recv = self.plan.swap_core(self.other)

    def sums(self, begin, end, arrays):
        total = self.own[begin:end].astype(F32) + self.recv[begin:end].astype(F32)
        for a in arrays:
            total = total + a.astype(F32)
        return total

    def by_y(self):
        size = self.plan.zs * self.rows
        self.y_got = [
            self.plan.from_y(self.sums(t * size, (t + 1) * size, ()).astype(BF16), -t)
            for t in range(1, self.plan.ys)
        ]

    def part(self, s):
        at = slice(s * self.rows, (s + 1) * self.rows)
        return self.sums(at.start, at.stop, [a[at] for a in self.y_got])

    def by_z(self):
        parts = [self.part(s).astype(BF16) for s in range(1, self.plan.zs)]
        self.z_got = [self.plan.from_z(a, -s - 1) for s, a in enumerate(parts)]

    def total(self):
        total = self.part(0)
        for a in self.z_got:
            total = total + a.astype(F32)
        return total.astype(BF16)


def smem():
    return pl.BlockSpec(memory_space=pltpu.SMEM)


def whole(shape):
    return pl.BlockSpec(shape, lambda *_: (0,) * len(shape))


def params(mib=58):
    return pltpu.CompilerParams(
        dimension_semantics=("arbitrary",), vmem_limit_bytes=mib * MIB
    )


def cost(flops, nbytes, exps=0):
    return pl.CostEstimate(flops=int(flops), bytes_accessed=int(nbytes), transcendentals=int(exps))


def row_type(rows):
    return BF16 if rows % 16 == 0 else F32


def place(plan, pos_ref, refs, rows, out_ref):
    for i, piece in enumerate(plan.order):
        ref, at = refs[i // plan.zs], i % plan.zs * rows
        part = ref[at : at + rows, :].astype(out_ref.dtype)
        out_ref[pl.ds(plan.row(pos_ref, piece, rows), rows), :] = part


def turn(plan, pos_ref, from_ref, rows, put):
    for i, piece in enumerate(plan.order):
        put(i * rows, from_ref[pl.ds(plan.row(pos_ref, piece, rows), rows), :])


def pack_in(plan, in_weight, vec_t):
    rows = in_weight.shape[0]

    def kernel(pos_ref, w_ref, vec_ref, mlp_ref, qkv_ref):
        plane = pos_ref[3]
        gain = vec_ref[:, :1]

        def take(source, width):
            at = pl.ds(pl.multiple_of(source, PAIR), width)
            low = w_ref[:, at].astype(BF16).astype(F32)
            return (low * gain).astype(BF16)

        mlp_ref[...] = take(3 * D + plane * FH, FH)
        for pair in range(PAIRS):
            for which in range(3):
                to = pair * QKV + which * PAIR
                source = which * D + plane * DH + pair * PAIR
                qkv_ref[:, to : to + PAIR] = take(source, PAIR)
        qkv_ref[:, QW:] = vec_ref[...].astype(BF16)

    return pl.pallas_call(
        kernel,
        grid=(1,),
        in_specs=[smem(), whole(in_weight.shape), whole((rows, VEC))],
        out_specs=[whole((rows, FH)), whole((rows, QW + VEC))],
        out_shape=[
            jax.ShapeDtypeStruct((rows, FH), BF16),
            jax.ShapeDtypeStruct((rows, QW + VEC), BF16),
        ],
        compiler_params=params(16),
        cost_estimate=cost(2 * rows * 3 * D, 6 * rows * 7 * D),
        name="pack_in",
    )(plan.pos, in_weight, vec_t)


def split_out(plan, out_weight, rows):
    width = out_weight.shape[0]

    def kernel(w_ref, out_ref):
        full = w_ref[...].T.astype(BF16)
        for i in range(plan.n):
            out_ref[i] = full[i * rows : (i + 1) * rows]

    shape = (plan.n, rows, width)
    return pl.pallas_call(
        kernel,
        grid=(1,),
        in_specs=[whole(out_weight.shape)],
        out_specs=whole(shape),
        out_shape=jax.ShapeDtypeStruct(shape, BF16),
        compiler_params=params(16),
        cost_estimate=cost(0, 6 * width * D),
        name="split_out",
    )(out_weight)


def pack_out(plan, blocks):
    n, rows, width = blocks.shape

    def kernel(pos_ref, in_ref, out_ref, full_ref):
        plane = pos_ref[3]
        for i in range(n):
            full_ref[:, i * width : (i + 1) * width] = in_ref[i].astype(F32)
        mlp = full_ref[:, pl.ds(pl.multiple_of(D + plane * FH, PAIR), FH)]
        out_ref[:, :FH] = mlp.astype(BF16)
        heads = full_ref[:, pl.ds(pl.multiple_of(plane * DH, PAIR), DH)]
        out_ref[:, FH:] = heads.astype(BF16)

    return pl.pallas_call(
        kernel,
        grid=(1,),
        in_specs=[smem(), whole(blocks.shape)],
        out_specs=whole((rows, FH + DH)),
        out_shape=jax.ShapeDtypeStruct((rows, FH + DH), BF16),
        scratch_shapes=[pltpu.VMEM((rows, D + FF), F32)],
        compiler_params=params(16),
        cost_estimate=cost(rows * (D + FF), 6 * rows * D),
        name="pack_out",
    )(plan.pos, blocks)


def unpack_out(plan, own, swap):
    rows = own.shape[0]
    width = (D + FF) // plan.n

    def kernel(pos_ref, own_ref, swap_ref, out_ref, full_ref):
        first = pos_ref[3] == 0
        a, b = own_ref[...].astype(F32), swap_ref[...].astype(F32)
        for plane, part in enumerate((jnp.where(first, a, b), jnp.where(first, b, a))):
            full_ref[:, D + plane * FH : D + (plane + 1) * FH] = part[:, :FH]
            full_ref[:, plane * DH : (plane + 1) * DH] = part[:, FH:]
        for i in range(plan.n):
            out_ref[i] = full_ref[:, i * width : (i + 1) * width].astype(BF16)

    return pl.pallas_call(
        kernel,
        grid=(1,),
        in_specs=[smem(), whole(own.shape), whole(own.shape)],
        out_specs=whole((plan.n, rows, width)),
        out_shape=jax.ShapeDtypeStruct((plan.n, rows, width), BF16),
        scratch_shapes=[pltpu.VMEM((rows, D + FF), F32)],
        compiler_params=params(16),
        cost_estimate=cost(rows * (D + FF), 6 * rows * D),
        name="unpack_out",
    )(plan.pos, own, swap)


def stack(pieces):
    rows, width = pieces[0].shape

    def kernel(*refs):
        for i, ref in enumerate(refs[:-1]):
            refs[-1][i * rows : (i + 1) * rows, :] = ref[...]

    shape = (len(pieces) * rows, width)
    return pl.pallas_call(
        kernel,
        grid=(1,),
        in_specs=[whole((rows, width))] * len(pieces),
        out_specs=whole(shape),
        out_shape=jax.ShapeDtypeStruct(shape, BF16),
        compiler_params=params(8),
        cost_estimate=cost(0, 4 * shape[0] * width),
        name="stack",
    )(*pieces)


def fold(a):
    total = a[:, :PAIR]
    for i in range(1, a.shape[1] // PAIR):
        total = total + a[:, i * PAIR : (i + 1) * PAIR]
    return total


def finish_out(blocks):
    n, rows, width = blocks.shape

    def kernel(in_ref, out_ref, sq_ref):
        grad = in_ref[...].reshape(n * rows, width).astype(F32).T
        out_ref[...] = grad
        sq_ref[...] = jnp.broadcast_to(
            jnp.sum(fold(grad * grad), axis=0, keepdims=True) * 0.125, (8, PAIR)
        )

    return pl.pallas_call(
        kernel,
        grid=(1,),
        in_specs=[whole(blocks.shape)],
        out_specs=[whole((width, D)), whole((8, PAIR))],
        out_shape=[
            jax.ShapeDtypeStruct((width, D), F32),
            jax.ShapeDtypeStruct((8, PAIR), F32),
        ],
        compiler_params=params(16),
        cost_estimate=cost(4 * width * D, 6 * width * D),
        name="finish_out",
    )(blocks)


def finish_mlp(plan, own, swap, in_weight, vec_t):
    rows = in_weight.shape[0]

    def kernel(pos_ref, own_ref, swap_ref, w_ref, vec_ref, grad_ref, sq_ref, dot_ref):
        step = pl.program_id(0)

        @pl.when(step == 0)
        def _():
            sq_ref[...] = jnp.zeros_like(sq_ref)
            dot_ref[...] = jnp.zeros_like(dot_ref)

        mine = step // 2 == pos_ref[3]
        hat = jnp.where(mine, own_ref[...].astype(F32), swap_ref[...].astype(F32))
        grad = hat * vec_ref[:, :1]
        grad_ref[...] = grad
        sq_ref[...] += fold(grad * grad)
        dot_ref[...] += fold(w_ref[...].astype(BF16).astype(F32) * hat)

    part = pl.BlockSpec((rows, D), lambda j: (0, j % 2))
    columns = pl.BlockSpec((rows, D), lambda j: (0, 3 + j))
    small = jax.ShapeDtypeStruct((rows, VEC), F32)
    return pl.pallas_call(
        kernel,
        grid=(FF // D,),
        in_specs=[smem(), part, part, columns, whole((rows, VEC))],
        out_specs=[columns, whole((rows, VEC)), whole((rows, VEC))],
        out_shape=[jax.ShapeDtypeStruct(in_weight.shape, F32), small, small],
        compiler_params=params(16),
        cost_estimate=cost(8 * rows * FF, 12 * rows * FF),
        name="finish_mlp",
    )(plan.pos, own, swap, in_weight, vec_t)


def finish_qkv(plan, own, swap, in_weight, vec_t, grad, sq, dot, sq_out):
    rows = in_weight.shape[0]

    def kernel(
        pos_ref, own_ref, swap_ref, w_ref, vec_ref, _,
        sq_in_ref, dot_in_ref, sqo_ref, grad_ref, vg_ref, total_ref, sq_ref, dot_ref,
    ):
        step = pl.program_id(0)

        @pl.when(step == 0)
        def _():
            sq_ref[...] = sq_in_ref[...]
            dot_ref[...] = dot_in_ref[...]

        first = pos_ref[3] == 0
        parts = []
        for pair in range(PAIRS):
            at = pl.ds(pl.multiple_of(pair * QKV + step * PAIR, PAIR), PAIR)
            parts.append([ref[:, at].astype(F32) for ref in (own_ref, swap_ref)])
        low = [jnp.where(first, a, b) for a, b in parts]
        high = [jnp.where(first, b, a) for a, b in parts]
        hat = jnp.concatenate(low + high, axis=1)
        grad = hat * vec_ref[:, :1]
        grad_ref[...] = grad
        sq_ref[...] += fold(grad * grad)
        dot_ref[...] += fold(w_ref[...].astype(BF16).astype(F32) * hat)

        @pl.when(step == 2)
        def _():
            tail = own_ref[:, QW:].astype(F32) + swap_ref[:, QW:].astype(F32)
            gain = jnp.sum(dot_ref[...], axis=1, keepdims=True)
            lane = lax.broadcasted_iota(jnp.int32, tail.shape, 1)
            vec = jnp.where(lane == 0, gain, tail)
            vg_ref[...] = vec
            total = jnp.sum(sq_ref[...] + vec * vec, axis=0, keepdims=True)
            total_ref[...] = jnp.broadcast_to(total * 0.125, (8, PAIR)) + sqo_ref[...]

    columns = pl.BlockSpec((rows, D), lambda j: (0, j))
    small = whole((rows, VEC))
    return pl.pallas_call(
        kernel,
        grid=(3,),
        in_specs=[
            smem(), whole(own.shape), whole(own.shape), columns, small,
            pl.BlockSpec(memory_space=pl.ANY), small, small, whole((8, PAIR)),
        ],
        out_specs=[columns, small, whole((8, PAIR))],
        out_shape=[
            jax.ShapeDtypeStruct(in_weight.shape, F32),
            jax.ShapeDtypeStruct((rows, VEC), F32),
            jax.ShapeDtypeStruct((8, PAIR), F32),
        ],
        scratch_shapes=[pltpu.VMEM((rows, VEC), F32)] * 2,
        input_output_aliases={5: 0},
        compiler_params=params(16),
        cost_estimate=cost(24 * rows * D, 36 * rows * D),
        name="finish_qkv",
    )(plan.pos, own, swap, in_weight, vec_t, grad, sq, dot, sq_out)


IDS = 16


def normalize(tokens, cotangent, ids):
    tok = tokens.shape[0]

    def kernel(t_ref, c_ref, id_ref, out_ref):
        rows = t_ref[...].astype(F32)
        centre = rows - jnp.mean(rows, axis=-1, keepdims=True)
        r = lax.rsqrt(jnp.mean(centre * centre, axis=-1, keepdims=True) + norm_eps)
        out_ref[:tok, :D] = (centre * r).astype(BF16)
        out_ref[:tok, D:] = c_ref[...]
        out_ref[tok:, :] = jnp.zeros((IDS, 2 * D), BF16)
        numbers = jnp.broadcast_to(id_ref[...].astype(F32), (IDS, tok))
        out_ref[tok:, :tok] = numbers.astype(BF16)

    return pl.pallas_call(
        kernel,
        grid=(1,),
        in_specs=[whole((tok, D)), whole((tok, D)), whole((1, tok))],
        out_specs=whole((tok + IDS, 2 * D)),
        out_shape=jax.ShapeDtypeStruct((tok + IDS, 2 * D), BF16),
        compiler_params=params(16),
        cost_estimate=cost(10 * tok * D, 8 * tok * D),
        name="normalize",
    )(tokens, cotangent, ids)


def transposes(plan, xc_own, xc_other, rows):
    tok = xc_own.shape[0] - IDS
    kind = row_type(rows)

    def kernel(pos_ref, own_ref, other_ref, out_ref, sum_ref, t_ref):
        for half, ref in enumerate((own_ref, other_ref)):
            t_ref[...] = ref[...].astype(F32).T.astype(kind)

            def put(at, a):
                out_ref[0, at : at + rows, half * tok : (half + 1) * tok] = a.astype(BF16)

            turn(plan, pos_ref, t_ref, rows, put)
        total = jnp.sum(own_ref[...].astype(F32), axis=0, keepdims=True)
        sum_ref[0] = jnp.broadcast_to(total, (8, D))

    return pl.pallas_call(
        kernel,
        grid=(2,),
        in_specs=[smem()] + [pl.BlockSpec((tok, D), lambda j: (0, j))] * 2,
        out_specs=[
            pl.BlockSpec((1, D, 2 * tok), lambda j: (j, 0, 0)),
            pl.BlockSpec((1, 8, D), lambda j: (j, 0, 0)),
        ],
        out_shape=[
            jax.ShapeDtypeStruct((2, D, 2 * tok), BF16),
            jax.ShapeDtypeStruct((2, 8, D), F32),
        ],
        scratch_shapes=[pltpu.VMEM((D, tok), kind)],
        compiler_params=params(24),
        cost_estimate=cost(10 * tok * D, 16 * tok * D),
        name="transposes",
    )(plan.pos, xc_own, xc_other)


def mlp_forward(plan, xc_own, xc_other, turned, pieces):
    tok = xc_own.shape[0] - IDS
    rows = pieces[0].shape[0] // plan.zs
    tile = 512
    n = len(pieces)

    half_d = D // 2

    def kernel(pos_ref, xo_ref, xp_ref, ct_ref, *rest):
        refs, (mix_ref, slope_ref, g_own_ref, g_other_ref, w_ref) = rest[:n], rest[n:]
        place(plan, pos_ref, refs, rows, w_ref)
        w = w_ref[...].astype(BF16)
        for half, x_ref in enumerate((xo_ref, xp_ref)):
            v = mm(x_ref[...], w)
            v2 = v * v
            t = jnp.tanh(v * (GELU_C + (GELU_C * 0.044715) * v2))
            h = 0.5 + 0.5 * t
            g = v * h
            slope = h + 2.0 * g * (1.0 - h) * (GELU_C + (3.0 * GELU_C * 0.044715) * v2)
            mix_ref[half] = g.astype(BF16)
            slope_ref[half] = slope.astype(BF16)
        g = mm(ct_ref[0], mix_ref[...].reshape(2 * tok, tile)).astype(BF16)
        g_own_ref[...] = g[:half_d]
        g_other_ref[...] = g[half_d:]

    block = pl.BlockSpec((2, tok, tile), lambda j: (0, 0, j))
    grad = pl.BlockSpec((half_d, tile), lambda j: (0, j))
    return pl.pallas_call(
        kernel,
        grid=(FH // tile,),
        in_specs=[smem()]
        + [pl.BlockSpec((tok, D), lambda j: (0, 0))] * 2
        + [pl.BlockSpec((1, D, 2 * tok), lambda j: (1, 0, 0))]
        + [pl.BlockSpec((plan.zs * rows, tile), lambda j: (0, j))] * n,
        out_specs=[block, block, grad, grad],
        out_shape=[jax.ShapeDtypeStruct((2, tok, FH), BF16)] * 2
        + [jax.ShapeDtypeStruct((half_d, FH + DH), BF16)] * 2,
        scratch_shapes=[pltpu.VMEM((D, tile), row_type(rows))],
        compiler_params=params(),
        cost_estimate=cost(8 * tok * D * FH, 12 * tok * FH, 2 * tok * FH),
        name="mlp_forward",
    )(plan.pos, xc_own, xc_other, turned, *pieces)


def head_means(a, block_ref):
    high = a.astype(BF16)
    low = (a - high.astype(F32)).astype(BF16)
    return mm(high, block_ref[...]) + mm(low, block_ref[...])


def attention_forward(plan, xc_own, xc_other, pieces, block, turned, g_own, g_other):
    tok = xc_own.shape[0] - IDS
    rows = pieces[0].shape[0] // plan.zs
    n = len(pieces)

    half_d = D // 2

    def kernel(pos_ref, xo_ref, xp_ref, ido_ref, idp_ref, block_ref, ct_ref, _, __, *rest):
        refs, vec_refs = rest[:n], rest[n : 2 * n]
        (
            q_ref, k_ref, v_ref, nq_ref, nk_ref, rq_ref, rk_ref, att_ref, p_ref, gain_ref,
            g_own_ref, g_other_ref, w_ref, vs_ref,
        ) = rest[2 * n :]
        step = pl.program_id(0)

        @pl.when(step == 0)
        def _():
            place(plan, pos_ref, vec_refs, rows, vs_ref)
            gain_ref[...] = vs_ref[...].astype(F32).T[:8]

        place(plan, pos_ref, refs, rows, w_ref)
        w = w_ref[...].astype(BF16)
        column = pl.ds(pl.multiple_of(pos_ref[3] * DH + step * PAIR, PAIR), PAIR)
        q_gain = gain_ref[1:2, column] * (HD ** (-0.5))
        k_gain = gain_ref[2:3, column]
        lane = lax.broadcasted_iota(jnp.int32, (tok, PAIR), 1)
        first = lane < HD
        for half, x_ref in enumerate((xo_ref, xp_ref)):
            raw = mm(x_ref[...], w)

            def normed(a, gain, n_ref, r_ref, out_ref):
                centre = a - head_means(a, block_ref)
                r = lax.rsqrt(head_means(centre * centre, block_ref) + norm_eps)
                normal = centre * r
                n_ref[half] = normal.astype(BF16)
                r_ref[half] = r.astype(BF16)
                low = (normal * gain).astype(BF16)
                out_ref[half] = low
                return low

            q = normed(raw[:, :PAIR], q_gain, nq_ref, rq_ref, q_ref)
            k = normed(raw[:, PAIR : 2 * PAIR], k_gain, nk_ref, rk_ref, k_ref)
            v = raw[:, 2 * PAIR :].astype(BF16)
            v_ref[half] = v
            numbers = (ido_ref, idp_ref)[half][:8].astype(F32)
            same = numbers.T[:, :1] == numbers[:1]
            att = []
            zero = jnp.zeros_like(q)
            for head in range(2):
                qh = jnp.where(first, q, zero) if head == 0 else jnp.where(first, zero, q)
                e = jnp.where(same, jnp.exp(mm(qh, k, NT)), 0.0)
                p = (e * (1.0 / jnp.sum(e, axis=1, keepdims=True))).astype(BF16)
                p_ref[half, head] = p
                att.append(mm(p, v))
            att_ref[half] = jnp.where(first, att[0], att[1]).astype(BF16)
        g = mm(ct_ref[0], att_ref[...].reshape(2 * tok, PAIR)).astype(BF16)
        g_own_ref[...] = g[:half_d]
        g_other_ref[...] = g[half_d:]

    pair = pl.BlockSpec((2, tok, PAIR), lambda j: (0, 0, j))
    small = jax.ShapeDtypeStruct((2, tok, DH), BF16)
    return pl.pallas_call(
        kernel,
        grid=(PAIRS,),
        in_specs=[smem()]
        + [pl.BlockSpec((tok, D), lambda j: (0, 0))] * 2
        + [pl.BlockSpec((IDS, tok), lambda j: (tok // IDS, 0))] * 2
        + [whole((PAIR, PAIR))]
        + [pl.BlockSpec((1, D, 2 * tok), lambda j: (1, 0, 0))]
        + [pl.BlockSpec(memory_space=pl.ANY)] * 2
        + [pl.BlockSpec((plan.zs * rows, QKV), lambda j: (0, j))] * n
        + [pl.BlockSpec((plan.zs * rows, VEC), lambda j: (0, QW // VEC))] * n,
        out_specs=[pair] * 8
        + [pl.BlockSpec((2, 2, tok, tok), lambda j: (0, j, 0, 0)), whole((8, D))]
        + [pl.BlockSpec((half_d, PAIR), lambda j: (0, FH // PAIR + j))] * 2,
        out_shape=[small] * 8
        + [
            jax.ShapeDtypeStruct((2, 2 * PAIRS, tok, tok), BF16),
            jax.ShapeDtypeStruct((8, D), F32),
            jax.ShapeDtypeStruct(g_own.shape, BF16),
            jax.ShapeDtypeStruct(g_own.shape, BF16),
        ],
        input_output_aliases={7: 10, 8: 11},
        scratch_shapes=[
            pltpu.VMEM((D, QKV), row_type(rows)),
            pltpu.VMEM((D, VEC), row_type(rows)),
        ],
        compiler_params=params(),
        cost_estimate=cost(4 * tok * D * QW, 20 * MIB, 12 * tok * tok),
        name="attention_forward",
    )(
        plan.pos, xc_own, xc_other, xc_own, xc_other, block, turned, g_own, g_other,
        *pieces, *pieces,
    )


def output_columns(plan, rows, tile, steps):
    return pl.BlockSpec(
        (plan.zs * rows, tile), lambda j: (0, jnp.where(j == 0, steps - 1, j - 1))
    )


def output_step(plan, att, mixed, slope, xc_own, xc_other, pieces):
    tok = xc_own.shape[0] - IDS
    rows = pieces[0].shape[0] // plan.zs
    n = len(pieces)
    tile = DH
    steps = 1 + FH // tile

    def kernel(pos_ref, att_ref, mix_ref, slope_ref, co_ref, cp_ref, *rest):
        refs = rest[:n]
        out_own_ref, out_other_ref, d_att_ref, d_in_ref, w_ref, acc_ref = rest[n:]
        step = pl.program_id(0)
        place(plan, pos_ref, refs, rows, w_ref)
        w = w_ref[...].astype(BF16)

        @pl.when(step == 0)
        def _():
            for half, ref in enumerate((co_ref, cp_ref)):
                d_att_ref[half] = mm(ref[...], w).astype(BF16)
                acc_ref[half] = mm(att_ref[half], w, NT)

        @pl.when(step > 0)
        def _():
            for half, ref in enumerate((co_ref, cp_ref)):
                d = mm(ref[...], w)
                d_in_ref[half] = (d * slope_ref[half].astype(F32)).astype(BF16)
                acc_ref[half] += mm(mix_ref[half], w, NT)

        @pl.when(step == steps - 1)
        def _():
            out_own_ref[...] = acc_ref[0]
            out_other_ref[...] = acc_ref[1].astype(BF16)

    hidden = pl.BlockSpec((2, tok, tile), lambda j: (0, 0, jnp.maximum(j - 1, 0)))
    return pl.pallas_call(
        kernel,
        grid=(steps,),
        in_specs=[smem(), whole((2, tok, tile)), hidden, hidden]
        + [pl.BlockSpec((tok, D), lambda j: (0, 1))] * 2
        + [output_columns(plan, rows, tile, steps)] * n,
        out_specs=[whole((tok, D)), whole((tok, D)), whole((2, tok, tile)), hidden],
        out_shape=[
            jax.ShapeDtypeStruct((tok, D), F32),
            jax.ShapeDtypeStruct((tok, D), BF16),
            jax.ShapeDtypeStruct((2, tok, DH), BF16),
            jax.ShapeDtypeStruct((2, tok, FH), BF16),
        ],
        scratch_shapes=[
            pltpu.VMEM((D, tile), row_type(rows)),
            pltpu.VMEM((2, tok, D), F32),
        ],
        compiler_params=params(),
        cost_estimate=cost(8 * tok * steps * tile * D, 20 * MIB),
        name="output_step",
    )(plan.pos, att, mixed, slope, xc_own, xc_other, *pieces)


def mlp_gradient(turned, d_inner):
    tok = d_inner.shape[1]
    half_d = D // 2
    tile = 512

    def kernel(xt_ref, d_ref, g_own_ref, g_other_ref):
        g = mm(xt_ref[0], d_ref[...].reshape(2 * tok, tile)).astype(BF16)
        g_own_ref[...] = g[:half_d]
        g_other_ref[...] = g[half_d:]

    grad = pl.BlockSpec((half_d, tile), lambda j: (0, j))
    return pl.pallas_call(
        kernel,
        grid=(FH // tile,),
        in_specs=[
            pl.BlockSpec((1, D, 2 * tok), lambda j: (0, 0, 0)),
            pl.BlockSpec((2, tok, tile), lambda j: (0, 0, j)),
        ],
        out_specs=[grad, grad],
        out_shape=[jax.ShapeDtypeStruct((half_d, FH), BF16)] * 2,
        compiler_params=params(),
        cost_estimate=cost(4 * tok * D * FH, 8 * MIB),
        name="mlp_gradient",
    )(turned, d_inner)


def scaled_gradient(plan, d_inner, d_qkv, mlp_pieces, qkv_pieces):
    tok = d_inner.shape[1]
    rows = mlp_pieces[0].shape[0] // plan.zs
    n = len(mlp_pieces)
    tile = QKV
    count = FH // tile
    steps = count + PAIRS

    def kernel(pos_ref, dm_ref, dq_ref, *rest):
        refs_m, refs_q = rest[:n], rest[n : 2 * n]
        e_own_ref, e_other_ref, w_ref, acc_ref = rest[2 * n :]
        step = pl.program_id(0)

        @pl.when(step == 0)
        def _():
            acc_ref[...] = jnp.zeros_like(acc_ref)

        def add(ref):
            w = w_ref[...].astype(BF16)
            for half in range(2):
                acc_ref[half] += mm(ref[half], w, NT)

        @pl.when(step < count)
        def _():
            place(plan, pos_ref, refs_m, rows, w_ref)
            add(dm_ref)

        @pl.when(step >= count)
        def _():
            place(plan, pos_ref, refs_q, rows, w_ref)
            add(dq_ref)

        @pl.when(step == steps - 1)
        def _():
            e_own_ref[...] = acc_ref[0]
            e_other_ref[...] = acc_ref[1].astype(BF16)

    def mlp_at(j):
        return jnp.minimum(j, count - 1)

    def qkv_at(j):
        return jnp.maximum(j - count, 0)

    return pl.pallas_call(
        kernel,
        grid=(steps,),
        in_specs=[
            smem(),
            pl.BlockSpec((2, tok, tile), lambda j: (0, 0, mlp_at(j))),
            pl.BlockSpec((2, tok, tile), lambda j: (0, 0, qkv_at(j))),
        ]
        + [pl.BlockSpec((plan.zs * rows, tile), lambda j: (0, mlp_at(j)))] * n
        + [pl.BlockSpec((plan.zs * rows, tile), lambda j: (0, qkv_at(j)))] * n,
        out_specs=[whole((tok, D)), whole((tok, D))],
        out_shape=[
            jax.ShapeDtypeStruct((tok, D), F32),
            jax.ShapeDtypeStruct((tok, D), BF16),
        ],
        scratch_shapes=[
            pltpu.VMEM((D, tile), row_type(rows)),
            pltpu.VMEM((2, tok, D), F32),
        ],
        compiler_params=params(),
        cost_estimate=cost(4 * tok * steps * tile * D, 16 * MIB),
        name="scaled_gradient",
    )(plan.pos, d_inner, d_qkv, *mlp_pieces, *qkv_pieces)


def attention_backward(plan, turned, saved, d_att, block, gains, cot_sum, before, begin, end, rows):
    q, k, v, nq, nk, rq, rk, probs = saved
    tok = d_att.shape[1]
    half_d = D // 2
    kind = row_type(rows)
    width = (end - begin) * QKV + (VEC if end == PAIRS else 0)

    def kernel(pos_ref, xt_ref, q_ref, k_ref, v_ref, nq_ref, nk_ref, rq_ref, rk_ref, p_ref,
               da_ref, block_ref, gain_ref, cot_ref, *rest):
        befores = rest[: len(before)]
        g_own_ref, g_other_ref, d_ref, vec_ref, turn_ref = rest[len(before) :]
        step = pl.program_id(0) + begin

        @pl.when(step == begin)
        def _():
            if befores:
                vec_ref[...] = befores[0][...]
            else:
                vec_ref[...] = jnp.zeros_like(vec_ref)
                vec_ref[3:4, :] = cot_ref[0, :1]

        column = pl.ds(pl.multiple_of(pos_ref[3] * DH + step * PAIR, PAIR), PAIR)
        q_gain = gain_ref[1:2, column]
        k_gain = gain_ref[2:3, column]
        first = lax.broadcasted_iota(jnp.int32, (tok, PAIR), 1) < HD
        for half in range(2):
            qb, kb, vb, da = q_ref[half], k_ref[half], v_ref[half], da_ref[half]
            q_t, da_t = qb.T, da.T
            zero = jnp.zeros_like(da)
            dq, dk_t, dv_t = [], [], []
            for head in range(2):
                at = slice(head * HD, (head + 1) * HD)
                dah = jnp.where(first, da, zero) if head == 0 else jnp.where(first, zero, da)
                p_low = p_ref[half, head]
                p = p_low.astype(F32)
                t = p * mm(dah, vb, NT)
                ds = (t - p * jnp.sum(t, axis=1, keepdims=True)).astype(BF16)
                dv_t.append(mm(da_t[at], p_low))
                dk_t.append(mm(q_t[at], ds))
                dq.append(mm(ds, kb))
            d_query = jnp.where(first, dq[0], dq[1])
            d_key = jnp.concatenate(dk_t, axis=0).T
            d_value = jnp.concatenate(dv_t, axis=0).T

            def back(d, gain, n_ref, r_ref, which, factor):
                normal = n_ref[half].astype(F32)
                d = d * factor
                vec_ref[which : which + 1, column] += jnp.sum(d * normal, axis=0, keepdims=True)
                e = d * gain
                mean = head_means(e, block_ref)
                along = head_means(e * normal, block_ref)
                return (r_ref[half].astype(F32) * (e - mean - normal * along)).astype(BF16)

            d_ref[half, :, :PAIR] = back(d_query, q_gain, nq_ref, rq_ref, 1, HD ** (-0.5))
            d_ref[half, :, PAIR : 2 * PAIR] = back(d_key, k_gain, nk_ref, rk_ref, 2, 1.0)
            d_ref[half, :, 2 * PAIR :] = d_value.astype(BF16)
        g = mm(xt_ref[0], d_ref[...].reshape(2 * tok, QKV)).astype(BF16)
        at = pl.ds(pl.multiple_of((step - begin) * QKV, QKV), QKV)
        g_own_ref[:, at] = g[:half_d]
        g_other_ref[:, at] = g[half_d:]
        if end < PAIRS:
            return

        @pl.when(step == PAIRS - 1)
        def _():
            turn_ref[...] = vec_ref[...].T.astype(kind)

            def put(at, a):
                ref = g_own_ref if at < half_d else g_other_ref
                ref[at % half_d : at % half_d + rows, width - VEC :] = a.astype(BF16)

            turn(plan, pos_ref, turn_ref, rows, put)

    pair = pl.BlockSpec((2, tok, PAIR), lambda j: (0, 0, begin + j))
    return pl.pallas_call(
        kernel,
        grid=(end - begin,),
        in_specs=[smem(), pl.BlockSpec((1, D, 2 * tok), lambda j: (0, 0, 0))]
        + [pair] * 7
        + [
            pl.BlockSpec((2, 2, tok, tok), lambda j: (0, begin + j, 0, 0)),
            pair,
            whole((PAIR, PAIR)),
            whole((8, D)),
            pl.BlockSpec((1, 8, D), lambda j: (1, 0, 0)),
        ]
        + [whole(a.shape) for a in before],
        out_specs=[whole((half_d, width))] * 2
        + [pl.BlockSpec((2, tok, QKV), lambda j: (0, 0, j)), whole((VEC, D))],
        out_shape=[jax.ShapeDtypeStruct((half_d, width), BF16)] * 2
        + [
            jax.ShapeDtypeStruct((2, tok, (end - begin) * QKV), BF16),
            jax.ShapeDtypeStruct((VEC, D), F32),
        ],
        scratch_shapes=[pltpu.VMEM((D, VEC), kind)],
        compiler_params=params(),
        cost_estimate=cost(16 * tok * D * QKV * (end - begin), 8 * MIB * (end - begin)),
        name="attention_backward",
    )(
        plan.pos, turned, q, k, v, nq, nk, rq, rk, probs, d_att, block, gains, cot_sum, *before,
    )


def token_gradient(tokens, cotangent, e_own, e_recv):
    tok = tokens.shape[0]

    def kernel(t_ref, c_ref, own_ref, recv_ref, out_ref):
        rows = t_ref[...].astype(F32)
        centre = rows - jnp.mean(rows, axis=-1, keepdims=True)
        r = lax.rsqrt(jnp.mean(centre * centre, axis=-1, keepdims=True) + norm_eps)
        normal = centre * r
        e = own_ref[...] + recv_ref[...].astype(F32)
        mean = jnp.mean(e, axis=-1, keepdims=True)
        along = jnp.mean(e * normal, axis=-1, keepdims=True)
        out_ref[...] = c_ref[...].astype(F32) + r * (e - mean - normal * along)

    block = pl.BlockSpec((tok // 4, D), lambda j: (j, 0))
    return pl.pallas_call(
        kernel,
        grid=(4,),
        in_specs=[block] * 4,
        out_specs=block,
        out_shape=jax.ShapeDtypeStruct((tok, D), F32),
        compiler_params=params(16),
        cost_estimate=cost(20 * tok * D, 14 * tok * D),
        name="token_gradient",
    )(tokens, cotangent, e_own, e_recv)


def adamw(master, first, second, grad, factor):
    clipped = grad * factor
    first_new = beta_one * first + (1.0 - beta_one) * clipped
    second_new = beta_two * second + (1.0 - beta_two) * clipped * clipped
    first_hat = first_new * (1.0 / (1.0 - beta_one**ADAM_STEP))
    second_hat = second_new * (1.0 / (1.0 - beta_two**ADAM_STEP))
    update = -learning * (first_hat / (jnp.sqrt(second_hat) + epsilon) + decay_rate * master)
    return (update, first_new, second_new)


def optimize(total, vec_cols, ins, outs, vecs):
    rows, out_rows = ins[0].shape[0], outs[0].shape[0]
    steps = 3

    def kernel(total_ref, cols_ref, *refs):
        in_refs, out_refs, vec_refs, rest = refs[:4], refs[4:8], refs[8:11], refs[11:]
        vec_grad_ref, norm_ref, pad_ref = rest[0], rest[1], rest[-1]
        sums = jnp.sum(jnp.sum(total_ref[...], axis=1, keepdims=True), axis=0, keepdims=True)
        norm = jnp.sqrt(sums)
        factor = jnp.minimum(1.0, math.sqrt(PARAMS) / norm)
        for group, results in ((in_refs, rest[2:5]), (out_refs, rest[5:8])):
            for ref, value in zip(results, adamw(*[ref[...] for ref in group], factor)):
                ref[...] = value

        @pl.when(pl.program_id(0) == 0)
        def _():
            norm_ref[...] = jnp.broadcast_to(norm, (8, 128))
            pad_ref[...] = jnp.zeros_like(pad_ref)
            pad_ref[:rows] = cols_ref[...]
            grad = pad_ref[...].T[:4, :rows]
            vec_grad_ref[...] = grad
            values = adamw(*[ref[...] for ref in vec_refs], grad, factor)
            for ref, value in zip(rest[8:11], values):
                ref[...] = value

    in_block = pl.BlockSpec((rows, 7 * D // steps), lambda j: (0, j))
    out_block = pl.BlockSpec((out_rows // steps, D), lambda j: (j, 0))
    shapes = [jax.ShapeDtypeStruct(a.shape, F32) for a in (ins[0], outs[0], vecs[0])]
    return pl.pallas_call(
        kernel,
        grid=(steps,),
        in_specs=[whole((8, 128)), whole(vec_cols.shape)]
        + [in_block] * 4
        + [out_block] * 4
        + [whole(vecs[0].shape)] * 3,
        out_specs=[whole(vecs[0].shape), whole((8, 128))]
        + [in_block] * 3
        + [out_block] * 3
        + [whole(vecs[0].shape)] * 3,
        out_shape=[shapes[2], jax.ShapeDtypeStruct((8, 128), F32)]
        + [shapes[0]] * 3
        + [shapes[1]] * 3
        + [shapes[2]] * 3,
        scratch_shapes=[pltpu.VMEM((128, 128), F32)],
        compiler_params=params(16),
        cost_estimate=cost(20 * 7 * D * rows, 28 * 13 * D * rows),
        name="optimize",
    )(total, vec_cols, *ins, *outs, *vecs)


def local(
    tokens,
    cotangent,
    image_ids,
    in_weight,
    out_weight,
    vectors,
    in_moment,
    out_moment,
    vec_moment,
    in_second,
    out_second,
    vec_second,
):
    plan = Plan(lax.axis_size("fsdp"), lax.axis_size("dp"))
    rows = in_weight.shape[0]

    low_vec = vectors.astype(BF16).astype(F32)
    vec_t = jnp.pad(low_vec.T, ((0, 0), (0, VEC - 4)))
    blocks = lax.all_to_all(split_out(plan, out_weight, rows), "fsdp", 0, 0)
    mlp_piece, qkv_piece = pack_in(plan, in_weight, vec_t)
    xc_own = normalize(tokens, cotangent, image_ids[None, :])

    def z_all(piece):
        return [plan.from_z(piece, s) for s in range(1, plan.zs)]

    def y_all(column):
        return [plan.from_y(column, t) for t in range(1, plan.ys)]

    def core_all(arrays):
        return [plan.swap_core(a) for a in arrays]

    def held(groups):
        flat = iter(fence(*[a for group in groups for a in group]))
        return [[next(flat) for _ in group] for group in groups]

    mlp_z = z_all(mlp_piece)
    xc_other = plan.swap_plane(xc_own)
    mlp_z, (qkv_piece,) = held([mlp_z, [qkv_piece]])
    mlp_col = stack([mlp_piece] + mlp_z)
    mlp_y = y_all(mlp_col)
    mlp_core = core_all([mlp_col])
    qkv_z = z_all(qkv_piece)
    out_piece = pack_out(plan, blocks)
    mlp_y, mlp_core, qkv_z, (out_piece, xc_other) = held(
        [mlp_y, mlp_core, qkv_z, [out_piece, xc_other]]
    )
    mlp_pieces = [mlp_col] + mlp_y + mlp_core + core_all(mlp_y)
    qkv_col = stack([qkv_piece] + qkv_z)
    qkv_y = y_all(qkv_col)
    qkv_core = core_all([qkv_col])
    out_z = z_all(out_piece)
    turned, cot_sum = transposes(plan, xc_own, xc_other, rows)
    mixed, slope, g_own, g_other = mlp_forward(plan, xc_own, xc_other, turned, mlp_pieces)
    qkv_y, out_z, qkv_core, (mixed, slope, g_own, g_other) = held(
        [qkv_y, out_z, qkv_core, [mixed, slope, g_own, g_other]]
    )
    qkv_pieces = [qkv_col] + qkv_y + qkv_core + core_all(qkv_y)
    out_col = stack([out_piece] + out_z)
    out_y = y_all(out_col)
    out_core = core_all([out_col])
    lane = jnp.arange(PAIR) // HD
    block = jnp.where(lane[:, None] == lane[None, :], 1.0 / HD, 0.0).astype(BF16)
    *saved, att, probs, gains, g_own, g_other = attention_forward(
        plan, xc_own, xc_other, qkv_pieces, block, turned, g_own, g_other
    )
    saved = tuple(saved) + (probs,)
    out_y, out_core, (att, g_own, g_other) = held([out_y, out_core, [att, g_own, g_other]])
    s_out = Scatter(plan, g_own, g_other)
    s_out.by_core()
    out_core = out_core + core_all(out_y)
    s_out.recv, *out_core = fence(s_out.recv, *out_core)
    s_out.by_y()
    out_pieces = [out_col] + out_y + out_core
    out_mine, out_theirs, d_att, d_inner = output_step(
        plan, att, mixed, slope, xc_own, xc_other, out_pieces
    )
    s_out.y_got, (out_theirs, d_att, d_inner) = held([s_out.y_got, [out_theirs, d_att, d_inner]])
    s_out.by_z()
    g_own, g_other = mlp_gradient(turned, d_inner)
    s_mlp = Scatter(plan, g_own, g_other)
    s_mlp.by_core()
    out_recv = plan.swap_plane(out_theirs)
    s_mlp.recv, d_att = fence(s_mlp.recv, d_att)
    s_mlp.by_y()
    g_own, g_other, d_qkv, _ = attention_backward(
        plan, turned, saved, d_att, block, gains, cot_sum, (), 0, PAIRS, rows
    )
    s_out.z_got, s_mlp.y_got, (g_own, g_other, d_qkv, out_recv) = held(
        [s_out.z_got, s_mlp.y_got, [g_own, g_other, d_qkv, out_recv]]
    )
    s_qkv = Scatter(plan, g_own, g_other)
    s_qkv.by_core()
    out_sum = s_out.total()
    out_swap = plan.swap_plane(out_sum)
    s_qkv.recv, out_sum = fence(s_qkv.recv, out_sum)
    s_qkv.by_y()
    s_mlp.by_z()
    blocks = unpack_out(plan, plan.over_pairs(out_sum), plan.over_pairs(out_swap))
    result = (
        tokens.astype(F32) + out_mine + out_recv.astype(F32) + gains[3][None, :]
    ).astype(BF16)
    s_qkv.y_got, (blocks, result, d_qkv) = held([s_qkv.y_got, [blocks, result, d_qkv]])
    s_qkv.by_z()
    blocks = lax.all_to_all(blocks, "fsdp", 0, 0)
    e_own, e_other = scaled_gradient(plan, d_inner, d_qkv, mlp_pieces, qkv_pieces)
    s_qkv.z_got, s_mlp.z_got, (e_other,) = held([s_qkv.z_got, s_mlp.z_got, [e_other]])
    qkv_sum, mlp_sum = s_qkv.total(), s_mlp.total()
    qkv_swap, mlp_swap = plan.swap_plane(qkv_sum), plan.swap_plane(mlp_sum)
    out_grad, sq_out = finish_out(blocks)
    qkv_swap, mlp_swap, out_grad, e_other = fence(qkv_swap, mlp_swap, out_grad, e_other)
    e_recv = plan.swap_plane(e_other)
    in_grad, sq, dot = finish_mlp(
        plan, plan.over_pairs(mlp_sum), plan.over_pairs(mlp_swap), in_weight, vec_t
    )
    in_grad, vec_cols, square = finish_qkv(
        plan, plan.over_pairs(qkv_sum), plan.over_pairs(qkv_swap), in_weight, vec_t, in_grad,
        sq, dot, sq_out,
    )
    input_grad = token_gradient(tokens, cotangent, e_own, e_recv)
    vec_grad, norm, *updates = optimize(
        plan.total(square),
        vec_cols,
        (in_weight, in_moment, in_second, in_grad),
        (out_weight, out_moment, out_second, out_grad),
        (vectors, vec_moment, vec_second),
    )
    in_update, in_mean, in_square = updates[:3]
    out_update, out_mean, out_square = updates[3:6]
    vec_update, vec_mean, vec_square = updates[6:]
    return (
        result,
        input_grad,
        in_grad,
        out_grad,
        vec_grad,
        norm[0, 0],
        in_update,
        out_update,
        vec_update,
        in_mean,
        out_mean,
        vec_mean,
        in_square,
        out_square,
        vec_square,
    )


def solution(mesh):
    in_specs = (
        P(("dp", "fsdp"), None),
        P(("dp", "fsdp"), None),
        P(("dp", "fsdp")),
        P("fsdp", None),
        P("fsdp", None),
        P(None, "fsdp"),
        P("fsdp", None),
        P("fsdp", None),
        P(None, "fsdp"),
        P("fsdp", None),
        P("fsdp", None),
        P(None, "fsdp"),
    )
    out_specs = (
        P(("dp", "fsdp"), None),
        P(("dp", "fsdp"), None),
        P("fsdp", None),
        P("fsdp", None),
        P(None, "fsdp"),
        P(),
        P("fsdp", None),
        P("fsdp", None),
        P(None, "fsdp"),
        P("fsdp", None),
        P("fsdp", None),
        P(None, "fsdp"),
        P("fsdp", None),
        P("fsdp", None),
        P(None, "fsdp"),
    )
    return jax.shard_map(local, mesh=mesh, in_specs=in_specs, out_specs=out_specs, check_vma=False)
```

```python
import math

import jax
import jax.numpy as jnp
from jax import lax
from jax.experimental import pallas as pl
from jax.experimental.pallas import tpu as pltpu
from jax.sharding import PartitionSpec as P

D = 768
H = 12
HD = 64
FF = 3072
ADAM_STEP = 10
PARAMS = 7080960

beta_one = 0.9
beta_two = 0.95
learning = 0.03
decay_rate = 0.1
epsilon = 1e-08
norm_eps = 1e-06

F32 = jnp.float32
BF16 = jnp.bfloat16
DH = D // 2
FH = FF // 2
PAIR = 128
PAIRS = DH // PAIR
QKV = 3 * PAIR
QW = PAIRS * QKV
VEC = 128
GELU_C = math.sqrt(2.0 / math.pi)
MIB = 1 << 20

NT = (((1,), (1,)), ((), ()))
TN = (((0,), (0,)), ((), ()))


def mm(a, b, dims=(((1,), (0,)), ((), ()))):
    return lax.dot_general(a, b, dims, preferred_element_type=F32)


def fence(*arrays):
    return lax.optimization_barrier(arrays)


class Plan:
    def __init__(self, n_fsdp, n_dp):
        chips = n_fsdp // 2
        self.n, self.n_dp, self.chips = n_fsdp, n_dp, chips
        self.zs = 4 if chips % 4 == 0 else chips
        self.ys = chips // self.zs
        index = lax.axis_index("fsdp")
        self.core = index % 2
        self.y = (index // 2) % self.ys
        self.z = index // (2 * self.ys)
        self.plane = lax.axis_index("dp") % 2
        self.pos = jnp.stack([self.z, self.y, self.core, self.plane]).astype(jnp.int32)
        self.order = [
            (c, t, s) for c in range(2) for t in range(self.ys) for s in range(self.zs)
        ]

    def index(self, z, y, core):
        return ((z % self.zs) * self.ys + y % self.ys) * 2 + core

    def all(self):
        return [
            (z, y, c) for z in range(self.zs) for y in range(self.ys) for c in range(2)
        ]

    def from_z(self, a, s):
        pairs = [(self.index(z + s, y, c), self.index(z, y, c)) for z, y, c in self.all()]
        return lax.ppermute(a, "fsdp", pairs)

    def from_y(self, a, t):
        pairs = [(self.index(z, y + t, c), self.index(z, y, c)) for z, y, c in self.all()]
        return lax.ppermute(a, "fsdp", pairs)

    def swap_core(self, a):
        pairs = [(self.index(z, y, c), self.index(z, y, 1 - c)) for z, y, c in self.all()]
        return lax.ppermute(a, "fsdp", pairs)

    def swap_plane(self, a):
        return lax.ppermute(a, "dp", [(i, i ^ 1) for i in range(self.n_dp)])

    def over_pairs(self, a):
        if self.n_dp == 2:
            return a
        groups = [list(range(p, self.n_dp, 2)) for p in range(2)]
        return lax.psum(a.astype(F32), "dp", axis_index_groups=groups)

    def total(self, a):
        a = a + self.swap_core(a)
        for step, size in ((2, self.ys), (2 * self.ys, self.zs)):
            m = 1
            while m < size:
                pairs = [(i, i ^ (m * step)) for i in range(self.n)]
                a = a + lax.ppermute(a, "fsdp", pairs)
                m *= 2
        return a

    def row(self, pos_ref, piece, rows):
        c, t, s = piece
        z = lax.rem(pos_ref[0] + s, self.zs)
        y = lax.rem(pos_ref[1] + t, self.ys)
        core = lax.rem(pos_ref[2] + c, 2)
        at = ((z * self.ys + y) * 2 + core) * rows
        return pl.multiple_of(at, math.gcd(rows, 16))


class Scatter:
    def __init__(self, plan, own, other):
        self.plan, self.own, self.other = plan, own, other
        self.rows = own.shape[0] // plan.chips

    def by_core(self):
        self.recv = self.plan.swap_core(self.other)

    def sums(self, begin, end, arrays):
        total = self.own[begin:end].astype(F32) + self.recv[begin:end].astype(F32)
        for a in arrays:
            total = total + a.astype(F32)
        return total

    def y_parts(self):
        size = self.plan.zs * self.rows
        return [
            self.sums(t * size, (t + 1) * size, ()).astype(BF16)
            for t in range(1, self.plan.ys)
        ]

    def by_y(self, parts=None):
        parts = self.y_parts() if parts is None else parts
        self.y_got = [self.plan.from_y(a, -t - 1) for t, a in enumerate(parts)]

    def part(self, s):
        at = slice(s * self.rows, (s + 1) * self.rows)
        return self.sums(at.start, at.stop, [a[at] for a in self.y_got])

    def by_z(self):
        parts = [self.part(s).astype(BF16) for s in range(1, self.plan.zs)]
        self.z_got = [self.plan.from_z(a, -s - 1) for s, a in enumerate(parts)]

    def total(self):
        total = self.part(0)
        for a in self.z_got:
            total = total + a.astype(F32)
        return total.astype(BF16)


def smem():
    return pl.BlockSpec(memory_space=pltpu.SMEM)


def whole(shape):
    return pl.BlockSpec(shape, lambda *_: (0,) * len(shape))


def params(mib=58):
    return pltpu.CompilerParams(
        dimension_semantics=("arbitrary",), vmem_limit_bytes=mib * MIB
    )


def cost(flops, nbytes, exps=0):
    return pl.CostEstimate(flops=int(flops), bytes_accessed=int(nbytes), transcendentals=int(exps))


def row_type(rows):
    return BF16 if rows % 16 == 0 else F32


def place(plan, pos_ref, refs, rows, out_ref):
    for i, piece in enumerate(plan.order):
        ref, at = refs[i // plan.zs], i % plan.zs * rows
        part = ref[at : at + rows, :].astype(out_ref.dtype)
        out_ref[pl.ds(plan.row(pos_ref, piece, rows), rows), :] = part


def turn(plan, pos_ref, from_ref, rows, put):
    for i, piece in enumerate(plan.order):
        put(i * rows, from_ref[pl.ds(plan.row(pos_ref, piece, rows), rows), :])


def pack_in(plan, in_weight, vec_t):
    rows = in_weight.shape[0]

    def kernel(pos_ref, w_ref, vec_ref, mlp_ref, qkv_ref):
        plane = pos_ref[3]
        gain = vec_ref[:, :1]

        def take(source, width):
            at = pl.ds(pl.multiple_of(source, PAIR), width)
            low = w_ref[:, at].astype(BF16).astype(F32)
            return (low * gain).astype(BF16)

        mlp_ref[...] = take(3 * D + plane * FH, FH)
        for pair in range(PAIRS):
            for which in range(3):
                to = pair * QKV + which * PAIR
                source = which * D + plane * DH + pair * PAIR
                qkv_ref[:, to : to + PAIR] = take(source, PAIR)
        qkv_ref[:, QW:] = vec_ref[...].astype(BF16)

    return pl.pallas_call(
        kernel,
        grid=(1,),
        in_specs=[smem(), whole(in_weight.shape), whole((rows, VEC))],
        out_specs=[whole((rows, FH)), whole((rows, QW + VEC))],
        out_shape=[
            jax.ShapeDtypeStruct((rows, FH), BF16),
            jax.ShapeDtypeStruct((rows, QW + VEC), BF16),
        ],
        compiler_params=params(16),
        cost_estimate=cost(2 * rows * 3 * D, 6 * rows * 7 * D),
        name="pack_in",
    )(plan.pos, in_weight, vec_t)


def split_out(plan, out_weight, rows):
    width = out_weight.shape[0]

    def kernel(w_ref, out_ref):
        full = w_ref[...].T.astype(BF16)
        for i in range(plan.n):
            out_ref[i] = full[i * rows : (i + 1) * rows]

    shape = (plan.n, rows, width)
    return pl.pallas_call(
        kernel,
        grid=(1,),
        in_specs=[whole(out_weight.shape)],
        out_specs=whole(shape),
        out_shape=jax.ShapeDtypeStruct(shape, BF16),
        compiler_params=params(16),
        cost_estimate=cost(0, 6 * width * D),
        name="split_out",
    )(out_weight)


def pack_out(plan, blocks):
    n, rows, width = blocks.shape

    def kernel(pos_ref, in_ref, out_ref, full_ref):
        plane = pos_ref[3]
        for i in range(n):
            full_ref[:, i * width : (i + 1) * width] = in_ref[i].astype(F32)
        mlp = full_ref[:, pl.ds(pl.multiple_of(D + plane * FH, PAIR), FH)]
        out_ref[:, :FH] = mlp.astype(BF16)
        heads = full_ref[:, pl.ds(pl.multiple_of(plane * DH, PAIR), DH)]
        out_ref[:, FH:] = heads.astype(BF16)

    return pl.pallas_call(
        kernel,
        grid=(1,),
        in_specs=[smem(), whole(blocks.shape)],
        out_specs=whole((rows, FH + DH)),
        out_shape=jax.ShapeDtypeStruct((rows, FH + DH), BF16),
        scratch_shapes=[pltpu.VMEM((rows, D + FF), F32)],
        compiler_params=params(16),
        cost_estimate=cost(rows * (D + FF), 6 * rows * D),
        name="pack_out",
    )(plan.pos, blocks)


def unpack_out(plan, own, swap):
    rows = own.shape[0]
    width = (D + FF) // plan.n

    def kernel(pos_ref, own_ref, swap_ref, out_ref, full_ref):
        first = pos_ref[3] == 0
        a, b = own_ref[...].astype(F32), swap_ref[...].astype(F32)
        for plane, part in enumerate((jnp.where(first, a, b), jnp.where(first, b, a))):
            full_ref[:, D + plane * FH : D + (plane + 1) * FH] = part[:, :FH]
            full_ref[:, plane * DH : (plane + 1) * DH] = part[:, FH:]
        for i in range(plan.n):
            out_ref[i] = full_ref[:, i * width : (i + 1) * width].astype(BF16)

    return pl.pallas_call(
        kernel,
        grid=(1,),
        in_specs=[smem(), whole(own.shape), whole(own.shape)],
        out_specs=whole((plan.n, rows, width)),
        out_shape=jax.ShapeDtypeStruct((plan.n, rows, width), BF16),
        scratch_shapes=[pltpu.VMEM((rows, D + FF), F32)],
        compiler_params=params(16),
        cost_estimate=cost(rows * (D + FF), 6 * rows * D),
        name="unpack_out",
    )(plan.pos, own, swap)


def stack(pieces):
    rows, width = pieces[0].shape

    def kernel(*refs):
        for i, ref in enumerate(refs[:-1]):
            refs[-1][i * rows : (i + 1) * rows, :] = ref[...]

    shape = (len(pieces) * rows, width)
    return pl.pallas_call(
        kernel,
        grid=(1,),
        in_specs=[whole((rows, width))] * len(pieces),
        out_specs=whole(shape),
        out_shape=jax.ShapeDtypeStruct(shape, BF16),
        compiler_params=params(8),
        cost_estimate=cost(0, 4 * shape[0] * width),
        name="stack",
    )(*pieces)


def fold(a):
    total = a[:, :PAIR]
    for i in range(1, a.shape[1] // PAIR):
        total = total + a[:, i * PAIR : (i + 1) * PAIR]
    return total


def finish_out(blocks):
    n, rows, width = blocks.shape

    def kernel(in_ref, out_ref, sq_ref):
        grad = in_ref[...].reshape(n * rows, width).astype(F32).T
        out_ref[...] = grad
        sq_ref[...] = jnp.broadcast_to(
            jnp.sum(fold(grad * grad), axis=0, keepdims=True) * 0.125, (8, PAIR)
        )

    return pl.pallas_call(
        kernel,
        grid=(1,),
        in_specs=[whole(blocks.shape)],
        out_specs=[whole((width, D)), whole((8, PAIR))],
        out_shape=[
            jax.ShapeDtypeStruct((width, D), F32),
            jax.ShapeDtypeStruct((8, PAIR), F32),
        ],
        compiler_params=params(16),
        cost_estimate=cost(4 * width * D, 6 * width * D),
        name="finish_out",
    )(blocks)


def finish_mlp(plan, own, swap, in_weight, vec_t):
    rows = in_weight.shape[0]

    def kernel(pos_ref, own_ref, swap_ref, w_ref, vec_ref, grad_ref, sq_ref, dot_ref):
        step = pl.program_id(0)

        @pl.when(step == 0)
        def _():
            sq_ref[...] = jnp.zeros_like(sq_ref)
            dot_ref[...] = jnp.zeros_like(dot_ref)

        mine = step // 2 == pos_ref[3]
        hat = jnp.where(mine, own_ref[...].astype(F32), swap_ref[...].astype(F32))
        grad = hat * vec_ref[:, :1]
        grad_ref[...] = grad
        sq_ref[...] += fold(grad * grad)
        dot_ref[...] += fold(w_ref[...].astype(BF16).astype(F32) * hat)

    part = pl.BlockSpec((rows, D), lambda j: (0, j % 2))
    columns = pl.BlockSpec((rows, D), lambda j: (0, 3 + j))
    small = jax.ShapeDtypeStruct((rows, VEC), F32)
    return pl.pallas_call(
        kernel,
        grid=(FF // D,),
        in_specs=[smem(), part, part, columns, whole((rows, VEC))],
        out_specs=[columns, whole((rows, VEC)), whole((rows, VEC))],
        out_shape=[jax.ShapeDtypeStruct(in_weight.shape, F32), small, small],
        compiler_params=params(16),
        cost_estimate=cost(8 * rows * FF, 12 * rows * FF),
        name="finish_mlp",
    )(plan.pos, own, swap, in_weight, vec_t)


def finish_qkv(plan, own, swap, in_weight, vec_t, grad, sq, dot, sq_out):
    rows = in_weight.shape[0]

    def kernel(
        pos_ref, own_ref, swap_ref, w_ref, vec_ref, _,
        sq_in_ref, dot_in_ref, sqo_ref, grad_ref, vg_ref, total_ref, sq_ref, dot_ref,
    ):
        step = pl.program_id(0)

        @pl.when(step == 0)
        def _():
            sq_ref[...] = sq_in_ref[...]
            dot_ref[...] = dot_in_ref[...]

        first = pos_ref[3] == 0
        parts = []
        for pair in range(PAIRS):
            at = pl.ds(pl.multiple_of(pair * QKV + step * PAIR, PAIR), PAIR)
            parts.append([ref[:, at].astype(F32) for ref in (own_ref, swap_ref)])
        low = [jnp.where(first, a, b) for a, b in parts]
        high = [jnp.where(first, b, a) for a, b in parts]
        hat = jnp.concatenate(low + high, axis=1)
        grad = hat * vec_ref[:, :1]
        grad_ref[...] = grad
        sq_ref[...] += fold(grad * grad)
        dot_ref[...] += fold(w_ref[...].astype(BF16).astype(F32) * hat)

        @pl.when(step == 2)
        def _():
            tail = own_ref[:, QW:].astype(F32) + swap_ref[:, QW:].astype(F32)
            gain = jnp.sum(dot_ref[...], axis=1, keepdims=True)
            lane = lax.broadcasted_iota(jnp.int32, tail.shape, 1)
            vec = jnp.where(lane == 0, gain, tail)
            vg_ref[...] = vec
            total = jnp.sum(sq_ref[...] + vec * vec, axis=0, keepdims=True)
            total_ref[...] = jnp.broadcast_to(total * 0.125, (8, PAIR)) + sqo_ref[...]

    columns = pl.BlockSpec((rows, D), lambda j: (0, j))
    small = whole((rows, VEC))
    return pl.pallas_call(
        kernel,
        grid=(3,),
        in_specs=[
            smem(), whole(own.shape), whole(own.shape), columns, small,
            pl.BlockSpec(memory_space=pl.ANY), small, small, whole((8, PAIR)),
        ],
        out_specs=[columns, small, whole((8, PAIR))],
        out_shape=[
            jax.ShapeDtypeStruct(in_weight.shape, F32),
            jax.ShapeDtypeStruct((rows, VEC), F32),
            jax.ShapeDtypeStruct((8, PAIR), F32),
        ],
        scratch_shapes=[pltpu.VMEM((rows, VEC), F32)] * 2,
        input_output_aliases={5: 0},
        compiler_params=params(16),
        cost_estimate=cost(24 * rows * D, 36 * rows * D),
        name="finish_qkv",
    )(plan.pos, own, swap, in_weight, vec_t, grad, sq, dot, sq_out)


def prepare(plan, tokens, other_tokens, cotangent, other_cotangent, rows):
    tok = tokens.shape[0]
    kind = row_type(rows)

    def kernel(pos_ref, to_ref, tp_ref, co_ref, cp_ref, xo_ref, xp_ref, turned_ref, sum_ref, t_ref):
        for half, (from_ref, cot_ref, x_ref) in enumerate(
            ((to_ref, co_ref, xo_ref), (tp_ref, cp_ref, xp_ref))
        ):
            values = from_ref[...].astype(F32)
            centre = values - jnp.mean(values, axis=-1, keepdims=True)
            r = lax.rsqrt(jnp.mean(centre * centre, axis=-1, keepdims=True) + norm_eps)
            normal = centre * r
            x_ref[...] = normal.astype(BF16)
            cot = cot_ref[...].astype(F32)
            if half == 0:
                total = jnp.sum(cot, axis=0, keepdims=True)
                sum_ref[...] = jnp.broadcast_to(total, (8, D))
            for which, value in enumerate((normal, cot)):
                t_ref[...] = value.T.astype(kind)

                def put(at, a):
                    columns = slice(half * tok, (half + 1) * tok)
                    turned_ref[which, at : at + rows, columns] = a.astype(BF16)

                turn(plan, pos_ref, t_ref, rows, put)

    low = jax.ShapeDtypeStruct((tok, D), BF16)
    return pl.pallas_call(
        kernel,
        grid=(1,),
        in_specs=[smem()] + [whole((tok, D))] * 4,
        out_specs=[whole((tok, D))] * 2 + [whole((2, D, 2 * tok)), whole((8, D))],
        out_shape=[
            low,
            low,
            jax.ShapeDtypeStruct((2, D, 2 * tok), BF16),
            jax.ShapeDtypeStruct((8, D), F32),
        ],
        scratch_shapes=[pltpu.VMEM((D, tok), kind)],
        compiler_params=params(),
        cost_estimate=cost(40 * tok * D, 20 * tok * D),
        name="prepare",
    )(plan.pos, tokens, other_tokens, cotangent, other_cotangent)


def mlp_forward(plan, x_own, x_other, turned, pieces):
    tok = x_own.shape[0]
    rows = pieces[0].shape[0] // plan.zs
    tile = 512
    n = len(pieces)

    half_d = D // 2

    def kernel(pos_ref, xo_ref, xp_ref, ct_ref, *rest):
        refs, (mix_ref, slope_ref, g_own_ref, g_other_ref, w_ref) = rest[:n], rest[n:]
        place(plan, pos_ref, refs, rows, w_ref)
        w = w_ref[...].astype(BF16)
        for half, x_ref in enumerate((xo_ref, xp_ref)):
            v = mm(x_ref[...], w)
            v2 = v * v
            t = jnp.tanh(v * (GELU_C + (GELU_C * 0.044715) * v2))
            h = 0.5 + 0.5 * t
            g = v * h
            slope = h + 2.0 * g * (1.0 - h) * (GELU_C + (3.0 * GELU_C * 0.044715) * v2)
            mix_ref[half] = g.astype(BF16)
            slope_ref[half] = slope.astype(BF16)
        g = mm(ct_ref[0], mix_ref[...].reshape(2 * tok, tile)).astype(BF16)
        g_own_ref[...] = g[:half_d]
        g_other_ref[...] = g[half_d:]

    block = pl.BlockSpec((2, tok, tile), lambda j: (0, 0, j))
    grad = pl.BlockSpec((half_d, tile), lambda j: (0, j))
    return pl.pallas_call(
        kernel,
        grid=(FH // tile,),
        in_specs=[smem()]
        + [whole((tok, D))] * 2
        + [pl.BlockSpec((1, D, 2 * tok), lambda j: (1, 0, 0))]
        + [pl.BlockSpec((plan.zs * rows, tile), lambda j: (0, j))] * n,
        out_specs=[block, block, grad, grad],
        out_shape=[jax.ShapeDtypeStruct((2, tok, FH), BF16)] * 2
        + [jax.ShapeDtypeStruct((half_d, FH + DH), BF16)] * 2,
        scratch_shapes=[pltpu.VMEM((D, tile), row_type(rows))],
        compiler_params=params(),
        cost_estimate=cost(8 * tok * D * FH, 12 * tok * FH, 2 * tok * FH),
        name="mlp_forward",
    )(plan.pos, x_own, x_other, turned, *pieces)


def head_means(a, block_ref):
    high = a.astype(BF16)
    low = (a - high.astype(F32)).astype(BF16)
    return mm(high, block_ref[...]) + mm(low, block_ref[...])


def attention_forward(plan, x_own, x_other, pieces, ids, block, turned, g_own, g_other):
    tok = x_own.shape[0]
    rows = pieces[0].shape[0] // plan.zs
    n = len(pieces)
    half_d = D // 2

    def kernel(pos_ref, xo_ref, xp_ref, ido_ref, idp_ref, block_ref, ct_ref, _, __, *rest):
        refs, vec_refs = rest[:n], rest[n : 2 * n]
        (
            qk_ref, v_ref, n_ref, r_ref, att_ref, p_ref, gain_ref, g_own_ref, g_other_ref,
            w_ref, vs_ref, all_ref,
        ) = rest[2 * n :]
        step = pl.program_id(0)

        @pl.when(step == 0)
        def _():
            place(plan, pos_ref, vec_refs, rows, vs_ref)
            gain_ref[...] = vs_ref[...].astype(F32).T[:8]

        place(plan, pos_ref, refs, rows, w_ref)
        w = w_ref[...].astype(BF16)
        column = pl.ds(pl.multiple_of(pos_ref[3] * DH + step * PAIR, PAIR), PAIR)
        gain = jnp.concatenate(
            [gain_ref[1:2, column] * (HD ** (-0.5)), gain_ref[2:3, column]], axis=1
        )
        first = lax.broadcasted_iota(jnp.int32, (tok, PAIR), 1) < HD
        for half, x_ref in enumerate((xo_ref, xp_ref)):
            raw = mm(x_ref[...], w)
            qk = raw[:, : 2 * PAIR]
            centre = qk - head_means(qk, block_ref)
            r = lax.rsqrt(mm((centre * centre).astype(BF16), block_ref[...]) + norm_eps)
            normal = centre * r
            n_ref[half] = normal.astype(BF16)
            r_ref[half] = r.astype(BF16)
            low = (normal * gain).astype(BF16)
            qk_ref[half] = low
            q, k = low[:, :PAIR], low[:, PAIR:]
            v = raw[:, 2 * PAIR :].astype(BF16)
            v_ref[half] = v
            number = (ido_ref, idp_ref)[half][...].astype(F32)
            same = jnp.broadcast_to(number, (8, tok)).T[:, :1] == number
            att = []
            zero = jnp.zeros_like(q)
            for head in range(2):
                qh = jnp.where(first, q, zero) if head == 0 else jnp.where(first, zero, q)
                e = jnp.where(same, jnp.exp(mm(qh, k, NT)), 0.0)
                p = (e * (1.0 / jnp.sum(e, axis=1, keepdims=True))).astype(BF16)
                p_ref[half, head] = p
                att.append(mm(p, v))
            att_low = jnp.where(first, att[0], att[1]).astype(BF16)
            att_ref[half] = att_low
            at = pl.ds(pl.multiple_of(step * PAIR, PAIR), PAIR)
            all_ref[half * tok : (half + 1) * tok, at] = att_low

        @pl.when(step == PAIRS - 1)
        def _():
            g = mm(ct_ref[0], all_ref[...]).astype(BF16)
            g_own_ref[...] = g[:half_d]
            g_other_ref[...] = g[half_d:]

    pair = pl.BlockSpec((2, tok, PAIR), lambda j: (0, 0, j))
    pair2 = pl.BlockSpec((2, tok, 2 * PAIR), lambda j: (0, 0, j))
    small = jax.ShapeDtypeStruct((2, tok, DH), BF16)
    small2 = jax.ShapeDtypeStruct((2, tok, 2 * DH), BF16)
    heads = pl.BlockSpec((half_d, DH), lambda j: (0, FH // DH))
    return pl.pallas_call(
        kernel,
        grid=(PAIRS,),
        in_specs=[smem()]
        + [whole((tok, D))] * 2
        + [whole((1, tok))] * 2
        + [whole((2 * PAIR, 2 * PAIR))]
        + [pl.BlockSpec((1, D, 2 * tok), lambda j: (1, 0, 0))]
        + [pl.BlockSpec(memory_space=pl.ANY)] * 2
        + [pl.BlockSpec((plan.zs * rows, QKV), lambda j: (0, j))] * n
        + [pl.BlockSpec((plan.zs * rows, VEC), lambda j: (0, QW // VEC))] * n,
        out_specs=[pair2, pair, pair2, pair2, pair]
        + [pl.BlockSpec((2, 2, tok, tok), lambda j: (0, j, 0, 0)), whole((8, D))]
        + [heads, heads],
        out_shape=[small2, small, small2, small2, small]
        + [
            jax.ShapeDtypeStruct((2, 2 * PAIRS, tok, tok), BF16),
            jax.ShapeDtypeStruct((8, D), F32),
            jax.ShapeDtypeStruct(g_own.shape, BF16),
            jax.ShapeDtypeStruct(g_own.shape, BF16),
        ],
        input_output_aliases={7: 7, 8: 8},
        scratch_shapes=[
            pltpu.VMEM((D, QKV), row_type(rows)),
            pltpu.VMEM((D, VEC), row_type(rows)),
            pltpu.VMEM((2 * tok, DH), BF16),
        ],
        compiler_params=params(),
        cost_estimate=cost(4 * tok * D * QW, 20 * MIB, 12 * tok * tok),
        name="attention_forward",
    )(
        plan.pos, x_own, x_other, *ids, block, turned, g_own, g_other, *pieces, *pieces,
    )


TILE = 256


def token_tiles(tok):
    per = tok // TILE

    def pair(j):
        return (j // per, j % per, 0)

    def own(j):
        return jnp.minimum(j, per - 1)

    def other(j):
        return jnp.maximum(j - per, 0)

    return per, pair, own, other


def output_step(plan, att, mixed, slope, cot_own, cot_other, pieces):
    tok = cot_own.shape[0]
    rows = pieces[0].shape[0] // plan.zs
    n = len(pieces)
    per, pair, own, other = token_tiles(tok)

    def kernel(pos_ref, att_ref, mix_ref, slope_ref, co_ref, cp_ref, *rest):
        refs = rest[:n]
        out_own_ref, out_other_ref, d_att_ref, d_in_ref, w_ref = rest[n:]
        step = pl.program_id(0)

        @pl.when(step == 0)
        def _():
            place(plan, pos_ref, refs, rows, w_ref)

        w = w_ref[...].astype(BF16)
        cot = jnp.where(step < per, co_ref[...], cp_ref[...])
        for at in range(0, FH, DH):
            d = mm(cot, w[:, at : at + DH])
            slopes = slope_ref[0, :, at : at + DH].astype(F32)
            d_in_ref[0, :, at : at + DH] = (d * slopes).astype(BF16)
        d_att_ref[0] = mm(cot, w[:, FH:]).astype(BF16)
        out = mm(mix_ref[0], w[:, :FH], NT) + mm(att_ref[0], w[:, FH:], NT)

        @pl.when(step < per)
        def _():
            out_own_ref[...] = out

        @pl.when(step >= per)
        def _():
            out_other_ref[...] = out.astype(BF16)

    return pl.pallas_call(
        kernel,
        grid=(2 * per,),
        in_specs=[
            smem(),
            pl.BlockSpec((1, TILE, DH), pair),
            pl.BlockSpec((1, TILE, FH), pair),
            pl.BlockSpec((1, TILE, FH), pair),
            pl.BlockSpec((TILE, D), lambda j: (own(j), 0)),
            pl.BlockSpec((TILE, D), lambda j: (other(j), 0)),
        ]
        + [whole(pieces[0].shape)] * n,
        out_specs=[
            pl.BlockSpec((TILE, D), lambda j: (own(j), 0)),
            pl.BlockSpec((TILE, D), lambda j: (other(j), 0)),
            pl.BlockSpec((1, TILE, DH), pair),
            pl.BlockSpec((1, TILE, FH), pair),
        ],
        out_shape=[
            jax.ShapeDtypeStruct((tok, D), F32),
            jax.ShapeDtypeStruct((tok, D), BF16),
            jax.ShapeDtypeStruct((2, tok, DH), BF16),
            jax.ShapeDtypeStruct((2, tok, FH), BF16),
        ],
        scratch_shapes=[pltpu.VMEM((D, FH + DH), row_type(rows))],
        compiler_params=params(),
        cost_estimate=cost(8 * tok * (FH + DH) * D, 20 * MIB),
        name="output_step",
    )(plan.pos, att, mixed, slope, cot_own, cot_other, *pieces)


def mlp_gradient(turned, d_inner):
    tok = d_inner.shape[1]
    half_d = D // 2
    tile = 512

    def kernel(xt_ref, d_ref, g_own_ref, g_other_ref):
        g = mm(xt_ref[0], d_ref[...].reshape(2 * tok, tile)).astype(BF16)
        g_own_ref[...] = g[:half_d]
        g_other_ref[...] = g[half_d:]

    grad = pl.BlockSpec((half_d, tile), lambda j: (0, j))
    return pl.pallas_call(
        kernel,
        grid=(FH // tile,),
        in_specs=[
            pl.BlockSpec((1, D, 2 * tok), lambda j: (0, 0, 0)),
            pl.BlockSpec((2, tok, tile), lambda j: (0, 0, j)),
        ],
        out_specs=[grad, grad],
        out_shape=[jax.ShapeDtypeStruct((half_d, FH), BF16)] * 2,
        compiler_params=params(),
        cost_estimate=cost(4 * tok * D * FH, 8 * MIB),
        name="mlp_gradient",
    )(turned, d_inner)


def scaled_gradient(plan, d_inner, d_qkv, mlp_pieces, qkv_pieces):
    tok = d_inner.shape[1]
    rows = mlp_pieces[0].shape[0] // plan.zs
    n = len(mlp_pieces)
    per, pair, own, other = token_tiles(tok)

    def kernel(pos_ref, dm_ref, dq_ref, *rest):
        refs_m, refs_q = rest[:n], rest[n : 2 * n]
        e_own_ref, e_other_ref, wm_ref, wq_ref = rest[2 * n :]
        step = pl.program_id(0)

        @pl.when(step == 0)
        def _():
            place(plan, pos_ref, refs_m, rows, wm_ref)
            place(plan, pos_ref, refs_q, rows, wq_ref)

        e = mm(dm_ref[0], wm_ref[...].astype(BF16), NT)
        e = e + mm(dq_ref[0], wq_ref[...].astype(BF16)[:, :QW], NT)

        @pl.when(step < per)
        def _():
            e_own_ref[...] = e

        @pl.when(step >= per)
        def _():
            e_other_ref[...] = e.astype(BF16)

    return pl.pallas_call(
        kernel,
        grid=(2 * per,),
        in_specs=[
            smem(),
            pl.BlockSpec((1, TILE, FH), pair),
            pl.BlockSpec((1, TILE, QW), pair),
        ]
        + [whole(mlp_pieces[0].shape)] * n
        + [whole(qkv_pieces[0].shape)] * n,
        out_specs=[
            pl.BlockSpec((TILE, D), lambda j: (own(j), 0)),
            pl.BlockSpec((TILE, D), lambda j: (other(j), 0)),
        ],
        out_shape=[
            jax.ShapeDtypeStruct((tok, D), F32),
            jax.ShapeDtypeStruct((tok, D), BF16),
        ],
        scratch_shapes=[
            pltpu.VMEM((D, FH), row_type(rows)),
            pltpu.VMEM((D, QW + VEC), row_type(rows)),
        ],
        compiler_params=params(),
        cost_estimate=cost(4 * tok * (FH + QW) * D, 16 * MIB),
        name="scaled_gradient",
    )(plan.pos, d_inner, d_qkv, *mlp_pieces, *qkv_pieces)


def attention_backward(plan, turned, saved, d_att, block, gains, cot_sum, rows):
    qk, v, normals, factors, probs = saved
    tok = d_att.shape[1]
    half_d = D // 2
    kind = row_type(rows)

    def kernel(pos_ref, xt_ref, qk_ref, v_ref, n_ref, r_ref, p_ref, da_ref, block_ref, gain_ref,
               cot_ref, g_own_ref, g_other_ref, d_ref, vec_ref, turn_ref):
        step = pl.program_id(0)

        @pl.when(step == 0)
        def _():
            vec_ref[...] = jnp.zeros_like(vec_ref)
            vec_ref[3:4, :] = cot_ref[:1]

        column = pl.ds(pl.multiple_of(pos_ref[3] * DH + step * PAIR, PAIR), PAIR)
        gain = jnp.concatenate(
            [gain_ref[1:2, column] * (HD ** (-0.5)), gain_ref[2:3, column]], axis=1
        )
        first = lax.broadcasted_iota(jnp.int32, (tok, PAIR), 1) < HD

        def heads(a):
            zero = jnp.zeros_like(a)
            return jnp.concatenate([jnp.where(first, a, zero), jnp.where(first, zero, a)], axis=0)

        for half in range(2):
            qb, kb, vb = qk_ref[half, :, :PAIR], qk_ref[half, :, PAIR:], v_ref[half]
            da = heads(da_ref[half])
            p_low = p_ref[half].reshape(2 * tok, tok)
            p = p_low.astype(F32)
            t = p * mm(da, vb, NT)
            ds = (t - p * jnp.sum(t, axis=1, keepdims=True)).astype(BF16)
            d_value = mm(da.T, p_low).T
            d_key = mm(heads(qb).T, ds).T
            dq = mm(ds, kb)
            d_query = jnp.where(first, dq[:tok], dq[tok:])
            d = jnp.concatenate([d_query, d_key], axis=1)
            normal = n_ref[half].astype(F32)
            sums = jnp.sum(d * normal, axis=0, keepdims=True)
            vec_ref[1:2, column] += sums[:, :PAIR] * (HD ** (-0.5))
            vec_ref[2:3, column] += sums[:, PAIR:]
            e = d * gain
            along = mm((e * normal).astype(BF16), block_ref[...])
            d_raw = r_ref[half].astype(F32) * (e - head_means(e, block_ref) - normal * along)
            d_ref[half, :, : 2 * PAIR] = d_raw.astype(BF16)
            d_ref[half, :, 2 * PAIR :] = d_value.astype(BF16)
        g = mm(xt_ref[0], d_ref[...].reshape(2 * tok, QKV)).astype(BF16)
        at = pl.ds(pl.multiple_of(step * QKV, QKV), QKV)
        g_own_ref[:, at] = g[:half_d]
        g_other_ref[:, at] = g[half_d:]

        @pl.when(step == PAIRS - 1)
        def _():
            turn_ref[...] = vec_ref[...].T.astype(kind)

            def put(at, a):
                ref = g_own_ref if at < half_d else g_other_ref
                ref[at % half_d : at % half_d + rows, QW:] = a.astype(BF16)

            turn(plan, pos_ref, turn_ref, rows, put)

    pair = pl.BlockSpec((2, tok, PAIR), lambda j: (0, 0, j))
    pair2 = pl.BlockSpec((2, tok, 2 * PAIR), lambda j: (0, 0, j))
    return pl.pallas_call(
        kernel,
        grid=(PAIRS,),
        in_specs=[smem(), pl.BlockSpec((1, D, 2 * tok), lambda j: (0, 0, 0))]
        + [pair2, pair, pair2, pair2]
        + [
            pl.BlockSpec((2, 2, tok, tok), lambda j: (0, j, 0, 0)),
            pair,
            whole((2 * PAIR, 2 * PAIR)),
            whole((8, D)),
            whole((8, D)),
        ],
        out_specs=[whole((half_d, QW + VEC))] * 2
        + [pl.BlockSpec((2, tok, QKV), lambda j: (0, 0, j))],
        out_shape=[jax.ShapeDtypeStruct((half_d, QW + VEC), BF16)] * 2
        + [jax.ShapeDtypeStruct((2, tok, QW), BF16)],
        scratch_shapes=[pltpu.VMEM((VEC, D), F32), pltpu.VMEM((D, VEC), kind)],
        compiler_params=params(),
        cost_estimate=cost(16 * tok * D * QW, 24 * MIB),
        name="attention_backward",
    )(plan.pos, turned, qk, v, normals, factors, probs, d_att, block, gains, cot_sum)


def token_gradient(tokens, cotangent, e_own, e_recv):
    tok = tokens.shape[0]

    def kernel(t_ref, c_ref, own_ref, recv_ref, out_ref):
        rows = t_ref[...].astype(F32)
        centre = rows - jnp.mean(rows, axis=-1, keepdims=True)
        r = lax.rsqrt(jnp.mean(centre * centre, axis=-1, keepdims=True) + norm_eps)
        normal = centre * r
        e = own_ref[...] + recv_ref[...].astype(F32)
        mean = jnp.mean(e, axis=-1, keepdims=True)
        along = jnp.mean(e * normal, axis=-1, keepdims=True)
        out_ref[...] = c_ref[...].astype(F32) + r * (e - mean - normal * along)

    block = pl.BlockSpec((tok // 4, D), lambda j: (j, 0))
    return pl.pallas_call(
        kernel,
        grid=(4,),
        in_specs=[block] * 4,
        out_specs=block,
        out_shape=jax.ShapeDtypeStruct((tok, D), F32),
        compiler_params=params(16),
        cost_estimate=cost(20 * tok * D, 14 * tok * D),
        name="token_gradient",
    )(tokens, cotangent, e_own, e_recv)


def adamw(master, first, second, grad, factor):
    clipped = grad * factor
    first_new = beta_one * first + (1.0 - beta_one) * clipped
    second_new = beta_two * second + (1.0 - beta_two) * clipped * clipped
    first_hat = first_new * (1.0 / (1.0 - beta_one**ADAM_STEP))
    second_hat = second_new * (1.0 / (1.0 - beta_two**ADAM_STEP))
    update = -learning * (first_hat / (jnp.sqrt(second_hat) + epsilon) + decay_rate * master)
    return (update, first_new, second_new)


def optimize(total, vec_cols, ins, outs, vecs):
    rows, out_rows = ins[0].shape[0], outs[0].shape[0]
    steps = 3

    def kernel(total_ref, cols_ref, *refs):
        in_refs, out_refs, vec_refs, rest = refs[:4], refs[4:8], refs[8:11], refs[11:]
        vec_grad_ref, norm_ref, pad_ref = rest[0], rest[1], rest[-1]
        sums = jnp.sum(jnp.sum(total_ref[...], axis=1, keepdims=True), axis=0, keepdims=True)
        norm = jnp.sqrt(sums)
        factor = jnp.minimum(1.0, math.sqrt(PARAMS) / norm)
        for group, results in ((in_refs, rest[2:5]), (out_refs, rest[5:8])):
            for ref, value in zip(results, adamw(*[ref[...] for ref in group], factor)):
                ref[...] = value

        @pl.when(pl.program_id(0) == 0)
        def _():
            norm_ref[...] = norm
            pad_ref[...] = jnp.zeros_like(pad_ref)
            pad_ref[:rows] = cols_ref[...]
            grad = pad_ref[...].T[:4, :rows]
            vec_grad_ref[...] = grad
            values = adamw(*[ref[...] for ref in vec_refs], grad, factor)
            for ref, value in zip(rest[8:11], values):
                ref[...] = value

    in_block = pl.BlockSpec((rows, 7 * D // steps), lambda j: (0, j))
    out_block = pl.BlockSpec((out_rows // steps, D), lambda j: (j, 0))
    shapes = [jax.ShapeDtypeStruct(a.shape, F32) for a in (ins[0], outs[0], vecs[0])]
    return pl.pallas_call(
        kernel,
        grid=(steps,),
        in_specs=[whole((8, 128)), whole(vec_cols.shape)]
        + [in_block] * 4
        + [out_block] * 4
        + [whole(vecs[0].shape)] * 3,
        out_specs=[whole(vecs[0].shape), whole((1, 1))]
        + [in_block] * 3
        + [out_block] * 3
        + [whole(vecs[0].shape)] * 3,
        out_shape=[shapes[2], jax.ShapeDtypeStruct((1, 1), F32)]
        + [shapes[0]] * 3
        + [shapes[1]] * 3
        + [shapes[2]] * 3,
        scratch_shapes=[pltpu.VMEM((128, 128), F32)],
        compiler_params=params(16),
        cost_estimate=cost(20 * 7 * D * rows, 28 * 13 * D * rows),
        name="optimize",
    )(total, vec_cols, *ins, *outs, *vecs)


def local(
    tokens,
    cotangent,
    image_ids,
    in_weight,
    out_weight,
    vectors,
    in_moment,
    out_moment,
    vec_moment,
    in_second,
    out_second,
    vec_second,
):
    plan = Plan(lax.axis_size("fsdp"), lax.axis_size("dp"))
    rows = in_weight.shape[0]

    low_vec = vectors.astype(BF16).astype(F32)
    vec_t = jnp.pad(low_vec.T, ((0, 0), (0, VEC - 4)))
    mlp_piece, qkv_piece = pack_in(plan, in_weight, vec_t)
    other_tokens = plan.swap_plane(tokens)
    other_cotangent = plan.swap_plane(cotangent)
    blocks = lax.all_to_all(split_out(plan, out_weight, rows), "fsdp", 0, 0)

    def z_all(piece):
        return [plan.from_z(piece, s) for s in range(1, plan.zs)]

    def y_all(column):
        return [plan.from_y(column, t) for t in range(1, plan.ys)]

    def core_all(arrays):
        return [plan.swap_core(a) for a in arrays]

    def held(groups):
        flat = iter(fence(*[a for group in groups for a in group]))
        return [[next(flat) for _ in group] for group in groups]

    mlp_z = z_all(mlp_piece)
    mlp_z, (qkv_piece,) = held([mlp_z, [qkv_piece]])
    mlp_col = stack([mlp_piece] + mlp_z)
    mlp_y = y_all(mlp_col)
    qkv_z = z_all(qkv_piece)
    out_piece = pack_out(plan, blocks)
    x_own, x_other, turned, cot_sum = prepare(
        plan, tokens, other_tokens, cotangent, other_cotangent, rows
    )
    mlp_y, qkv_z, (mlp_col, out_piece, x_own) = held(
        [mlp_y, qkv_z, [mlp_col, out_piece, x_own]]
    )
    mlp_pieces = [mlp_col] + mlp_y + core_all([mlp_col] + mlp_y)
    qkv_col = stack([qkv_piece] + qkv_z)
    qkv_y = y_all(qkv_col)
    out_z = z_all(out_piece)
    mixed, slope, g_own, g_other = mlp_forward(plan, x_own, x_other, turned, mlp_pieces)
    qkv_y, out_z, (qkv_col, mixed, slope, g_own, g_other, ids_now) = held(
        [qkv_y, out_z, [qkv_col, mixed, slope, g_own, g_other, image_ids]]
    )
    other_ids = plan.swap_plane(ids_now)
    qkv_pieces = [qkv_col] + qkv_y + core_all([qkv_col] + qkv_y)
    out_col = stack([out_piece] + out_z)
    out_y = y_all(out_col)
    out_core = core_all([out_col])
    lane = jnp.arange(2 * PAIR) // HD
    block = jnp.where(lane[:, None] == lane[None, :], 1.0 / HD, 0.0).astype(BF16)
    *saved, att, probs, gains, g_own, g_other = attention_forward(
        plan, x_own, x_other, qkv_pieces, (image_ids[None, :], other_ids[None, :]), block,
        turned, g_own, g_other,
    )
    saved = tuple(saved) + (probs,)
    out_y, out_core, (att, g_own, g_other) = held([out_y, out_core, [att, g_own, g_other]])
    s_out = Scatter(plan, g_own, g_other)
    s_out.by_core()
    out_core = out_core + core_all(out_y)
    s_out.recv, *out_core = fence(s_out.recv, *out_core)
    s_out.by_y()
    out_pieces = [out_col] + out_y + out_core
    out_mine, out_theirs, d_att, d_inner = output_step(
        plan, att, mixed, slope, cotangent, other_cotangent, out_pieces
    )
    g_own, g_other = mlp_gradient(turned, d_inner)
    s_mlp = Scatter(plan, g_own, g_other)
    s_mlp.by_core()
    s_out.y_got, (out_theirs, g_own) = held([s_out.y_got, [out_theirs, g_own]])
    s_out.by_z()
    out_recv = plan.swap_plane(out_theirs)
    s_mlp.recv, d_att = fence(s_mlp.recv, d_att)
    s_mlp.by_y()
    g_own, g_other, d_qkv = attention_backward(
        plan, turned, saved, d_att, block, gains, cot_sum, rows
    )
    s_out.z_got, s_mlp.y_got, (g_own, g_other, d_qkv, out_recv) = held(
        [s_out.z_got, s_mlp.y_got, [g_own, g_other, d_qkv, out_recv]]
    )
    s_qkv = Scatter(plan, g_own, g_other)
    s_qkv.by_core()
    out_sum = s_out.total()
    out_swap = plan.swap_plane(out_sum)
    parts, s_mlp.y_got, (out_sum, d_qkv) = held([s_qkv.y_parts(), s_mlp.y_got, [out_sum, d_qkv]])
    s_qkv.by_y(parts)
    s_mlp.by_z()
    e_own, e_other = scaled_gradient(plan, d_inner, d_qkv, mlp_pieces, qkv_pieces)
    out_swap, e_other, e_own = fence(out_swap, e_other, e_own)
    e_recv = plan.swap_plane(e_other)
    blocks = unpack_out(plan, plan.over_pairs(out_sum), plan.over_pairs(out_swap))
    s_qkv.y_got, s_mlp.z_got, (blocks,) = held([s_qkv.y_got, s_mlp.z_got, [blocks]])
    s_qkv.by_z()
    blocks = lax.all_to_all(blocks, "fsdp", 0, 0)
    result = (
        tokens.astype(F32) + out_mine + out_recv.astype(F32) + gains[3][None, :]
    ).astype(BF16)
    mlp_sum = s_mlp.total()
    mlp_swap = plan.swap_plane(mlp_sum)
    s_qkv.z_got, (result,) = held([s_qkv.z_got, [result]])
    qkv_sum = s_qkv.total()
    qkv_swap = plan.swap_plane(qkv_sum)
    out_grad, sq_out = finish_out(blocks)
    in_grad, sq, dot = finish_mlp(
        plan, plan.over_pairs(mlp_sum), plan.over_pairs(mlp_swap), in_weight, vec_t
    )
    qkv_swap, in_grad, out_grad = fence(qkv_swap, in_grad, out_grad)
    in_grad, vec_cols, square = finish_qkv(
        plan, plan.over_pairs(qkv_sum), plan.over_pairs(qkv_swap), in_weight, vec_t, in_grad,
        sq, dot, sq_out,
    )
    input_grad = token_gradient(tokens, cotangent, e_own, e_recv)
    vec_grad, norm, *updates = optimize(
        plan.total(square),
        vec_cols,
        (in_weight, in_moment, in_second, in_grad),
        (out_weight, out_moment, out_second, out_grad),
        (vectors, vec_moment, vec_second),
    )
    in_update, in_mean, in_square = updates[:3]
    out_update, out_mean, out_square = updates[3:6]
    vec_update, vec_mean, vec_square = updates[6:]
    return (
        result,
        input_grad,
        in_grad,
        out_grad,
        vec_grad,
        norm.reshape(()),
        in_update,
        out_update,
        vec_update,
        in_mean,
        out_mean,
        vec_mean,
        in_square,
        out_square,
        vec_square,
    )


def solution(mesh):
    in_specs = (
        P(("dp", "fsdp"), None),
        P(("dp", "fsdp"), None),
        P(("dp", "fsdp")),
        P("fsdp", None),
        P("fsdp", None),
        P(None, "fsdp"),
        P("fsdp", None),
        P("fsdp", None),
        P(None, "fsdp"),
        P("fsdp", None),
        P("fsdp", None),
        P(None, "fsdp"),
    )
    out_specs = (
        P(("dp", "fsdp"), None),
        P(("dp", "fsdp"), None),
        P("fsdp", None),
        P("fsdp", None),
        P(None, "fsdp"),
        P(),
        P("fsdp", None),
        P("fsdp", None),
        P(None, "fsdp"),
        P("fsdp", None),
        P("fsdp", None),
        P(None, "fsdp"),
        P("fsdp", None),
        P("fsdp", None),
        P(None, "fsdp"),
    )
    return jax.shard_map(local, mesh=mesh, in_specs=in_specs, out_specs=out_specs, check_vma=False)
```

```python
import math

import jax
import jax.numpy as jnp
from jax import lax
from jax.experimental import pallas as pl
from jax.experimental.pallas import tpu as pltpu
from jax.sharding import PartitionSpec as P

D = 768
H = 12
HD = 64
FF = 3072
ADAM_STEP = 10
PARAMS = 7080960

beta_one = 0.9
beta_two = 0.95
learning = 0.03
decay_rate = 0.1
epsilon = 1e-08
norm_eps = 1e-06

F32 = jnp.float32
BF16 = jnp.bfloat16
DH = D // 2
FH = FF // 2
PAIR = 128
PAIRS = DH // PAIR
QKV = 3 * PAIR
QW = PAIRS * QKV
VEC = 128
GELU_C = math.sqrt(2.0 / math.pi)
MIB = 1 << 20

NT = (((1,), (1,)), ((), ()))
TN = (((0,), (0,)), ((), ()))


def mm(a, b, dims=(((1,), (0,)), ((), ()))):
    return lax.dot_general(a, b, dims, preferred_element_type=F32)


def fence(*arrays):
    return lax.optimization_barrier(arrays)


class Plan:
    def __init__(self, n_fsdp, n_dp):
        chips = n_fsdp // 2
        self.n, self.n_dp, self.chips = n_fsdp, n_dp, chips
        self.zs = 4 if chips % 4 == 0 else chips
        self.ys = chips // self.zs
        index = lax.axis_index("fsdp")
        self.core = index % 2
        self.y = (index // 2) % self.ys
        self.z = index // (2 * self.ys)
        self.plane = lax.axis_index("dp") % 2
        self.pos = jnp.stack([self.z, self.y, self.core, self.plane]).astype(jnp.int32)
        self.order = [
            (c, t, s) for c in range(2) for t in range(self.ys) for s in range(self.zs)
        ]

    def index(self, z, y, core):
        return ((z % self.zs) * self.ys + y % self.ys) * 2 + core

    def all(self):
        return [
            (z, y, c) for z in range(self.zs) for y in range(self.ys) for c in range(2)
        ]

    def from_z(self, a, s):
        pairs = [(self.index(z + s, y, c), self.index(z, y, c)) for z, y, c in self.all()]
        return lax.ppermute(a, "fsdp", pairs)

    def from_y(self, a, t):
        pairs = [(self.index(z, y + t, c), self.index(z, y, c)) for z, y, c in self.all()]
        return lax.ppermute(a, "fsdp", pairs)

    def swap_core(self, a):
        pairs = [(self.index(z, y, c), self.index(z, y, 1 - c)) for z, y, c in self.all()]
        return lax.ppermute(a, "fsdp", pairs)

    def swap_plane(self, a):
        return lax.ppermute(a, "dp", [(i, i ^ 1) for i in range(self.n_dp)])

    def over_pairs(self, a):
        if self.n_dp == 2:
            return a
        groups = [list(range(p, self.n_dp, 2)) for p in range(2)]
        return lax.psum(a.astype(F32), "dp", axis_index_groups=groups)

    def total(self, a, *beside):
        a = a + self.swap_core(a)
        beside = list(beside)
        count = 0
        for step, size in ((2, self.ys), (2 * self.ys, self.zs)):
            m = 1
            while m < size:
                pairs = [(i, i ^ (m * step)) for i in range(self.n)]
                got = lax.ppermute(a, "fsdp", pairs)
                if count < len(beside):
                    got, beside[count] = fence(got, beside[count])
                a = a + got
                m, count = 2 * m, count + 1
        return [a] + beside

    def row(self, pos_ref, piece, rows):
        c, t, s = piece
        z = lax.rem(pos_ref[0] + s, self.zs)
        y = lax.rem(pos_ref[1] + t, self.ys)
        core = lax.rem(pos_ref[2] + c, 2)
        at = ((z * self.ys + y) * 2 + core) * rows
        return pl.multiple_of(at, math.gcd(rows, 16))


class Scatter:
    def __init__(self, plan, own, other):
        self.plan, self.own, self.other = plan, own, other
        self.rows = own.shape[0] // plan.chips

    def by_core(self):
        self.recv = self.plan.swap_core(self.other)

    def sums(self, begin, end, arrays):
        total = self.own[begin:end].astype(F32) + self.recv[begin:end].astype(F32)
        for a in arrays:
            total = total + a.astype(F32)
        return total

    def y_parts(self):
        size = self.plan.zs * self.rows
        return [
            self.sums(t * size, (t + 1) * size, ()).astype(BF16)
            for t in range(1, self.plan.ys)
        ]

    def by_y(self, parts=None):
        parts = self.y_parts() if parts is None else parts
        self.y_got = [self.plan.from_y(a, -t - 1) for t, a in enumerate(parts)]

    def part(self, s):
        at = slice(s * self.rows, (s + 1) * self.rows)
        return self.sums(at.start, at.stop, [a[at] for a in self.y_got])

    def by_z(self):
        parts = [self.part(s).astype(BF16) for s in range(1, self.plan.zs)]
        self.z_got = [self.plan.from_z(a, -s - 1) for s, a in enumerate(parts)]

    def total(self):
        total = self.part(0)
        for a in self.z_got:
            total = total + a.astype(F32)
        return total.astype(BF16)


def smem():
    return pl.BlockSpec(memory_space=pltpu.SMEM)


def whole(shape):
    return pl.BlockSpec(shape, lambda *_: (0,) * len(shape))


def params(mib=58):
    return pltpu.CompilerParams(
        dimension_semantics=("arbitrary",), vmem_limit_bytes=mib * MIB
    )


def cost(flops, nbytes, exps=0):
    return pl.CostEstimate(flops=int(flops), bytes_accessed=int(nbytes), transcendentals=int(exps))


def row_type(rows):
    return BF16 if rows % 16 == 0 else F32


def place(plan, pos_ref, refs, rows, out_ref):
    for i, piece in enumerate(plan.order):
        ref, at = refs[i // plan.zs], i % plan.zs * rows
        part = ref[at : at + rows, :].astype(out_ref.dtype)
        out_ref[pl.ds(plan.row(pos_ref, piece, rows), rows), :] = part


def turn(plan, pos_ref, from_ref, rows, put):
    for i, piece in enumerate(plan.order):
        put(i * rows, from_ref[pl.ds(plan.row(pos_ref, piece, rows), rows), :])


def pack_in(plan, in_weight, vec_t):
    rows = in_weight.shape[0]

    def kernel(pos_ref, w_ref, vec_ref, mlp_ref, qkv_ref):
        plane = pos_ref[3]
        gain = vec_ref[:, :1]

        def take(source, width):
            at = pl.ds(pl.multiple_of(source, PAIR), width)
            low = w_ref[:, at].astype(BF16).astype(F32)
            return (low * gain).astype(BF16)

        mlp_ref[...] = take(3 * D + plane * FH, FH)
        for pair in range(PAIRS):
            for which in range(3):
                to = pair * QKV + which * PAIR
                source = which * D + plane * DH + pair * PAIR
                qkv_ref[:, to : to + PAIR] = take(source, PAIR)
        qkv_ref[:, QW:] = vec_ref[...].astype(BF16)

    return pl.pallas_call(
        kernel,
        grid=(1,),
        in_specs=[smem(), whole(in_weight.shape), whole((rows, VEC))],
        out_specs=[whole((rows, FH)), whole((rows, QW + VEC))],
        out_shape=[
            jax.ShapeDtypeStruct((rows, FH), BF16),
            jax.ShapeDtypeStruct((rows, QW + VEC), BF16),
        ],
        compiler_params=params(16),
        cost_estimate=cost(2 * rows * 3 * D, 6 * rows * 7 * D),
        name="pack_in",
    )(plan.pos, in_weight, vec_t)


def split_out(plan, out_weight, rows):
    width = out_weight.shape[0]

    def kernel(w_ref, out_ref):
        full = w_ref[...].T.astype(BF16)
        for i in range(plan.n):
            out_ref[i] = full[i * rows : (i + 1) * rows]

    shape = (plan.n, rows, width)
    return pl.pallas_call(
        kernel,
        grid=(1,),
        in_specs=[whole(out_weight.shape)],
        out_specs=whole(shape),
        out_shape=jax.ShapeDtypeStruct(shape, BF16),
        compiler_params=params(16),
        cost_estimate=cost(0, 6 * width * D),
        name="split_out",
    )(out_weight)


def pack_out(plan, blocks):
    n, rows, width = blocks.shape

    def kernel(pos_ref, in_ref, out_ref, full_ref):
        plane = pos_ref[3]
        for i in range(n):
            full_ref[:, i * width : (i + 1) * width] = in_ref[i].astype(F32)
        mlp = full_ref[:, pl.ds(pl.multiple_of(D + plane * FH, PAIR), FH)]
        out_ref[:, :FH] = mlp.astype(BF16)
        heads = full_ref[:, pl.ds(pl.multiple_of(plane * DH, PAIR), DH)]
        out_ref[:, FH:] = heads.astype(BF16)

    return pl.pallas_call(
        kernel,
        grid=(1,),
        in_specs=[smem(), whole(blocks.shape)],
        out_specs=whole((rows, FH + DH)),
        out_shape=jax.ShapeDtypeStruct((rows, FH + DH), BF16),
        scratch_shapes=[pltpu.VMEM((rows, D + FF), F32)],
        compiler_params=params(16),
        cost_estimate=cost(rows * (D + FF), 6 * rows * D),
        name="pack_out",
    )(plan.pos, blocks)


def unpack_out(plan, own, swap):
    rows = own.shape[0]
    width = (D + FF) // plan.n

    def kernel(pos_ref, own_ref, swap_ref, out_ref, full_ref):
        first = pos_ref[3] == 0
        a, b = own_ref[...].astype(F32), swap_ref[...].astype(F32)
        for plane, part in enumerate((jnp.where(first, a, b), jnp.where(first, b, a))):
            full_ref[:, D + plane * FH : D + (plane + 1) * FH] = part[:, :FH]
            full_ref[:, plane * DH : (plane + 1) * DH] = part[:, FH:]
        for i in range(plan.n):
            out_ref[i] = full_ref[:, i * width : (i + 1) * width].astype(BF16)

    return pl.pallas_call(
        kernel,
        grid=(1,),
        in_specs=[smem(), whole(own.shape), whole(own.shape)],
        out_specs=whole((plan.n, rows, width)),
        out_shape=jax.ShapeDtypeStruct((plan.n, rows, width), BF16),
        scratch_shapes=[pltpu.VMEM((rows, D + FF), F32)],
        compiler_params=params(16),
        cost_estimate=cost(rows * (D + FF), 6 * rows * D),
        name="unpack_out",
    )(plan.pos, own, swap)


def stack(pieces):
    rows, width = pieces[0].shape

    def kernel(*refs):
        for i, ref in enumerate(refs[:-1]):
            refs[-1][i * rows : (i + 1) * rows, :] = ref[...]

    shape = (len(pieces) * rows, width)
    return pl.pallas_call(
        kernel,
        grid=(1,),
        in_specs=[whole((rows, width))] * len(pieces),
        out_specs=whole(shape),
        out_shape=jax.ShapeDtypeStruct(shape, BF16),
        compiler_params=params(8),
        cost_estimate=cost(0, 4 * shape[0] * width),
        name="stack",
    )(*pieces)


def fold(a):
    total = a[:, :PAIR]
    for i in range(1, a.shape[1] // PAIR):
        total = total + a[:, i * PAIR : (i + 1) * PAIR]
    return total


def partial_sums(plan, mlp, qkv, out, in_weight, vec_t):
    rows = in_weight.shape[0]

    def kernel(pos_ref, mlp_ref, qkv_ref, out_ref, w_ref, vec_ref, block_ref):
        plane = pos_ref[3]
        gain = vec_ref[:, :1]
        square = jnp.zeros((rows, PAIR), F32)
        dot = jnp.zeros((rows, PAIR), F32)

        def add(square, dot, hat, source, width):
            at = pl.ds(pl.multiple_of(source, PAIR), width)
            low = w_ref[:, at].astype(BF16).astype(F32)
            grad = hat * gain
            return square + fold(grad * grad), dot + fold(low * hat)

        hat = mlp_ref[:, :FH].astype(F32)
        square, dot = add(square, dot, hat, 3 * D + plane * FH, FH)
        for pair in range(PAIRS):
            for which in range(3):
                at = pair * QKV + which * PAIR
                hat = qkv_ref[:, at : at + PAIR].astype(F32)
                source = which * D + plane * DH + pair * PAIR
                square, dot = add(square, dot, hat, source, PAIR)
        value = out_ref[...].astype(F32)
        square = square + fold(value * value)
        lane = lax.broadcasted_iota(jnp.int32, (rows, VEC), 1)
        total = jnp.sum(dot, axis=1, keepdims=True)
        block_ref[:rows, :] = jnp.where(lane == 0, total, qkv_ref[:, QW:].astype(F32))
        square = jnp.sum(square, axis=0, keepdims=True) * 0.125
        block_ref[rows:, :] = jnp.broadcast_to(square, (8, PAIR))

    shape = (rows + 8, VEC)
    arrays = (mlp, qkv, out, in_weight, vec_t)
    return pl.pallas_call(
        kernel,
        grid=(1,),
        in_specs=[smem()] + [whole(a.shape) for a in arrays],
        out_specs=whole(shape),
        out_shape=jax.ShapeDtypeStruct(shape, F32),
        compiler_params=params(16),
        cost_estimate=cost(8 * rows * 6 * D, 14 * rows * 6 * D),
        name="partial_sums",
    )(plan.pos, *arrays)


def join_sums(own, swap):
    rows = own.shape[0] - 8

    def kernel(own_ref, swap_ref, vec_ref, total_ref):
        vec = own_ref[:rows, :] + swap_ref[:rows, :]
        vec_ref[...] = vec
        square = jnp.sum(vec * vec, axis=0, keepdims=True) * 0.125
        total_ref[...] = own_ref[rows:, :] + swap_ref[rows:, :] + jnp.broadcast_to(square, (8, VEC))

    return pl.pallas_call(
        kernel,
        grid=(1,),
        in_specs=[whole(own.shape)] * 2,
        out_specs=[whole((rows, VEC)), whole((8, VEC))],
        out_shape=[
            jax.ShapeDtypeStruct((rows, VEC), F32),
            jax.ShapeDtypeStruct((8, VEC), F32),
        ],
        compiler_params=params(16),
        cost_estimate=cost(4 * own.size, 12 * own.size),
        name="join_sums",
    )(own, swap)


def finish_out(blocks):
    n, rows, width = blocks.shape

    def kernel(in_ref, out_ref):
        out_ref[...] = in_ref[...].reshape(n * rows, width).astype(F32).T

    return pl.pallas_call(
        kernel,
        grid=(1,),
        in_specs=[whole(blocks.shape)],
        out_specs=whole((width, D)),
        out_shape=jax.ShapeDtypeStruct((width, D), F32),
        compiler_params=params(16),
        cost_estimate=cost(0, 6 * width * D),
        name="finish_out",
    )(blocks)


def finish_mlp(plan, own, swap, like, vec_t):
    rows = like.shape[0]

    def kernel(pos_ref, own_ref, swap_ref, vec_ref, grad_ref):
        mine = pl.program_id(0) // 2 == pos_ref[3]
        hat = jnp.where(mine, own_ref[...].astype(F32), swap_ref[...].astype(F32))
        grad_ref[...] = hat * vec_ref[:, :1]

    part = pl.BlockSpec((rows, D), lambda j: (0, j % 2))
    return pl.pallas_call(
        kernel,
        grid=(FF // D,),
        in_specs=[smem(), part, part, whole((rows, VEC))],
        out_specs=pl.BlockSpec((rows, D), lambda j: (0, 3 + j)),
        out_shape=jax.ShapeDtypeStruct(like.shape, F32),
        compiler_params=params(16),
        cost_estimate=cost(2 * rows * FF, 8 * rows * FF),
        name="finish_mlp",
    )(plan.pos, own, swap, vec_t)


def finish_qkv(plan, own, swap, vec_t, grad):
    rows = grad.shape[0]

    def kernel(pos_ref, own_ref, swap_ref, vec_ref, _, grad_ref):
        step = pl.program_id(0)
        first = pos_ref[3] == 0
        parts = []
        for pair in range(PAIRS):
            at = pl.ds(pl.multiple_of(pair * QKV + step * PAIR, PAIR), PAIR)
            parts.append([ref[:, at].astype(F32) for ref in (own_ref, swap_ref)])
        low = [jnp.where(first, a, b) for a, b in parts]
        high = [jnp.where(first, b, a) for a, b in parts]
        grad_ref[...] = jnp.concatenate(low + high, axis=1) * vec_ref[:, :1]

    return pl.pallas_call(
        kernel,
        grid=(3,),
        in_specs=[
            smem(),
            whole(own.shape),
            whole(own.shape),
            whole((rows, VEC)),
            pl.BlockSpec(memory_space=pl.ANY),
        ],
        out_specs=pl.BlockSpec((rows, D), lambda j: (0, j)),
        out_shape=jax.ShapeDtypeStruct(grad.shape, F32),
        input_output_aliases={4: 0},
        compiler_params=params(16),
        cost_estimate=cost(6 * rows * D, 24 * rows * D),
        name="finish_qkv",
    )(plan.pos, own, swap, vec_t, grad)


def prepare(plan, tokens, other_tokens, cotangent, other_cotangent, rows):
    tok = tokens.shape[0]
    kind = row_type(rows)

    def kernel(pos_ref, to_ref, tp_ref, co_ref, cp_ref, xo_ref, xp_ref, turned_ref, sum_ref, t_ref):
        for half, (from_ref, cot_ref, x_ref) in enumerate(
            ((to_ref, co_ref, xo_ref), (tp_ref, cp_ref, xp_ref))
        ):
            values = from_ref[...].astype(F32)
            centre = values - jnp.mean(values, axis=-1, keepdims=True)
            r = lax.rsqrt(jnp.mean(centre * centre, axis=-1, keepdims=True) + norm_eps)
            normal = centre * r
            x_ref[...] = normal.astype(BF16)
            cot = cot_ref[...].astype(F32)
            if half == 0:
                total = jnp.sum(cot, axis=0, keepdims=True)
                sum_ref[...] = jnp.broadcast_to(total, (8, D))
            for which, value in enumerate((normal, cot)):
                t_ref[...] = value.T.astype(kind)

                def put(at, a):
                    columns = slice(half * tok, (half + 1) * tok)
                    turned_ref[which, at : at + rows, columns] = a.astype(BF16)

                turn(plan, pos_ref, t_ref, rows, put)

    low = jax.ShapeDtypeStruct((tok, D), BF16)
    return pl.pallas_call(
        kernel,
        grid=(1,),
        in_specs=[smem()] + [whole((tok, D))] * 4,
        out_specs=[whole((tok, D))] * 2 + [whole((2, D, 2 * tok)), whole((8, D))],
        out_shape=[
            low,
            low,
            jax.ShapeDtypeStruct((2, D, 2 * tok), BF16),
            jax.ShapeDtypeStruct((8, D), F32),
        ],
        scratch_shapes=[pltpu.VMEM((D, tok), kind)],
        compiler_params=params(),
        cost_estimate=cost(40 * tok * D, 20 * tok * D),
        name="prepare",
    )(plan.pos, tokens, other_tokens, cotangent, other_cotangent)


def mlp_forward(plan, x_own, x_other, turned, pieces):
    tok = x_own.shape[0]
    rows = pieces[0].shape[0] // plan.zs
    tile = 512
    n = len(pieces)

    half_d = D // 2

    def kernel(pos_ref, xo_ref, xp_ref, ct_ref, *rest):
        refs, (mix_ref, slope_ref, g_own_ref, g_other_ref, w_ref) = rest[:n], rest[n:]
        place(plan, pos_ref, refs, rows, w_ref)
        w = w_ref[...].astype(BF16)
        for half, x_ref in enumerate((xo_ref, xp_ref)):
            v = mm(x_ref[...], w)
            v2 = v * v
            t = jnp.tanh(v * (GELU_C + (GELU_C * 0.044715) * v2))
            h = 0.5 + 0.5 * t
            g = v * h
            slope = h + 2.0 * g * (1.0 - h) * (GELU_C + (3.0 * GELU_C * 0.044715) * v2)
            mix_ref[half] = g.astype(BF16)
            slope_ref[half] = slope.astype(BF16)
        g = mm(ct_ref[0], mix_ref[...].reshape(2 * tok, tile)).astype(BF16)
        g_own_ref[...] = g[:half_d]
        g_other_ref[...] = g[half_d:]

    block = pl.BlockSpec((2, tok, tile), lambda j: (0, 0, j))
    grad = pl.BlockSpec((half_d, tile), lambda j: (0, j))
    return pl.pallas_call(
        kernel,
        grid=(FH // tile,),
        in_specs=[smem()]
        + [whole((tok, D))] * 2
        + [pl.BlockSpec((1, D, 2 * tok), lambda j: (1, 0, 0))]
        + [pl.BlockSpec((plan.zs * rows, tile), lambda j: (0, j))] * n,
        out_specs=[block, block, grad, grad],
        out_shape=[jax.ShapeDtypeStruct((2, tok, FH), BF16)] * 2
        + [jax.ShapeDtypeStruct((half_d, FH + DH), BF16)] * 2,
        scratch_shapes=[pltpu.VMEM((D, tile), row_type(rows))],
        compiler_params=params(),
        cost_estimate=cost(8 * tok * D * FH, 12 * tok * FH, 2 * tok * FH),
        name="mlp_forward",
    )(plan.pos, x_own, x_other, turned, *pieces)


def head_means(a, block_ref):
    high = a.astype(BF16)
    low = (a - high.astype(F32)).astype(BF16)
    return mm(high, block_ref[...]) + mm(low, block_ref[...])


def attention_forward(plan, x_own, x_other, pieces, ids, block, turned, g_own, g_other):
    tok = x_own.shape[0]
    rows = pieces[0].shape[0] // plan.zs
    n = len(pieces)
    half_d = D // 2

    def kernel(pos_ref, xo_ref, xp_ref, ido_ref, idp_ref, block_ref, ct_ref, _, __, *rest):
        refs, vec_refs = rest[:n], rest[n : 2 * n]
        (
            qk_ref, v_ref, n_ref, r_ref, att_ref, p_ref, gain_ref, g_own_ref, g_other_ref,
            w_ref, vs_ref, all_ref,
        ) = rest[2 * n :]
        step = pl.program_id(0)

        @pl.when(step == 0)
        def _():
            place(plan, pos_ref, vec_refs, rows, vs_ref)
            gain_ref[...] = vs_ref[...].astype(F32).T[:8]

        place(plan, pos_ref, refs, rows, w_ref)
        w = w_ref[...].astype(BF16)
        column = pl.ds(pl.multiple_of(pos_ref[3] * DH + step * PAIR, PAIR), PAIR)
        gain = jnp.concatenate(
            [gain_ref[1:2, column] * (HD ** (-0.5)), gain_ref[2:3, column]], axis=1
        )
        first = lax.broadcasted_iota(jnp.int32, (tok, PAIR), 1) < HD
        for half, x_ref in enumerate((xo_ref, xp_ref)):
            raw = mm(x_ref[...], w)
            qk = raw[:, : 2 * PAIR]
            centre = qk - head_means(qk, block_ref)
            r = lax.rsqrt(mm((centre * centre).astype(BF16), block_ref[...]) + norm_eps)
            normal = centre * r
            n_ref[half] = normal.astype(BF16)
            r_ref[half] = r.astype(BF16)
            low = (normal * gain).astype(BF16)
            qk_ref[half] = low
            q, k = low[:, :PAIR], low[:, PAIR:]
            v = raw[:, 2 * PAIR :].astype(BF16)
            v_ref[half] = v
            number = (ido_ref, idp_ref)[half][...].astype(F32)
            same = jnp.broadcast_to(number, (8, tok)).T[:, :1] == number
            att = []
            zero = jnp.zeros_like(q)
            for head in range(2):
                qh = jnp.where(first, q, zero) if head == 0 else jnp.where(first, zero, q)
                e = jnp.where(same, jnp.exp(mm(qh, k, NT)), 0.0)
                p = (e * (1.0 / jnp.sum(e, axis=1, keepdims=True))).astype(BF16)
                p_ref[half, head] = p
                att.append(mm(p, v))
            att_low = jnp.where(first, att[0], att[1]).astype(BF16)
            att_ref[half] = att_low
            at = pl.ds(pl.multiple_of(step * PAIR, PAIR), PAIR)
            all_ref[half * tok : (half + 1) * tok, at] = att_low

        @pl.when(step == PAIRS - 1)
        def _():
            g = mm(ct_ref[0], all_ref[...]).astype(BF16)
            g_own_ref[...] = g[:half_d]
            g_other_ref[...] = g[half_d:]

    pair = pl.BlockSpec((2, tok, PAIR), lambda j: (0, 0, j))
    pair2 = pl.BlockSpec((2, tok, 2 * PAIR), lambda j: (0, 0, j))
    small = jax.ShapeDtypeStruct((2, tok, DH), BF16)
    small2 = jax.ShapeDtypeStruct((2, tok, 2 * DH), BF16)
    heads = pl.BlockSpec((half_d, DH), lambda j: (0, FH // DH))
    return pl.pallas_call(
        kernel,
        grid=(PAIRS,),
        in_specs=[smem()]
        + [whole((tok, D))] * 2
        + [whole((1, tok))] * 2
        + [whole((2 * PAIR, 2 * PAIR))]
        + [pl.BlockSpec((1, D, 2 * tok), lambda j: (1, 0, 0))]
        + [pl.BlockSpec(memory_space=pl.ANY)] * 2
        + [pl.BlockSpec((plan.zs * rows, QKV), lambda j: (0, j))] * n
        + [pl.BlockSpec((plan.zs * rows, VEC), lambda j: (0, QW // VEC))] * n,
        out_specs=[pair2, pair, pair2, pair2, pair]
        + [pl.BlockSpec((2, 2, tok, tok), lambda j: (0, j, 0, 0)), whole((8, D))]
        + [heads, heads],
        out_shape=[small2, small, small2, small2, small]
        + [
            jax.ShapeDtypeStruct((2, 2 * PAIRS, tok, tok), BF16),
            jax.ShapeDtypeStruct((8, D), F32),
            jax.ShapeDtypeStruct(g_own.shape, BF16),
            jax.ShapeDtypeStruct(g_own.shape, BF16),
        ],
        input_output_aliases={7: 7, 8: 8},
        scratch_shapes=[
            pltpu.VMEM((D, QKV), row_type(rows)),
            pltpu.VMEM((D, VEC), row_type(rows)),
            pltpu.VMEM((2 * tok, DH), BF16),
        ],
        compiler_params=params(),
        cost_estimate=cost(4 * tok * D * QW, 20 * MIB, 12 * tok * tok),
        name="attention_forward",
    )(
        plan.pos, x_own, x_other, *ids, block, turned, g_own, g_other, *pieces, *pieces,
    )


TILE = 256


def token_tiles(tok):
    per = tok // TILE

    def pair(j):
        return (j // per, j % per, 0)

    def own(j):
        return jnp.minimum(j, per - 1)

    def other(j):
        return jnp.maximum(j - per, 0)

    return per, pair, own, other


def output_step(plan, att, mixed, slope, cot_own, cot_other, pieces):
    tok = cot_own.shape[0]
    rows = pieces[0].shape[0] // plan.zs
    n = len(pieces)
    per, pair, own, other = token_tiles(tok)

    def kernel(pos_ref, att_ref, mix_ref, slope_ref, co_ref, cp_ref, *rest):
        refs = rest[:n]
        out_own_ref, out_other_ref, d_att_ref, d_in_ref, w_ref = rest[n:]
        step = pl.program_id(0)

        @pl.when(step == 0)
        def _():
            place(plan, pos_ref, refs, rows, w_ref)

        w = w_ref[...].astype(BF16)
        cot = jnp.where(step < per, co_ref[...], cp_ref[...])
        for at in range(0, FH, DH):
            d = mm(cot, w[:, at : at + DH])
            slopes = slope_ref[0, :, at : at + DH].astype(F32)
            d_in_ref[0, :, at : at + DH] = (d * slopes).astype(BF16)
        d_att_ref[0] = mm(cot, w[:, FH:]).astype(BF16)
        out = mm(mix_ref[0], w[:, :FH], NT) + mm(att_ref[0], w[:, FH:], NT)

        @pl.when(step < per)
        def _():
            out_own_ref[...] = out

        @pl.when(step >= per)
        def _():
            out_other_ref[...] = out.astype(BF16)

    return pl.pallas_call(
        kernel,
        grid=(2 * per,),
        in_specs=[
            smem(),
            pl.BlockSpec((1, TILE, DH), pair),
            pl.BlockSpec((1, TILE, FH), pair),
            pl.BlockSpec((1, TILE, FH), pair),
            pl.BlockSpec((TILE, D), lambda j: (own(j), 0)),
            pl.BlockSpec((TILE, D), lambda j: (other(j), 0)),
        ]
        + [whole(pieces[0].shape)] * n,
        out_specs=[
            pl.BlockSpec((TILE, D), lambda j: (own(j), 0)),
            pl.BlockSpec((TILE, D), lambda j: (other(j), 0)),
            pl.BlockSpec((1, TILE, DH), pair),
            pl.BlockSpec((1, TILE, FH), pair),
        ],
        out_shape=[
            jax.ShapeDtypeStruct((tok, D), F32),
            jax.ShapeDtypeStruct((tok, D), BF16),
            jax.ShapeDtypeStruct((2, tok, DH), BF16),
            jax.ShapeDtypeStruct((2, tok, FH), BF16),
        ],
        scratch_shapes=[pltpu.VMEM((D, FH + DH), row_type(rows))],
        compiler_params=params(40),
        cost_estimate=cost(8 * tok * (FH + DH) * D, 20 * MIB),
        name="output_step",
    )(plan.pos, att, mixed, slope, cot_own, cot_other, *pieces)


def mlp_gradient(turned, d_inner):
    tok = d_inner.shape[1]
    half_d = D // 2
    tile = 512

    def kernel(xt_ref, d_ref, g_own_ref, g_other_ref):
        g = mm(xt_ref[0], d_ref[...].reshape(2 * tok, tile)).astype(BF16)
        g_own_ref[...] = g[:half_d]
        g_other_ref[...] = g[half_d:]

    grad = pl.BlockSpec((half_d, tile), lambda j: (0, j))
    return pl.pallas_call(
        kernel,
        grid=(FH // tile,),
        in_specs=[
            pl.BlockSpec((1, D, 2 * tok), lambda j: (0, 0, 0)),
            pl.BlockSpec((2, tok, tile), lambda j: (0, 0, j)),
        ],
        out_specs=[grad, grad],
        out_shape=[jax.ShapeDtypeStruct((half_d, FH), BF16)] * 2,
        compiler_params=params(40),
        cost_estimate=cost(4 * tok * D * FH, 8 * MIB),
        name="mlp_gradient",
    )(turned, d_inner)


def scaled_gradient(plan, d_inner, d_qkv, mlp_pieces, qkv_pieces):
    tok = d_inner.shape[1]
    rows = mlp_pieces[0].shape[0] // plan.zs
    n = len(mlp_pieces)
    per, pair, own, other = token_tiles(tok)

    def kernel(pos_ref, dm_ref, dq_ref, *rest):
        refs_m, refs_q = rest[:n], rest[n : 2 * n]
        e_own_ref, e_other_ref, wm_ref, wq_ref = rest[2 * n :]
        step = pl.program_id(0)

        @pl.when(step == 0)
        def _():
            place(plan, pos_ref, refs_m, rows, wm_ref)
            place(plan, pos_ref, refs_q, rows, wq_ref)

        e = mm(dm_ref[0], wm_ref[...].astype(BF16), NT)
        e = e + mm(dq_ref[0], wq_ref[...].astype(BF16)[:, :QW], NT)

        @pl.when(step < per)
        def _():
            e_own_ref[...] = e

        @pl.when(step >= per)
        def _():
            e_other_ref[...] = e.astype(BF16)

    return pl.pallas_call(
        kernel,
        grid=(2 * per,),
        in_specs=[
            smem(),
            pl.BlockSpec((1, TILE, FH), pair),
            pl.BlockSpec((1, TILE, QW), pair),
        ]
        + [whole(mlp_pieces[0].shape)] * n
        + [whole(qkv_pieces[0].shape)] * n,
        out_specs=[
            pl.BlockSpec((TILE, D), lambda j: (own(j), 0)),
            pl.BlockSpec((TILE, D), lambda j: (other(j), 0)),
        ],
        out_shape=[
            jax.ShapeDtypeStruct((tok, D), F32),
            jax.ShapeDtypeStruct((tok, D), BF16),
        ],
        scratch_shapes=[
            pltpu.VMEM((D, FH), row_type(rows)),
            pltpu.VMEM((D, QW + VEC), row_type(rows)),
        ],
        compiler_params=params(48),
        cost_estimate=cost(4 * tok * (FH + QW) * D, 16 * MIB),
        name="scaled_gradient",
    )(plan.pos, d_inner, d_qkv, *mlp_pieces, *qkv_pieces)


def attention_backward(plan, turned, saved, d_att, block, gains, cot_sum, rows):
    qk, v, normals, factors, probs = saved
    tok = d_att.shape[1]
    half_d = D // 2
    kind = row_type(rows)

    def kernel(pos_ref, xt_ref, qk_ref, v_ref, n_ref, r_ref, p_ref, da_ref, block_ref, gain_ref,
               cot_ref, g_own_ref, g_other_ref, d_ref, vec_ref, turn_ref):
        step = pl.program_id(0)

        @pl.when(step == 0)
        def _():
            vec_ref[...] = jnp.zeros_like(vec_ref)
            vec_ref[3:4, :] = cot_ref[:1]

        column = pl.ds(pl.multiple_of(pos_ref[3] * DH + step * PAIR, PAIR), PAIR)
        gain = jnp.concatenate(
            [gain_ref[1:2, column] * (HD ** (-0.5)), gain_ref[2:3, column]], axis=1
        )
        first = lax.broadcasted_iota(jnp.int32, (tok, PAIR), 1) < HD

        def heads(a):
            zero = jnp.zeros_like(a)
            return jnp.concatenate([jnp.where(first, a, zero), jnp.where(first, zero, a)], axis=0)

        for half in range(2):
            qb, kb, vb = qk_ref[half, :, :PAIR], qk_ref[half, :, PAIR:], v_ref[half]
            da = heads(da_ref[half])
            p_low = p_ref[half].reshape(2 * tok, tok)
            p = p_low.astype(F32)
            t = p * mm(da, vb, NT)
            ds = (t - p * jnp.sum(t, axis=1, keepdims=True)).astype(BF16)
            d_value = mm(da.T, p_low).T
            d_key = mm(heads(qb).T, ds).T
            dq = mm(ds, kb)
            d_query = jnp.where(first, dq[:tok], dq[tok:])
            d = jnp.concatenate([d_query, d_key], axis=1)
            normal = n_ref[half].astype(F32)
            sums = jnp.sum(d * normal, axis=0, keepdims=True)
            vec_ref[1:2, column] += sums[:, :PAIR] * (HD ** (-0.5))
            vec_ref[2:3, column] += sums[:, PAIR:]
            e = d * gain
            along = mm((e * normal).astype(BF16), block_ref[...])
            d_raw = r_ref[half].astype(F32) * (e - head_means(e, block_ref) - normal * along)
            d_ref[half, :, : 2 * PAIR] = d_raw.astype(BF16)
            d_ref[half, :, 2 * PAIR :] = d_value.astype(BF16)
        g = mm(xt_ref[0], d_ref[...].reshape(2 * tok, QKV)).astype(BF16)
        at = pl.ds(pl.multiple_of(step * QKV, QKV), QKV)
        g_own_ref[:, at] = g[:half_d]
        g_other_ref[:, at] = g[half_d:]

        @pl.when(step == PAIRS - 1)
        def _():
            turn_ref[...] = vec_ref[...].T.astype(kind)

            def put(at, a):
                ref = g_own_ref if at < half_d else g_other_ref
                ref[at % half_d : at % half_d + rows, QW:] = a.astype(BF16)

            turn(plan, pos_ref, turn_ref, rows, put)

    pair = pl.BlockSpec((2, tok, PAIR), lambda j: (0, 0, j))
    pair2 = pl.BlockSpec((2, tok, 2 * PAIR), lambda j: (0, 0, j))
    return pl.pallas_call(
        kernel,
        grid=(PAIRS,),
        in_specs=[smem(), pl.BlockSpec((1, D, 2 * tok), lambda j: (0, 0, 0))]
        + [pair2, pair, pair2, pair2]
        + [
            pl.BlockSpec((2, 2, tok, tok), lambda j: (0, j, 0, 0)),
            pair,
            whole((2 * PAIR, 2 * PAIR)),
            whole((8, D)),
            whole((8, D)),
        ],
        out_specs=[whole((half_d, QW + VEC))] * 2
        + [pl.BlockSpec((2, tok, QKV), lambda j: (0, 0, j))],
        out_shape=[jax.ShapeDtypeStruct((half_d, QW + VEC), BF16)] * 2
        + [jax.ShapeDtypeStruct((2, tok, QW), BF16)],
        scratch_shapes=[pltpu.VMEM((VEC, D), F32), pltpu.VMEM((D, VEC), kind)],
        compiler_params=params(48),
        cost_estimate=cost(16 * tok * D * QW, 24 * MIB),
        name="attention_backward",
    )(plan.pos, turned, qk, v, normals, factors, probs, d_att, block, gains, cot_sum)


def token_gradient(tokens, cotangent, e_own, e_recv):
    tok = tokens.shape[0]

    def kernel(t_ref, c_ref, own_ref, recv_ref, out_ref):
        rows = t_ref[...].astype(F32)
        centre = rows - jnp.mean(rows, axis=-1, keepdims=True)
        r = lax.rsqrt(jnp.mean(centre * centre, axis=-1, keepdims=True) + norm_eps)
        normal = centre * r
        e = own_ref[...] + recv_ref[...].astype(F32)
        mean = jnp.mean(e, axis=-1, keepdims=True)
        along = jnp.mean(e * normal, axis=-1, keepdims=True)
        out_ref[...] = c_ref[...].astype(F32) + r * (e - mean - normal * along)

    block = pl.BlockSpec((tok // 4, D), lambda j: (j, 0))
    return pl.pallas_call(
        kernel,
        grid=(4,),
        in_specs=[block] * 4,
        out_specs=block,
        out_shape=jax.ShapeDtypeStruct((tok, D), F32),
        compiler_params=params(16),
        cost_estimate=cost(20 * tok * D, 14 * tok * D),
        name="token_gradient",
    )(tokens, cotangent, e_own, e_recv)


def adamw(master, first, second, grad, factor):
    clipped = grad * factor
    first_new = beta_one * first + (1.0 - beta_one) * clipped
    second_new = beta_two * second + (1.0 - beta_two) * clipped * clipped
    first_hat = first_new * (1.0 / (1.0 - beta_one**ADAM_STEP))
    second_hat = second_new * (1.0 / (1.0 - beta_two**ADAM_STEP))
    update = -learning * (first_hat / (jnp.sqrt(second_hat) + epsilon) + decay_rate * master)
    return (update, first_new, second_new)


def optimize(total, vec_cols, ins, outs, vecs):
    rows, out_rows = ins[0].shape[0], outs[0].shape[0]
    steps = 3

    def kernel(total_ref, cols_ref, *refs):
        in_refs, out_refs, vec_refs, rest = refs[:4], refs[4:8], refs[8:11], refs[11:]
        vec_grad_ref, norm_ref, pad_ref = rest[0], rest[1], rest[-1]
        sums = jnp.sum(jnp.sum(total_ref[...], axis=1, keepdims=True), axis=0, keepdims=True)
        norm = jnp.sqrt(sums)
        factor = jnp.minimum(1.0, math.sqrt(PARAMS) / norm)
        for group, results in ((in_refs, rest[2:5]), (out_refs, rest[5:8])):
            for ref, value in zip(results, adamw(*[ref[...] for ref in group], factor)):
                ref[...] = value

        @pl.when(pl.program_id(0) == 0)
        def _():
            norm_ref[...] = norm
            pad_ref[...] = jnp.zeros_like(pad_ref)
            pad_ref[:rows] = cols_ref[...]
            grad = pad_ref[...].T[:4, :rows]
            vec_grad_ref[...] = grad
            values = adamw(*[ref[...] for ref in vec_refs], grad, factor)
            for ref, value in zip(rest[8:11], values):
                ref[...] = value

    in_block = pl.BlockSpec((rows, 7 * D // steps), lambda j: (0, j))
    out_block = pl.BlockSpec((out_rows // steps, D), lambda j: (j, 0))
    shapes = [jax.ShapeDtypeStruct(a.shape, F32) for a in (ins[0], outs[0], vecs[0])]
    return pl.pallas_call(
        kernel,
        grid=(steps,),
        in_specs=[whole((8, 128)), whole(vec_cols.shape)]
        + [in_block] * 4
        + [out_block] * 4
        + [whole(vecs[0].shape)] * 3,
        out_specs=[whole(vecs[0].shape), whole((1, 1))]
        + [in_block] * 3
        + [out_block] * 3
        + [whole(vecs[0].shape)] * 3,
        out_shape=[shapes[2], jax.ShapeDtypeStruct((1, 1), F32)]
        + [shapes[0]] * 3
        + [shapes[1]] * 3
        + [shapes[2]] * 3,
        scratch_shapes=[pltpu.VMEM((128, 128), F32)],
        compiler_params=params(16),
        cost_estimate=cost(20 * 7 * D * rows, 28 * 13 * D * rows),
        name="optimize",
    )(total, vec_cols, *ins, *outs, *vecs)


def local(
    tokens,
    cotangent,
    image_ids,
    in_weight,
    out_weight,
    vectors,
    in_moment,
    out_moment,
    vec_moment,
    in_second,
    out_second,
    vec_second,
):
    plan = Plan(lax.axis_size("fsdp"), lax.axis_size("dp"))
    rows = in_weight.shape[0]

    low_vec = vectors.astype(BF16).astype(F32)
    vec_t = jnp.pad(low_vec.T, ((0, 0), (0, VEC - 4)))
    mlp_piece, qkv_piece = pack_in(plan, in_weight, vec_t)
    other_tokens = plan.swap_plane(tokens)
    other_cotangent = plan.swap_plane(cotangent)
    blocks = lax.all_to_all(split_out(plan, out_weight, rows), "fsdp", 0, 0)

    def z_all(piece):
        return [plan.from_z(piece, s) for s in range(1, plan.zs)]

    def y_all(column):
        return [plan.from_y(column, t) for t in range(1, plan.ys)]

    def core_all(arrays):
        return [plan.swap_core(a) for a in arrays]

    def held(groups):
        flat = iter(fence(*[a for group in groups for a in group]))
        return [[next(flat) for _ in group] for group in groups]

    mlp_z = z_all(mlp_piece)
    mlp_z, (qkv_piece,) = held([mlp_z, [qkv_piece]])
    mlp_col = stack([mlp_piece] + mlp_z)
    mlp_y = y_all(mlp_col)
    qkv_z = z_all(qkv_piece)
    out_piece = pack_out(plan, blocks)
    x_own, x_other, turned, cot_sum = prepare(
        plan, tokens, other_tokens, cotangent, other_cotangent, rows
    )
    mlp_y, qkv_z, (mlp_col, out_piece, x_own) = held(
        [mlp_y, qkv_z, [mlp_col, out_piece, x_own]]
    )
    mlp_pieces = [mlp_col] + mlp_y + core_all([mlp_col] + mlp_y)
    qkv_col = stack([qkv_piece] + qkv_z)
    qkv_y = y_all(qkv_col)
    out_z = z_all(out_piece)
    mixed, slope, g_own, g_other = mlp_forward(plan, x_own, x_other, turned, mlp_pieces)
    qkv_y, out_z, (qkv_col, mixed, slope, g_own, g_other, ids_now) = held(
        [qkv_y, out_z, [qkv_col, mixed, slope, g_own, g_other, image_ids]]
    )
    other_ids = plan.swap_plane(ids_now)
    qkv_pieces = [qkv_col] + qkv_y + core_all([qkv_col] + qkv_y)
    out_col = stack([out_piece] + out_z)
    out_y = y_all(out_col)
    out_core = core_all([out_col])
    lane = jnp.arange(2 * PAIR) // HD
    block = jnp.where(lane[:, None] == lane[None, :], 1.0 / HD, 0.0).astype(BF16)
    *saved, att, probs, gains, g_own, g_other = attention_forward(
        plan, x_own, x_other, qkv_pieces, (image_ids[None, :], other_ids[None, :]), block,
        turned, g_own, g_other,
    )
    saved = tuple(saved) + (probs,)
    out_y, out_core, (att, g_own, g_other) = held([out_y, out_core, [att, g_own, g_other]])
    s_out = Scatter(plan, g_own, g_other)
    s_out.by_core()
    out_core = out_core + core_all(out_y)
    s_out.recv, *out_core = fence(s_out.recv, *out_core)
    s_out.by_y()
    out_pieces = [out_col] + out_y + out_core
    out_mine, out_theirs, d_att, d_inner = output_step(
        plan, att, mixed, slope, cotangent, other_cotangent, out_pieces
    )
    g_own, g_other = mlp_gradient(turned, d_inner)
    s_mlp = Scatter(plan, g_own, g_other)
    s_mlp.by_core()
    s_out.y_got, (out_theirs, g_own) = held([s_out.y_got, [out_theirs, g_own]])
    s_out.by_z()
    out_recv = plan.swap_plane(out_theirs)
    s_mlp.recv, d_att = fence(s_mlp.recv, d_att)
    s_mlp.by_y()
    g_own, g_other, d_qkv = attention_backward(
        plan, turned, saved, d_att, block, gains, cot_sum, rows
    )
    s_out.z_got, s_mlp.y_got, (g_own, g_other, d_qkv, out_recv) = held(
        [s_out.z_got, s_mlp.y_got, [g_own, g_other, d_qkv, out_recv]]
    )
    s_qkv = Scatter(plan, g_own, g_other)
    s_qkv.by_core()
    out_sum = s_out.total()
    out_swap = plan.swap_plane(out_sum)
    parts, s_mlp.y_got, (out_sum, d_qkv) = held([s_qkv.y_parts(), s_mlp.y_got, [out_sum, d_qkv]])
    s_qkv.by_y(parts)
    s_mlp.by_z()
    e_own, e_other = scaled_gradient(plan, d_inner, d_qkv, mlp_pieces, qkv_pieces)
    out_swap, e_other, e_own = fence(out_swap, e_other, e_own)
    e_recv = plan.swap_plane(e_other)
    blocks = unpack_out(plan, plan.over_pairs(out_sum), plan.over_pairs(out_swap))
    s_qkv.y_got, s_mlp.z_got, (blocks,) = held([s_qkv.y_got, s_mlp.z_got, [blocks]])
    s_qkv.by_z()
    blocks = lax.all_to_all(blocks, "fsdp", 0, 0)
    result = (
        tokens.astype(F32) + out_mine + out_recv.astype(F32) + gains[3][None, :]
    ).astype(BF16)
    mlp_sum = s_mlp.total()
    mlp_swap = plan.swap_plane(mlp_sum)
    s_qkv.z_got, (result,) = held([s_qkv.z_got, [result]])
    qkv_sum = plan.over_pairs(s_qkv.total())
    mlp_sum, out_sum = plan.over_pairs(mlp_sum), plan.over_pairs(out_sum)
    own = partial_sums(plan, mlp_sum, qkv_sum, out_sum, in_weight, vec_t)
    swap = plan.swap_plane(own)
    swap, qkv_sum, mlp_swap = fence(swap, qkv_sum, mlp_swap)
    vec_cols, square = join_sums(own, swap)
    qkv_swap = plan.swap_plane(qkv_sum)
    in_grad = finish_mlp(plan, mlp_sum, plan.over_pairs(mlp_swap), in_weight, vec_t)
    in_grad = finish_qkv(plan, qkv_sum, qkv_swap, vec_t, in_grad)
    out_grad = finish_out(blocks)
    input_grad = token_gradient(tokens, cotangent, e_own, e_recv)
    total, out_grad, in_grad = plan.total(square, out_grad, in_grad)
    vec_grad, norm, *updates = optimize(
        total,
        vec_cols,
        (in_weight, in_moment, in_second, in_grad),
        (out_weight, out_moment, out_second, out_grad),
        (vectors, vec_moment, vec_second),
    )
    in_update, in_mean, in_square = updates[:3]
    out_update, out_mean, out_square = updates[3:6]
    vec_update, vec_mean, vec_square = updates[6:]
    return (
        result,
        input_grad,
        in_grad,
        out_grad,
        vec_grad,
        norm.reshape(()),
        in_update,
        out_update,
        vec_update,
        in_mean,
        out_mean,
        vec_mean,
        in_square,
        out_square,
        vec_square,
    )


def solution(mesh):
    in_specs = (
        P(("dp", "fsdp"), None),
        P(("dp", "fsdp"), None),
        P(("dp", "fsdp")),
        P("fsdp", None),
        P("fsdp", None),
        P(None, "fsdp"),
        P("fsdp", None),
        P("fsdp", None),
        P(None, "fsdp"),
        P("fsdp", None),
        P("fsdp", None),
        P(None, "fsdp"),
    )
    out_specs = (
        P(("dp", "fsdp"), None),
        P(("dp", "fsdp"), None),
        P("fsdp", None),
        P("fsdp", None),
        P(None, "fsdp"),
        P(),
        P("fsdp", None),
        P("fsdp", None),
        P(None, "fsdp"),
        P("fsdp", None),
        P("fsdp", None),
        P(None, "fsdp"),
        P("fsdp", None),
        P("fsdp", None),
        P(None, "fsdp"),
    )
    return jax.shard_map(local, mesh=mesh, in_specs=in_specs, out_specs=out_specs, check_vma=False)
```

```python
import math

import jax
import jax.numpy as jnp
from jax import lax
from jax.experimental import pallas as pl
from jax.experimental.pallas import tpu as pltpu
from jax.sharding import PartitionSpec as P

D = 768
H = 12
HD = 64
FF = 3072
ADAM_STEP = 10
PARAMS = 7080960

beta_one = 0.9
beta_two = 0.95
learning = 0.03
decay_rate = 0.1
epsilon = 1e-08
norm_eps = 1e-06

F32 = jnp.float32
BF16 = jnp.bfloat16
DH = D // 2
FH = FF // 2
PAIR = 128
PAIRS = DH // PAIR
QKV = 3 * PAIR
QW = PAIRS * QKV
VEC = 128
GELU_C = math.sqrt(2.0 / math.pi)
MIB = 1 << 20

NT = (((1,), (1,)), ((), ()))
TN = (((0,), (0,)), ((), ()))


def mm(a, b, dims=(((1,), (0,)), ((), ()))):
    return lax.dot_general(a, b, dims, preferred_element_type=F32)


def fence(*arrays):
    return lax.optimization_barrier(arrays)


class Plan:
    def __init__(self, n_fsdp, n_dp):
        chips = n_fsdp // 2
        self.n, self.n_dp, self.chips = n_fsdp, n_dp, chips
        self.zs = 4 if chips % 4 == 0 else chips
        self.ys = chips // self.zs
        index = lax.axis_index("fsdp")
        self.core = index % 2
        self.y = (index // 2) % self.ys
        self.z = index // (2 * self.ys)
        self.plane = lax.axis_index("dp") % 2
        self.pos = jnp.stack([self.z, self.y, self.core, self.plane]).astype(jnp.int32)
        self.order = [
            (c, t, s) for c in range(2) for t in range(self.ys) for s in range(self.zs)
        ]

    def index(self, z, y, core):
        return ((z % self.zs) * self.ys + y % self.ys) * 2 + core

    def all(self):
        return [
            (z, y, c) for z in range(self.zs) for y in range(self.ys) for c in range(2)
        ]

    def from_z(self, a, s):
        pairs = [(self.index(z + s, y, c), self.index(z, y, c)) for z, y, c in self.all()]
        return lax.ppermute(a, "fsdp", pairs)

    def from_y(self, a, t):
        pairs = [(self.index(z, y + t, c), self.index(z, y, c)) for z, y, c in self.all()]
        return lax.ppermute(a, "fsdp", pairs)

    def swap_core(self, a):
        pairs = [(self.index(z, y, c), self.index(z, y, 1 - c)) for z, y, c in self.all()]
        return lax.ppermute(a, "fsdp", pairs)

    def swap_plane(self, a):
        return lax.ppermute(a, "dp", [(i, i ^ 1) for i in range(self.n_dp)])

    def over_pairs(self, a):
        if self.n_dp == 2:
            return a
        groups = [list(range(p, self.n_dp, 2)) for p in range(2)]
        return lax.psum(a.astype(F32), "dp", axis_index_groups=groups)

    def total(self, a, *beside):
        a = a + self.swap_core(a)
        beside = list(beside)
        count = 0
        for step, size in ((2, self.ys), (2 * self.ys, self.zs)):
            m = 1
            while m < size:
                pairs = [(i, i ^ (m * step)) for i in range(self.n)]
                got = lax.ppermute(a, "fsdp", pairs)
                if count < len(beside):
                    if callable(beside[count]):
                        beside[count] = beside[count](beside[count - 1])
                    got, beside[count] = fence(got, beside[count])
                a = a + got
                m, count = 2 * m, count + 1
        for i in range(count, len(beside)):
            beside[i] = beside[i](beside[i - 1])
        return [a] + beside

    def row(self, pos_ref, piece, rows):
        c, t, s = piece
        z = lax.rem(pos_ref[0] + s, self.zs)
        y = lax.rem(pos_ref[1] + t, self.ys)
        core = lax.rem(pos_ref[2] + c, 2)
        at = ((z * self.ys + y) * 2 + core) * rows
        return pl.multiple_of(at, math.gcd(rows, 16))


class Scatter:
    def __init__(self, plan, own, other):
        self.plan, self.own, self.other = plan, own, other
        self.rows = own.shape[0] // plan.chips

    def by_core(self):
        self.recv = self.plan.swap_core(self.other)

    def sums(self, begin, end, arrays):
        total = self.own[begin:end].astype(F32) + self.recv[begin:end].astype(F32)
        for a in arrays:
            total = total + a.astype(F32)
        return total

    def y_parts(self):
        size = self.plan.zs * self.rows
        return [
            self.sums(t * size, (t + 1) * size, ()).astype(BF16)
            for t in range(1, self.plan.ys)
        ]

    def by_y(self, parts=None):
        parts = self.y_parts() if parts is None else parts
        self.y_got = [self.plan.from_y(a, -t - 1) for t, a in enumerate(parts)]

    def part(self, s):
        at = slice(s * self.rows, (s + 1) * self.rows)
        return self.sums(at.start, at.stop, [a[at] for a in self.y_got])

    def by_z(self):
        parts = [self.part(s).astype(BF16) for s in range(1, self.plan.zs)]
        self.z_got = [self.plan.from_z(a, -s - 1) for s, a in enumerate(parts)]

    def total(self):
        total = self.part(0)
        for a in self.z_got:
            total = total + a.astype(F32)
        return total.astype(BF16)


def smem():
    return pl.BlockSpec(memory_space=pltpu.SMEM)


def whole(shape):
    return pl.BlockSpec(shape, lambda *_: (0,) * len(shape))


def params(mib=58):
    return pltpu.CompilerParams(
        dimension_semantics=("arbitrary",), vmem_limit_bytes=mib * MIB
    )


def cost(flops, nbytes, exps=0):
    return pl.CostEstimate(flops=int(flops), bytes_accessed=int(nbytes), transcendentals=int(exps))


def row_type(rows):
    return BF16 if rows % 16 == 0 else F32


def place(plan, pos_ref, refs, rows, out_ref):
    for i, piece in enumerate(plan.order):
        ref, at = refs[i // plan.zs], i % plan.zs * rows
        part = ref[at : at + rows, :].astype(out_ref.dtype)
        out_ref[pl.ds(plan.row(pos_ref, piece, rows), rows), :] = part


def turn(plan, pos_ref, from_ref, rows, put):
    for i, piece in enumerate(plan.order):
        put(i * rows, from_ref[pl.ds(plan.row(pos_ref, piece, rows), rows), :])


def pack_in(plan, in_weight, vec_t):
    rows = in_weight.shape[0]

    def kernel(pos_ref, w_ref, vec_ref, mlp_ref, qkv_ref):
        plane = pos_ref[3]
        gain = vec_ref[:, :1]

        def take(source, width):
            at = pl.ds(pl.multiple_of(source, PAIR), width)
            low = w_ref[:, at].astype(BF16).astype(F32)
            return (low * gain).astype(BF16)

        mlp_ref[...] = take(3 * D + plane * FH, FH)
        for pair in range(PAIRS):
            for which in range(3):
                to = pair * QKV + which * PAIR
                source = which * D + plane * DH + pair * PAIR
                qkv_ref[:, to : to + PAIR] = take(source, PAIR)
        qkv_ref[:, QW:] = vec_ref[...].astype(BF16)

    return pl.pallas_call(
        kernel,
        grid=(1,),
        in_specs=[smem(), whole(in_weight.shape), whole((rows, VEC))],
        out_specs=[whole((rows, FH)), whole((rows, QW + VEC))],
        out_shape=[
            jax.ShapeDtypeStruct((rows, FH), BF16),
            jax.ShapeDtypeStruct((rows, QW + VEC), BF16),
        ],
        compiler_params=params(16),
        cost_estimate=cost(2 * rows * 3 * D, 6 * rows * 7 * D),
        name="pack_in",
    )(plan.pos, in_weight, vec_t)


def split_out(plan, out_weight, rows):
    width = out_weight.shape[0]

    def kernel(w_ref, out_ref):
        full = w_ref[...].T.astype(BF16)
        for i in range(plan.n):
            out_ref[i] = full[i * rows : (i + 1) * rows]

    shape = (plan.n, rows, width)
    return pl.pallas_call(
        kernel,
        grid=(1,),
        in_specs=[whole(out_weight.shape)],
        out_specs=whole(shape),
        out_shape=jax.ShapeDtypeStruct(shape, BF16),
        compiler_params=params(16),
        cost_estimate=cost(0, 6 * width * D),
        name="split_out",
    )(out_weight)


def pack_out(plan, blocks):
    n, rows, width = blocks.shape

    def kernel(pos_ref, in_ref, out_ref, full_ref):
        plane = pos_ref[3]
        for i in range(n):
            full_ref[:, i * width : (i + 1) * width] = in_ref[i].astype(F32)
        mlp = full_ref[:, pl.ds(pl.multiple_of(D + plane * FH, PAIR), FH)]
        out_ref[:, :FH] = mlp.astype(BF16)
        heads = full_ref[:, pl.ds(pl.multiple_of(plane * DH, PAIR), DH)]
        out_ref[:, FH:] = heads.astype(BF16)

    return pl.pallas_call(
        kernel,
        grid=(1,),
        in_specs=[smem(), whole(blocks.shape)],
        out_specs=whole((rows, FH + DH)),
        out_shape=jax.ShapeDtypeStruct((rows, FH + DH), BF16),
        scratch_shapes=[pltpu.VMEM((rows, D + FF), F32)],
        compiler_params=params(16),
        cost_estimate=cost(rows * (D + FF), 6 * rows * D),
        name="pack_out",
    )(plan.pos, blocks)


def unpack_out(plan, own, swap):
    rows = own.shape[0]
    width = (D + FF) // plan.n

    def kernel(pos_ref, own_ref, swap_ref, out_ref, full_ref):
        first = pos_ref[3] == 0
        a, b = own_ref[...].astype(F32), swap_ref[...].astype(F32)
        for plane, part in enumerate((jnp.where(first, a, b), jnp.where(first, b, a))):
            full_ref[:, D + plane * FH : D + (plane + 1) * FH] = part[:, :FH]
            full_ref[:, plane * DH : (plane + 1) * DH] = part[:, FH:]
        for i in range(plan.n):
            out_ref[i] = full_ref[:, i * width : (i + 1) * width].astype(BF16)

    return pl.pallas_call(
        kernel,
        grid=(1,),
        in_specs=[smem(), whole(own.shape), whole(own.shape)],
        out_specs=whole((plan.n, rows, width)),
        out_shape=jax.ShapeDtypeStruct((plan.n, rows, width), BF16),
        scratch_shapes=[pltpu.VMEM((rows, D + FF), F32)],
        compiler_params=params(16),
        cost_estimate=cost(rows * (D + FF), 6 * rows * D),
        name="unpack_out",
    )(plan.pos, own, swap)


def stack(pieces):
    rows, width = pieces[0].shape

    def kernel(*refs):
        for i, ref in enumerate(refs[:-1]):
            refs[-1][i * rows : (i + 1) * rows, :] = ref[...]

    shape = (len(pieces) * rows, width)
    return pl.pallas_call(
        kernel,
        grid=(1,),
        in_specs=[whole((rows, width))] * len(pieces),
        out_specs=whole(shape),
        out_shape=jax.ShapeDtypeStruct(shape, BF16),
        compiler_params=params(8),
        cost_estimate=cost(0, 4 * shape[0] * width),
        name="stack",
    )(*pieces)


def fold(a):
    total = a[:, :PAIR]
    for i in range(1, a.shape[1] // PAIR):
        total = total + a[:, i * PAIR : (i + 1) * PAIR]
    return total


def partial_sums(plan, mlp, qkv, out, in_weight, vec_t):
    rows = in_weight.shape[0]

    def kernel(pos_ref, mlp_ref, qkv_ref, out_ref, w_ref, vec_ref, block_ref):
        plane = pos_ref[3]
        gain = vec_ref[:, :1]
        square = jnp.zeros((rows, PAIR), F32)
        dot = jnp.zeros((rows, PAIR), F32)

        def add(square, dot, hat, source, width):
            at = pl.ds(pl.multiple_of(source, PAIR), width)
            low = w_ref[:, at].astype(BF16).astype(F32)
            grad = hat * gain
            return square + fold(grad * grad), dot + fold(low * hat)

        hat = mlp_ref[:, :FH].astype(F32)
        square, dot = add(square, dot, hat, 3 * D + plane * FH, FH)
        for pair in range(PAIRS):
            for which in range(3):
                at = pair * QKV + which * PAIR
                hat = qkv_ref[:, at : at + PAIR].astype(F32)
                source = which * D + plane * DH + pair * PAIR
                square, dot = add(square, dot, hat, source, PAIR)
        value = out_ref[...].astype(F32)
        square = square + fold(value * value)
        lane = lax.broadcasted_iota(jnp.int32, (rows, VEC), 1)
        total = jnp.sum(dot, axis=1, keepdims=True)
        block_ref[:rows, :] = jnp.where(lane == 0, total, qkv_ref[:, QW:].astype(F32))
        square = jnp.sum(square, axis=0, keepdims=True) * 0.125
        block_ref[rows:, :] = jnp.broadcast_to(square, (8, PAIR))

    shape = (rows + 8, VEC)
    arrays = (mlp, qkv, out, in_weight, vec_t)
    return pl.pallas_call(
        kernel,
        grid=(1,),
        in_specs=[smem()] + [whole(a.shape) for a in arrays],
        out_specs=whole(shape),
        out_shape=jax.ShapeDtypeStruct(shape, F32),
        compiler_params=params(16),
        cost_estimate=cost(8 * rows * 6 * D, 14 * rows * 6 * D),
        name="partial_sums",
    )(plan.pos, *arrays)


def join_sums(own, swap):
    rows = own.shape[0] - 8

    def kernel(own_ref, swap_ref, vec_ref, total_ref):
        vec = own_ref[:rows, :] + swap_ref[:rows, :]
        vec_ref[...] = vec
        square = jnp.sum(vec * vec, axis=0, keepdims=True) * 0.125
        total_ref[...] = own_ref[rows:, :] + swap_ref[rows:, :] + jnp.broadcast_to(square, (8, VEC))

    return pl.pallas_call(
        kernel,
        grid=(1,),
        in_specs=[whole(own.shape)] * 2,
        out_specs=[whole((rows, VEC)), whole((8, VEC))],
        out_shape=[
            jax.ShapeDtypeStruct((rows, VEC), F32),
            jax.ShapeDtypeStruct((8, VEC), F32),
        ],
        compiler_params=params(16),
        cost_estimate=cost(4 * own.size, 12 * own.size),
        name="join_sums",
    )(own, swap)


def finish_out(blocks):
    n, rows, width = blocks.shape

    def kernel(in_ref, out_ref):
        out_ref[...] = in_ref[...].reshape(n * rows, width).astype(F32).T

    return pl.pallas_call(
        kernel,
        grid=(1,),
        in_specs=[whole(blocks.shape)],
        out_specs=whole((width, D)),
        out_shape=jax.ShapeDtypeStruct((width, D), F32),
        compiler_params=params(16),
        cost_estimate=cost(0, 6 * width * D),
        name="finish_out",
    )(blocks)


def finish_mlp(plan, own, swap, like, vec_t):
    rows = like.shape[0]

    def kernel(pos_ref, own_ref, swap_ref, vec_ref, grad_ref):
        mine = pl.program_id(0) // 2 == pos_ref[3]
        hat = jnp.where(mine, own_ref[...].astype(F32), swap_ref[...].astype(F32))
        grad_ref[...] = hat * vec_ref[:, :1]

    part = pl.BlockSpec((rows, D), lambda j: (0, j % 2))
    return pl.pallas_call(
        kernel,
        grid=(FF // D,),
        in_specs=[smem(), part, part, whole((rows, VEC))],
        out_specs=pl.BlockSpec((rows, D), lambda j: (0, 3 + j)),
        out_shape=jax.ShapeDtypeStruct(like.shape, F32),
        compiler_params=params(16),
        cost_estimate=cost(2 * rows * FF, 8 * rows * FF),
        name="finish_mlp",
    )(plan.pos, own, swap, vec_t)


def finish_qkv(plan, own, swap, vec_t, grad):
    rows = grad.shape[0]

    def kernel(pos_ref, own_ref, swap_ref, vec_ref, _, grad_ref):
        step = pl.program_id(0)
        first = pos_ref[3] == 0
        parts = []
        for pair in range(PAIRS):
            at = pl.ds(pl.multiple_of(pair * QKV + step * PAIR, PAIR), PAIR)
            parts.append([ref[:, at].astype(F32) for ref in (own_ref, swap_ref)])
        low = [jnp.where(first, a, b) for a, b in parts]
        high = [jnp.where(first, b, a) for a, b in parts]
        grad_ref[...] = jnp.concatenate(low + high, axis=1) * vec_ref[:, :1]

    return pl.pallas_call(
        kernel,
        grid=(3,),
        in_specs=[
            smem(),
            whole(own.shape),
            whole(own.shape),
            whole((rows, VEC)),
            pl.BlockSpec(memory_space=pl.ANY),
        ],
        out_specs=pl.BlockSpec((rows, D), lambda j: (0, j)),
        out_shape=jax.ShapeDtypeStruct(grad.shape, F32),
        input_output_aliases={4: 0},
        compiler_params=params(16),
        cost_estimate=cost(6 * rows * D, 24 * rows * D),
        name="finish_qkv",
    )(plan.pos, own, swap, vec_t, grad)


def prepare(plan, tokens, other_tokens, cotangent, other_cotangent, rows):
    tok = tokens.shape[0]
    kind = row_type(rows)

    def kernel(pos_ref, to_ref, tp_ref, co_ref, cp_ref, xo_ref, xp_ref, turned_ref, sum_ref, t_ref):
        for half, (from_ref, cot_ref, x_ref) in enumerate(
            ((to_ref, co_ref, xo_ref), (tp_ref, cp_ref, xp_ref))
        ):
            values = from_ref[...].astype(F32)
            centre = values - jnp.mean(values, axis=-1, keepdims=True)
            r = lax.rsqrt(jnp.mean(centre * centre, axis=-1, keepdims=True) + norm_eps)
            normal = centre * r
            x_ref[...] = normal.astype(BF16)
            cot = cot_ref[...].astype(F32)
            if half == 0:
                total = jnp.sum(cot, axis=0, keepdims=True)
                sum_ref[...] = jnp.broadcast_to(total, (8, D))
            for which, value in enumerate((normal, cot)):
                t_ref[...] = value.T.astype(kind)

                def put(at, a):
                    columns = slice(half * tok, (half + 1) * tok)
                    turned_ref[which, at : at + rows, columns] = a.astype(BF16)

                turn(plan, pos_ref, t_ref, rows, put)

    low = jax.ShapeDtypeStruct((tok, D), BF16)
    return pl.pallas_call(
        kernel,
        grid=(1,),
        in_specs=[smem()] + [whole((tok, D))] * 4,
        out_specs=[whole((tok, D))] * 2 + [whole((2, D, 2 * tok)), whole((8, D))],
        out_shape=[
            low,
            low,
            jax.ShapeDtypeStruct((2, D, 2 * tok), BF16),
            jax.ShapeDtypeStruct((8, D), F32),
        ],
        scratch_shapes=[pltpu.VMEM((D, tok), kind)],
        compiler_params=params(),
        cost_estimate=cost(40 * tok * D, 20 * tok * D),
        name="prepare",
    )(plan.pos, tokens, other_tokens, cotangent, other_cotangent)


def mlp_forward(plan, x_own, x_other, turned, pieces):
    tok = x_own.shape[0]
    rows = pieces[0].shape[0] // plan.zs
    tile = 512
    n = len(pieces)

    half_d = D // 2

    def kernel(pos_ref, xo_ref, xp_ref, ct_ref, *rest):
        refs, (mix_ref, slope_ref, g_own_ref, g_other_ref, w_ref) = rest[:n], rest[n:]
        place(plan, pos_ref, refs, rows, w_ref)
        w = w_ref[...].astype(BF16)
        for half, x_ref in enumerate((xo_ref, xp_ref)):
            v = mm(x_ref[...], w)
            v2 = v * v
            t = jnp.tanh(v * (GELU_C + (GELU_C * 0.044715) * v2))
            h = 0.5 + 0.5 * t
            g = v * h
            slope = h + 2.0 * g * (1.0 - h) * (GELU_C + (3.0 * GELU_C * 0.044715) * v2)
            mix_ref[half] = g.astype(BF16)
            slope_ref[half] = slope.astype(BF16)
        g = mm(ct_ref[0], mix_ref[...].reshape(2 * tok, tile)).astype(BF16)
        g_own_ref[...] = g[:half_d]
        g_other_ref[...] = g[half_d:]

    block = pl.BlockSpec((2, tok, tile), lambda j: (0, 0, j))
    grad = pl.BlockSpec((half_d, tile), lambda j: (0, j))
    return pl.pallas_call(
        kernel,
        grid=(FH // tile,),
        in_specs=[smem()]
        + [whole((tok, D))] * 2
        + [pl.BlockSpec((1, D, 2 * tok), lambda j: (1, 0, 0))]
        + [pl.BlockSpec((plan.zs * rows, tile), lambda j: (0, j))] * n,
        out_specs=[block, block, grad, grad],
        out_shape=[jax.ShapeDtypeStruct((2, tok, FH), BF16)] * 2
        + [jax.ShapeDtypeStruct((half_d, FH + DH), BF16)] * 2,
        scratch_shapes=[pltpu.VMEM((D, tile), row_type(rows))],
        compiler_params=params(),
        cost_estimate=cost(8 * tok * D * FH, 12 * tok * FH, 2 * tok * FH),
        name="mlp_forward",
    )(plan.pos, x_own, x_other, turned, *pieces)


def head_means(a, block_ref):
    high = a.astype(BF16)
    low = (a - high.astype(F32)).astype(BF16)
    return mm(high, block_ref[...]) + mm(low, block_ref[...])


def attention_forward(plan, x_own, x_other, pieces, ids, block, turned, g_own, g_other):
    tok = x_own.shape[0]
    rows = pieces[0].shape[0] // plan.zs
    n = len(pieces)
    half_d = D // 2

    def kernel(pos_ref, xo_ref, xp_ref, ido_ref, idp_ref, block_ref, ct_ref, _, __, *rest):
        refs, vec_refs = rest[:n], rest[n : 2 * n]
        (
            qk_ref, v_ref, n_ref, r_ref, att_ref, p_ref, gain_ref, g_own_ref, g_other_ref,
            w_ref, vs_ref, all_ref,
        ) = rest[2 * n :]
        step = pl.program_id(0)

        @pl.when(step == 0)
        def _():
            place(plan, pos_ref, vec_refs, rows, vs_ref)
            gain_ref[...] = vs_ref[...].astype(F32).T[:8]

        place(plan, pos_ref, refs, rows, w_ref)
        w = w_ref[...].astype(BF16)
        column = pl.ds(pl.multiple_of(pos_ref[3] * DH + step * PAIR, PAIR), PAIR)
        gain = jnp.concatenate(
            [gain_ref[1:2, column] * (HD ** (-0.5)), gain_ref[2:3, column]], axis=1
        )
        first = lax.broadcasted_iota(jnp.int32, (tok, PAIR), 1) < HD
        for half, x_ref in enumerate((xo_ref, xp_ref)):
            raw = mm(x_ref[...], w)
            qk = raw[:, : 2 * PAIR]
            centre = qk - head_means(qk, block_ref)
            r = lax.rsqrt(mm((centre * centre).astype(BF16), block_ref[...]) + norm_eps)
            normal = centre * r
            n_ref[half] = normal.astype(BF16)
            r_ref[half] = r.astype(BF16)
            low = (normal * gain).astype(BF16)
            qk_ref[half] = low
            q, k = low[:, :PAIR], low[:, PAIR:]
            v = raw[:, 2 * PAIR :].astype(BF16)
            v_ref[half] = v
            number = (ido_ref, idp_ref)[half][...].astype(F32)
            same = jnp.broadcast_to(number, (8, tok)).T[:, :1] == number
            att = []
            zero = jnp.zeros_like(q)
            for head in range(2):
                qh = jnp.where(first, q, zero) if head == 0 else jnp.where(first, zero, q)
                e = jnp.where(same, jnp.exp(mm(qh, k, NT)), 0.0)
                p = (e * (1.0 / jnp.sum(e, axis=1, keepdims=True))).astype(BF16)
                p_ref[half, head] = p
                att.append(mm(p, v))
            att_low = jnp.where(first, att[0], att[1]).astype(BF16)
            att_ref[half] = att_low
            at = pl.ds(pl.multiple_of(step * PAIR, PAIR), PAIR)
            all_ref[half * tok : (half + 1) * tok, at] = att_low

        @pl.when(step == PAIRS - 1)
        def _():
            g = mm(ct_ref[0], all_ref[...]).astype(BF16)
            g_own_ref[...] = g[:half_d]
            g_other_ref[...] = g[half_d:]

    pair = pl.BlockSpec((2, tok, PAIR), lambda j: (0, 0, j))
    pair2 = pl.BlockSpec((2, tok, 2 * PAIR), lambda j: (0, 0, j))
    small = jax.ShapeDtypeStruct((2, tok, DH), BF16)
    small2 = jax.ShapeDtypeStruct((2, tok, 2 * DH), BF16)
    heads = pl.BlockSpec((half_d, DH), lambda j: (0, FH // DH))
    return pl.pallas_call(
        kernel,
        grid=(PAIRS,),
        in_specs=[smem()]
        + [whole((tok, D))] * 2
        + [whole((1, tok))] * 2
        + [whole((2 * PAIR, 2 * PAIR))]
        + [pl.BlockSpec((1, D, 2 * tok), lambda j: (1, 0, 0))]
        + [pl.BlockSpec(memory_space=pl.ANY)] * 2
        + [pl.BlockSpec((plan.zs * rows, QKV), lambda j: (0, j))] * n
        + [pl.BlockSpec((plan.zs * rows, VEC), lambda j: (0, QW // VEC))] * n,
        out_specs=[pair2, pair, pair2, pair2, pair]
        + [pl.BlockSpec((2, 2, tok, tok), lambda j: (0, j, 0, 0)), whole((8, D))]
        + [heads, heads],
        out_shape=[small2, small, small2, small2, small]
        + [
            jax.ShapeDtypeStruct((2, 2 * PAIRS, tok, tok), BF16),
            jax.ShapeDtypeStruct((8, D), F32),
            jax.ShapeDtypeStruct(g_own.shape, BF16),
            jax.ShapeDtypeStruct(g_own.shape, BF16),
        ],
        input_output_aliases={7: 7, 8: 8},
        scratch_shapes=[
            pltpu.VMEM((D, QKV), row_type(rows)),
            pltpu.VMEM((D, VEC), row_type(rows)),
            pltpu.VMEM((2 * tok, DH), BF16),
        ],
        compiler_params=params(),
        cost_estimate=cost(4 * tok * D * QW, 20 * MIB, 12 * tok * tok),
        name="attention_forward",
    )(
        plan.pos, x_own, x_other, *ids, block, turned, g_own, g_other, *pieces, *pieces,
    )


TILE = 256


def token_tiles(tok):
    per = tok // TILE

    def pair(j):
        return (j // per, j % per, 0)

    def own(j):
        return jnp.minimum(j, per - 1)

    def other(j):
        return jnp.maximum(j - per, 0)

    return per, pair, own, other


def output_step(plan, att, mixed, slope, cot_own, cot_other, pieces):
    tok = cot_own.shape[0]
    rows = pieces[0].shape[0] // plan.zs
    n = len(pieces)
    per, pair, own, other = token_tiles(tok)

    def kernel(pos_ref, att_ref, mix_ref, slope_ref, co_ref, cp_ref, *rest):
        refs = rest[:n]
        out_own_ref, out_other_ref, d_att_ref, d_in_ref, w_ref = rest[n:]
        step = pl.program_id(0)

        @pl.when(step == 0)
        def _():
            place(plan, pos_ref, refs, rows, w_ref)

        w = w_ref[...].astype(BF16)
        cot = jnp.where(step < per, co_ref[...], cp_ref[...])
        for at in range(0, FH, DH):
            d = mm(cot, w[:, at : at + DH])
            slopes = slope_ref[0, :, at : at + DH].astype(F32)
            d_in_ref[0, :, at : at + DH] = (d * slopes).astype(BF16)
        d_att_ref[0] = mm(cot, w[:, FH:]).astype(BF16)
        out = mm(mix_ref[0], w[:, :FH], NT) + mm(att_ref[0], w[:, FH:], NT)

        @pl.when(step < per)
        def _():
            out_own_ref[...] = out

        @pl.when(step >= per)
        def _():
            out_other_ref[...] = out.astype(BF16)

    return pl.pallas_call(
        kernel,
        grid=(2 * per,),
        in_specs=[
            smem(),
            pl.BlockSpec((1, TILE, DH), pair),
            pl.BlockSpec((1, TILE, FH), pair),
            pl.BlockSpec((1, TILE, FH), pair),
            pl.BlockSpec((TILE, D), lambda j: (own(j), 0)),
            pl.BlockSpec((TILE, D), lambda j: (other(j), 0)),
        ]
        + [whole(pieces[0].shape)] * n,
        out_specs=[
            pl.BlockSpec((TILE, D), lambda j: (own(j), 0)),
            pl.BlockSpec((TILE, D), lambda j: (other(j), 0)),
            pl.BlockSpec((1, TILE, DH), pair),
            pl.BlockSpec((1, TILE, FH), pair),
        ],
        out_shape=[
            jax.ShapeDtypeStruct((tok, D), F32),
            jax.ShapeDtypeStruct((tok, D), BF16),
            jax.ShapeDtypeStruct((2, tok, DH), BF16),
            jax.ShapeDtypeStruct((2, tok, FH), BF16),
        ],
        scratch_shapes=[pltpu.VMEM((D, FH + DH), row_type(rows))],
        compiler_params=params(40),
        cost_estimate=cost(8 * tok * (FH + DH) * D, 20 * MIB),
        name="output_step",
    )(plan.pos, att, mixed, slope, cot_own, cot_other, *pieces)


def mlp_gradient(turned, d_inner):
    tok = d_inner.shape[1]
    half_d = D // 2
    tile = 512

    def kernel(xt_ref, d_ref, g_own_ref, g_other_ref):
        g = mm(xt_ref[0], d_ref[...].reshape(2 * tok, tile)).astype(BF16)
        g_own_ref[...] = g[:half_d]
        g_other_ref[...] = g[half_d:]

    grad = pl.BlockSpec((half_d, tile), lambda j: (0, j))
    return pl.pallas_call(
        kernel,
        grid=(FH // tile,),
        in_specs=[
            pl.BlockSpec((1, D, 2 * tok), lambda j: (0, 0, 0)),
            pl.BlockSpec((2, tok, tile), lambda j: (0, 0, j)),
        ],
        out_specs=[grad, grad],
        out_shape=[jax.ShapeDtypeStruct((half_d, FH), BF16)] * 2,
        compiler_params=params(40),
        cost_estimate=cost(4 * tok * D * FH, 8 * MIB),
        name="mlp_gradient",
    )(turned, d_inner)


def scaled_gradient(plan, d_inner, d_qkv, mlp_pieces, qkv_pieces):
    tok = d_inner.shape[1]
    rows = mlp_pieces[0].shape[0] // plan.zs
    n = len(mlp_pieces)
    per, pair, own, other = token_tiles(tok)

    def kernel(pos_ref, dm_ref, dq_ref, *rest):
        refs_m, refs_q = rest[:n], rest[n : 2 * n]
        e_own_ref, e_other_ref, wm_ref, wq_ref = rest[2 * n :]
        step = pl.program_id(0)

        @pl.when(step == 0)
        def _():
            place(plan, pos_ref, refs_m, rows, wm_ref)
            place(plan, pos_ref, refs_q, rows, wq_ref)

        e = mm(dm_ref[0], wm_ref[...].astype(BF16), NT)
        e = e + mm(dq_ref[0], wq_ref[...].astype(BF16)[:, :QW], NT)

        @pl.when(step < per)
        def _():
            e_own_ref[...] = e

        @pl.when(step >= per)
        def _():
            e_other_ref[...] = e.astype(BF16)

    return pl.pallas_call(
        kernel,
        grid=(2 * per,),
        in_specs=[
            smem(),
            pl.BlockSpec((1, TILE, FH), pair),
            pl.BlockSpec((1, TILE, QW), pair),
        ]
        + [whole(mlp_pieces[0].shape)] * n
        + [whole(qkv_pieces[0].shape)] * n,
        out_specs=[
            pl.BlockSpec((TILE, D), lambda j: (own(j), 0)),
            pl.BlockSpec((TILE, D), lambda j: (other(j), 0)),
        ],
        out_shape=[
            jax.ShapeDtypeStruct((tok, D), F32),
            jax.ShapeDtypeStruct((tok, D), BF16),
        ],
        scratch_shapes=[
            pltpu.VMEM((D, FH), row_type(rows)),
            pltpu.VMEM((D, QW + VEC), row_type(rows)),
        ],
        compiler_params=params(48),
        cost_estimate=cost(4 * tok * (FH + QW) * D, 16 * MIB),
        name="scaled_gradient",
    )(plan.pos, d_inner, d_qkv, *mlp_pieces, *qkv_pieces)


def attention_backward(plan, turned, saved, d_att, block, gains, cot_sum, rows):
    qk, v, normals, factors, probs = saved
    tok = d_att.shape[1]
    half_d = D // 2
    kind = row_type(rows)

    def kernel(pos_ref, xt_ref, qk_ref, v_ref, n_ref, r_ref, p_ref, da_ref, block_ref, gain_ref,
               cot_ref, g_own_ref, g_other_ref, d_ref, vec_ref, turn_ref):
        step = pl.program_id(0)

        @pl.when(step == 0)
        def _():
            vec_ref[...] = jnp.zeros_like(vec_ref)
            vec_ref[3:4, :] = cot_ref[:1]

        column = pl.ds(pl.multiple_of(pos_ref[3] * DH + step * PAIR, PAIR), PAIR)
        gain = jnp.concatenate(
            [gain_ref[1:2, column] * (HD ** (-0.5)), gain_ref[2:3, column]], axis=1
        )
        first = lax.broadcasted_iota(jnp.int32, (tok, PAIR), 1) < HD

        def heads(a):
            zero = jnp.zeros_like(a)
            return jnp.concatenate([jnp.where(first, a, zero), jnp.where(first, zero, a)], axis=0)

        for half in range(2):
            qb, kb, vb = qk_ref[half, :, :PAIR], qk_ref[half, :, PAIR:], v_ref[half]
            da = heads(da_ref[half])
            p_low = p_ref[half].reshape(2 * tok, tok)
            p = p_low.astype(F32)
            t = p * mm(da, vb, NT)
            ds = (t - p * jnp.sum(t, axis=1, keepdims=True)).astype(BF16)
            d_value = mm(da.T, p_low).T
            d_key = mm(heads(qb).T, ds).T
            dq = mm(ds, kb)
            d_query = jnp.where(first, dq[:tok], dq[tok:])
            d = jnp.concatenate([d_query, d_key], axis=1)
            normal = n_ref[half].astype(F32)
            sums = jnp.sum(d * normal, axis=0, keepdims=True)
            vec_ref[1:2, column] += sums[:, :PAIR] * (HD ** (-0.5))
            vec_ref[2:3, column] += sums[:, PAIR:]
            e = d * gain
            along = mm((e * normal).astype(BF16), block_ref[...])
            d_raw = r_ref[half].astype(F32) * (e - head_means(e, block_ref) - normal * along)
            d_ref[half, :, : 2 * PAIR] = d_raw.astype(BF16)
            d_ref[half, :, 2 * PAIR :] = d_value.astype(BF16)
        g = mm(xt_ref[0], d_ref[...].reshape(2 * tok, QKV)).astype(BF16)
        at = pl.ds(pl.multiple_of(step * QKV, QKV), QKV)
        g_own_ref[:, at] = g[:half_d]
        g_other_ref[:, at] = g[half_d:]

        @pl.when(step == PAIRS - 1)
        def _():
            turn_ref[...] = vec_ref[...].T.astype(kind)

            def put(at, a):
                ref = g_own_ref if at < half_d else g_other_ref
                ref[at % half_d : at % half_d + rows, QW:] = a.astype(BF16)

            turn(plan, pos_ref, turn_ref, rows, put)

    pair = pl.BlockSpec((2, tok, PAIR), lambda j: (0, 0, j))
    pair2 = pl.BlockSpec((2, tok, 2 * PAIR), lambda j: (0, 0, j))
    return pl.pallas_call(
        kernel,
        grid=(PAIRS,),
        in_specs=[smem(), pl.BlockSpec((1, D, 2 * tok), lambda j: (0, 0, 0))]
        + [pair2, pair, pair2, pair2]
        + [
            pl.BlockSpec((2, 2, tok, tok), lambda j: (0, j, 0, 0)),
            pair,
            whole((2 * PAIR, 2 * PAIR)),
            whole((8, D)),
            whole((8, D)),
        ],
        out_specs=[whole((half_d, QW + VEC))] * 2
        + [pl.BlockSpec((2, tok, QKV), lambda j: (0, 0, j))],
        out_shape=[jax.ShapeDtypeStruct((half_d, QW + VEC), BF16)] * 2
        + [jax.ShapeDtypeStruct((2, tok, QW), BF16)],
        scratch_shapes=[pltpu.VMEM((VEC, D), F32), pltpu.VMEM((D, VEC), kind)],
        compiler_params=params(48),
        cost_estimate=cost(16 * tok * D * QW, 24 * MIB),
        name="attention_backward",
    )(plan.pos, turned, qk, v, normals, factors, probs, d_att, block, gains, cot_sum)


def token_gradient(tokens, cotangent, e_own, e_recv):
    tok = tokens.shape[0]

    def kernel(t_ref, c_ref, own_ref, recv_ref, out_ref):
        rows = t_ref[...].astype(F32)
        centre = rows - jnp.mean(rows, axis=-1, keepdims=True)
        r = lax.rsqrt(jnp.mean(centre * centre, axis=-1, keepdims=True) + norm_eps)
        normal = centre * r
        e = own_ref[...] + recv_ref[...].astype(F32)
        mean = jnp.mean(e, axis=-1, keepdims=True)
        along = jnp.mean(e * normal, axis=-1, keepdims=True)
        out_ref[...] = c_ref[...].astype(F32) + r * (e - mean - normal * along)

    block = pl.BlockSpec((tok // 4, D), lambda j: (j, 0))
    return pl.pallas_call(
        kernel,
        grid=(4,),
        in_specs=[block] * 4,
        out_specs=block,
        out_shape=jax.ShapeDtypeStruct((tok, D), F32),
        compiler_params=params(16),
        cost_estimate=cost(20 * tok * D, 14 * tok * D),
        name="token_gradient",
    )(tokens, cotangent, e_own, e_recv)


def adamw(master, first, second, grad, factor):
    clipped = grad * factor
    first_new = beta_one * first + (1.0 - beta_one) * clipped
    second_new = beta_two * second + (1.0 - beta_two) * clipped * clipped
    first_hat = first_new * (1.0 / (1.0 - beta_one**ADAM_STEP))
    second_hat = second_new * (1.0 / (1.0 - beta_two**ADAM_STEP))
    update = -learning * (first_hat / (jnp.sqrt(second_hat) + epsilon) + decay_rate * master)
    return (update, first_new, second_new)


def optimize(total, vec_cols, ins, outs, vecs):
    rows, out_rows = ins[0].shape[0], outs[0].shape[0]
    steps = 3

    def kernel(total_ref, cols_ref, *refs):
        in_refs, out_refs, vec_refs, rest = refs[:4], refs[4:8], refs[8:11], refs[11:]
        vec_grad_ref, norm_ref, pad_ref = rest[0], rest[1], rest[-1]
        sums = jnp.sum(jnp.sum(total_ref[...], axis=1, keepdims=True), axis=0, keepdims=True)
        norm = jnp.sqrt(sums)
        factor = jnp.minimum(1.0, math.sqrt(PARAMS) / norm)
        for group, results in ((in_refs, rest[2:5]), (out_refs, rest[5:8])):
            for ref, value in zip(results, adamw(*[ref[...] for ref in group], factor)):
                ref[...] = value

        @pl.when(pl.program_id(0) == 0)
        def _():
            norm_ref[...] = norm
            pad_ref[...] = jnp.zeros_like(pad_ref)
            pad_ref[:rows] = cols_ref[...]
            grad = pad_ref[...].T[:4, :rows]
            vec_grad_ref[...] = grad
            values = adamw(*[ref[...] for ref in vec_refs], grad, factor)
            for ref, value in zip(rest[8:11], values):
                ref[...] = value

    in_block = pl.BlockSpec((rows, 7 * D // steps), lambda j: (0, j))
    out_block = pl.BlockSpec((out_rows // steps, D), lambda j: (j, 0))
    shapes = [jax.ShapeDtypeStruct(a.shape, F32) for a in (ins[0], outs[0], vecs[0])]
    return pl.pallas_call(
        kernel,
        grid=(steps,),
        in_specs=[whole((8, 128)), whole(vec_cols.shape)]
        + [in_block] * 4
        + [out_block] * 4
        + [whole(vecs[0].shape)] * 3,
        out_specs=[whole(vecs[0].shape), whole((1, 1))]
        + [in_block] * 3
        + [out_block] * 3
        + [whole(vecs[0].shape)] * 3,
        out_shape=[shapes[2], jax.ShapeDtypeStruct((1, 1), F32)]
        + [shapes[0]] * 3
        + [shapes[1]] * 3
        + [shapes[2]] * 3,
        scratch_shapes=[pltpu.VMEM((128, 128), F32)],
        compiler_params=params(16),
        cost_estimate=cost(20 * 7 * D * rows, 28 * 13 * D * rows),
        name="optimize",
    )(total, vec_cols, *ins, *outs, *vecs)


def local(
    tokens,
    cotangent,
    image_ids,
    in_weight,
    out_weight,
    vectors,
    in_moment,
    out_moment,
    vec_moment,
    in_second,
    out_second,
    vec_second,
):
    plan = Plan(lax.axis_size("fsdp"), lax.axis_size("dp"))
    rows = in_weight.shape[0]

    low_vec = vectors.astype(BF16).astype(F32)
    vec_t = jnp.pad(low_vec.T, ((0, 0), (0, VEC - 4)))
    mlp_piece, qkv_piece = pack_in(plan, in_weight, vec_t)
    other_tokens = plan.swap_plane(tokens)
    other_cotangent = plan.swap_plane(cotangent)
    blocks = lax.all_to_all(split_out(plan, out_weight, rows), "fsdp", 0, 0)

    def z_all(piece):
        return [plan.from_z(piece, s) for s in range(1, plan.zs)]

    def y_all(column):
        return [plan.from_y(column, t) for t in range(1, plan.ys)]

    def core_all(arrays):
        return [plan.swap_core(a) for a in arrays]

    def held(groups):
        flat = iter(fence(*[a for group in groups for a in group]))
        return [[next(flat) for _ in group] for group in groups]

    mlp_z = z_all(mlp_piece)
    mlp_z, (qkv_piece,) = held([mlp_z, [qkv_piece]])
    mlp_col = stack([mlp_piece] + mlp_z)
    mlp_y = y_all(mlp_col)
    qkv_z = z_all(qkv_piece)
    out_piece = pack_out(plan, blocks)
    x_own, x_other, turned, cot_sum = prepare(
        plan, tokens, other_tokens, cotangent, other_cotangent, rows
    )
    mlp_y, qkv_z, (mlp_col, out_piece, x_own) = held(
        [mlp_y, qkv_z, [mlp_col, out_piece, x_own]]
    )
    mlp_pieces = [mlp_col] + mlp_y + core_all([mlp_col] + mlp_y)
    qkv_col = stack([qkv_piece] + qkv_z)
    qkv_y = y_all(qkv_col)
    out_z = z_all(out_piece)
    mixed, slope, g_own, g_other = mlp_forward(plan, x_own, x_other, turned, mlp_pieces)
    qkv_y, out_z, (qkv_col, mixed, slope, g_own, g_other, ids_now) = held(
        [qkv_y, out_z, [qkv_col, mixed, slope, g_own, g_other, image_ids]]
    )
    other_ids = plan.swap_plane(ids_now)
    qkv_pieces = [qkv_col] + qkv_y + core_all([qkv_col] + qkv_y)
    out_col = stack([out_piece] + out_z)
    out_y = y_all(out_col)
    out_core = core_all([out_col])
    lane = jnp.arange(2 * PAIR) // HD
    block = jnp.where(lane[:, None] == lane[None, :], 1.0 / HD, 0.0).astype(BF16)
    *saved, att, probs, gains, g_own, g_other = attention_forward(
        plan, x_own, x_other, qkv_pieces, (image_ids[None, :], other_ids[None, :]), block,
        turned, g_own, g_other,
    )
    saved = tuple(saved) + (probs,)
    out_y, out_core, (att, g_own, g_other) = held([out_y, out_core, [att, g_own, g_other]])
    s_out = Scatter(plan, g_own, g_other)
    s_out.by_core()
    out_core = out_core + core_all(out_y)
    s_out.recv, *out_core = fence(s_out.recv, *out_core)
    s_out.by_y()
    out_pieces = [out_col] + out_y + out_core
    out_mine, out_theirs, d_att, d_inner = output_step(
        plan, att, mixed, slope, cotangent, other_cotangent, out_pieces
    )
    g_own, g_other = mlp_gradient(turned, d_inner)
    s_mlp = Scatter(plan, g_own, g_other)
    s_mlp.by_core()
    s_out.y_got, (out_theirs, g_own) = held([s_out.y_got, [out_theirs, g_own]])
    s_out.by_z()
    out_recv = plan.swap_plane(out_theirs)
    s_mlp.recv, d_att = fence(s_mlp.recv, d_att)
    s_mlp.by_y()
    g_own, g_other, d_qkv = attention_backward(
        plan, turned, saved, d_att, block, gains, cot_sum, rows
    )
    s_out.z_got, s_mlp.y_got, (g_own, g_other, d_qkv, out_recv) = held(
        [s_out.z_got, s_mlp.y_got, [g_own, g_other, d_qkv, out_recv]]
    )
    s_qkv = Scatter(plan, g_own, g_other)
    s_qkv.by_core()
    out_sum = s_out.total()
    out_swap = plan.swap_plane(out_sum)
    parts, s_mlp.y_got, (out_sum, d_qkv) = held([s_qkv.y_parts(), s_mlp.y_got, [out_sum, d_qkv]])
    s_qkv.by_y(parts)
    s_mlp.by_z()
    e_own, e_other = scaled_gradient(plan, d_inner, d_qkv, mlp_pieces, qkv_pieces)
    out_swap, e_other, e_own = fence(out_swap, e_other, e_own)
    e_recv = plan.swap_plane(e_other)
    blocks = unpack_out(plan, plan.over_pairs(out_sum), plan.over_pairs(out_swap))
    s_qkv.y_got, s_mlp.z_got, (blocks,) = held([s_qkv.y_got, s_mlp.z_got, [blocks]])
    s_qkv.by_z()
    blocks = lax.all_to_all(blocks, "fsdp", 0, 0)
    result = (
        tokens.astype(F32) + out_mine + out_recv.astype(F32) + gains[3][None, :]
    ).astype(BF16)
    mlp_sum = s_mlp.total()
    mlp_swap = plan.swap_plane(mlp_sum)
    s_qkv.z_got, (result,) = held([s_qkv.z_got, [result]])
    qkv_sum = plan.over_pairs(s_qkv.total())
    mlp_sum, out_sum = plan.over_pairs(mlp_sum), plan.over_pairs(out_sum)
    own = partial_sums(plan, mlp_sum, qkv_sum, out_sum, in_weight, vec_t)
    swap = plan.swap_plane(own)
    input_grad = token_gradient(tokens, cotangent, e_own, e_recv)
    swap, qkv_sum, mlp_swap, input_grad = fence(swap, qkv_sum, mlp_swap, input_grad)
    vec_cols, square = join_sums(own, swap)
    qkv_swap = plan.swap_plane(qkv_sum)
    in_grad = finish_mlp(plan, mlp_sum, plan.over_pairs(mlp_swap), in_weight, vec_t)
    out_grad = finish_out(blocks)
    total, out_grad, _, in_grad = plan.total(
        square, out_grad, in_grad, lambda a: finish_qkv(plan, qkv_sum, qkv_swap, vec_t, a)
    )
    vec_grad, norm, *updates = optimize(
        total,
        vec_cols,
        (in_weight, in_moment, in_second, in_grad),
        (out_weight, out_moment, out_second, out_grad),
        (vectors, vec_moment, vec_second),
    )
    in_update, in_mean, in_square = updates[:3]
    out_update, out_mean, out_square = updates[3:6]
    vec_update, vec_mean, vec_square = updates[6:]
    return (
        result,
        input_grad,
        in_grad,
        out_grad,
        vec_grad,
        norm.reshape(()),
        in_update,
        out_update,
        vec_update,
        in_mean,
        out_mean,
        vec_mean,
        in_square,
        out_square,
        vec_square,
    )


def solution(mesh):
    in_specs = (
        P(("dp", "fsdp"), None),
        P(("dp", "fsdp"), None),
        P(("dp", "fsdp")),
        P("fsdp", None),
        P("fsdp", None),
        P(None, "fsdp"),
        P("fsdp", None),
        P("fsdp", None),
        P(None, "fsdp"),
        P("fsdp", None),
        P("fsdp", None),
        P(None, "fsdp"),
    )
    out_specs = (
        P(("dp", "fsdp"), None),
        P(("dp", "fsdp"), None),
        P("fsdp", None),
        P("fsdp", None),
        P(None, "fsdp"),
        P(),
        P("fsdp", None),
        P("fsdp", None),
        P(None, "fsdp"),
        P("fsdp", None),
        P("fsdp", None),
        P(None, "fsdp"),
        P("fsdp", None),
        P("fsdp", None),
        P(None, "fsdp"),
    )
    return jax.shard_map(local, mesh=mesh, in_specs=in_specs, out_specs=out_specs, check_vma=False)
```

```python
import math

import jax
import jax.numpy as jnp
import numpy as np
from jax import lax
from jax.experimental import pallas as pl
from jax.experimental.pallas import tpu as pltpu
from jax.sharding import PartitionSpec as P

D = 768
H = 12
HD = 64
FF = 3072
ADAM_STEP = 10
PARAMS = 7080960

beta_one = 0.9
beta_two = 0.95
learning = 0.03
decay_rate = 0.1
epsilon = 1e-08
norm_eps = 1e-06

F32 = jnp.float32
BF16 = jnp.bfloat16
DH = D // 2
FH = FF // 2
PAIR = 128
PAIRS = DH // PAIR
QKV = 3 * PAIR
QW = PAIRS * QKV
VEC = 128
GELU_C = math.sqrt(2.0 / math.pi)
MIB = 1 << 20

NT = (((1,), (1,)), ((), ()))
TN = (((0,), (0,)), ((), ()))


def mm(a, b, dims=(((1,), (0,)), ((), ()))):
    return lax.dot_general(a, b, dims, preferred_element_type=F32)


def fence(*arrays):
    return lax.optimization_barrier(arrays)


class Plan:
    def __init__(self, n_fsdp, n_dp):
        chips = n_fsdp // 2
        self.n, self.n_dp, self.chips = n_fsdp, n_dp, chips
        self.zs = 4 if chips % 4 == 0 else chips
        self.ys = chips // self.zs
        index = lax.axis_index("fsdp")
        self.core = index % 2
        self.y = (index // 2) % self.ys
        self.z = index // (2 * self.ys)
        self.plane = lax.axis_index("dp") % 2
        self.pos = jnp.stack([self.z, self.y, self.core, self.plane]).astype(jnp.int32)
        self.order = [
            (c, t, s) for c in range(2) for t in range(self.ys) for s in range(self.zs)
        ]

    def index(self, z, y, core):
        return ((z % self.zs) * self.ys + y % self.ys) * 2 + core

    def all(self):
        return [
            (z, y, c) for z in range(self.zs) for y in range(self.ys) for c in range(2)
        ]

    def from_z(self, a, s):
        pairs = [(self.index(z + s, y, c), self.index(z, y, c)) for z, y, c in self.all()]
        return lax.ppermute(a, "fsdp", pairs)

    def from_y(self, a, t):
        pairs = [(self.index(z, y + t, c), self.index(z, y, c)) for z, y, c in self.all()]
        return lax.ppermute(a, "fsdp", pairs)

    def swap_core(self, a):
        pairs = [(self.index(z, y, c), self.index(z, y, 1 - c)) for z, y, c in self.all()]
        return lax.ppermute(a, "fsdp", pairs)

    def swap_plane(self, a):
        return lax.ppermute(a, "dp", [(i, i ^ 1) for i in range(self.n_dp)])

    def over_pairs(self, a):
        if self.n_dp == 2:
            return a
        groups = [list(range(p, self.n_dp, 2)) for p in range(2)]
        return lax.psum(a.astype(F32), "dp", axis_index_groups=groups)

    def total(self, a, *beside):
        a = a + self.swap_core(a)
        beside = list(beside)
        count = 0
        for step, size in ((2, self.ys), (2 * self.ys, self.zs)):
            m = 1
            while m < size:
                pairs = [(i, i ^ (m * step)) for i in range(self.n)]
                got = lax.ppermute(a, "fsdp", pairs)
                if count < len(beside):
                    if callable(beside[count]):
                        beside[count] = beside[count](beside[count - 1])
                    got, beside[count] = fence(got, beside[count])
                a = a + got
                m, count = 2 * m, count + 1
        for i in range(count, len(beside)):
            beside[i] = beside[i](beside[i - 1])
        return [a] + beside

    def row(self, pos_ref, piece, rows):
        c, t, s = piece
        z = lax.rem(pos_ref[0] + s, self.zs)
        y = lax.rem(pos_ref[1] + t, self.ys)
        core = lax.rem(pos_ref[2] + c, 2)
        at = ((z * self.ys + y) * 2 + core) * rows
        return pl.multiple_of(at, math.gcd(rows, 16))


class Scatter:
    def __init__(self, plan, own, other):
        self.plan, self.own, self.other = plan, own, other
        self.rows = own.shape[0] // plan.chips

    def by_core(self):
        self.recv = self.plan.swap_core(self.other)

    def sums(self, begin, end, arrays):
        total = self.own[begin:end].astype(F32) + self.recv[begin:end].astype(F32)
        for a in arrays:
            total = total + a.astype(F32)
        return total

    def y_parts(self):
        size = self.plan.zs * self.rows
        return [
            self.sums(t * size, (t + 1) * size, ()).astype(BF16)
            for t in range(1, self.plan.ys)
        ]

    def by_y(self, parts=None):
        parts = self.y_parts() if parts is None else parts
        self.y_got = [self.plan.from_y(a, -t - 1) for t, a in enumerate(parts)]

    def part(self, s):
        at = slice(s * self.rows, (s + 1) * self.rows)
        return self.sums(at.start, at.stop, [a[at] for a in self.y_got])

    def by_z(self):
        parts = [self.part(s).astype(BF16) for s in range(1, self.plan.zs)]
        self.z_got = [self.plan.from_z(a, -s - 1) for s, a in enumerate(parts)]

    def total(self):
        total = self.part(0)
        for a in self.z_got:
            total = total + a.astype(F32)
        return total.astype(BF16)


def smem():
    return pl.BlockSpec(memory_space=pltpu.SMEM)


def whole(shape):
    return pl.BlockSpec(shape, lambda *_: (0,) * len(shape))


def params(mib=58):
    return pltpu.CompilerParams(
        dimension_semantics=("arbitrary",), vmem_limit_bytes=mib * MIB
    )


def cost(flops, nbytes, exps=0):
    return pl.CostEstimate(flops=int(flops), bytes_accessed=int(nbytes), transcendentals=int(exps))


def row_type(rows):
    return BF16 if rows % 16 == 0 else F32


def place(plan, pos_ref, refs, rows, out_ref):
    for i, piece in enumerate(plan.order):
        ref, at = refs[i // plan.zs], i % plan.zs * rows
        part = ref[at : at + rows, :].astype(out_ref.dtype)
        out_ref[pl.ds(plan.row(pos_ref, piece, rows), rows), :] = part


def turn(plan, pos_ref, from_ref, rows, put):
    for i, piece in enumerate(plan.order):
        put(i * rows, from_ref[pl.ds(plan.row(pos_ref, piece, rows), rows), :])


def pack_in(plan, in_weight, vec_t):
    rows = in_weight.shape[0]

    def kernel(pos_ref, w_ref, vec_ref, mlp_ref, qkv_ref):
        plane = pos_ref[3]
        gain = vec_ref[:, :1]

        def take(source, width):
            at = pl.ds(pl.multiple_of(source, PAIR), width)
            low = w_ref[:, at].astype(BF16).astype(F32)
            return (low * gain).astype(BF16)

        mlp_ref[...] = take(3 * D + plane * FH, FH)
        for pair in range(PAIRS):
            for which in range(3):
                to = pair * QKV + which * PAIR
                source = which * D + plane * DH + pair * PAIR
                qkv_ref[:, to : to + PAIR] = take(source, PAIR)
        qkv_ref[:, QW:] = vec_ref[...].astype(BF16)

    return pl.pallas_call(
        kernel,
        grid=(1,),
        in_specs=[smem(), whole(in_weight.shape), whole((rows, VEC))],
        out_specs=[whole((rows, FH)), whole((rows, QW + VEC))],
        out_shape=[
            jax.ShapeDtypeStruct((rows, FH), BF16),
            jax.ShapeDtypeStruct((rows, QW + VEC), BF16),
        ],
        compiler_params=params(16),
        cost_estimate=cost(2 * rows * 3 * D, 6 * rows * 7 * D),
        name="pack_in",
    )(plan.pos, in_weight, vec_t)


def split_out(plan, out_weight, rows):
    width = out_weight.shape[0]

    def kernel(w_ref, out_ref):
        full = w_ref[...].T.astype(BF16)
        for i in range(plan.n):
            out_ref[i] = full[i * rows : (i + 1) * rows]

    shape = (plan.n, rows, width)
    return pl.pallas_call(
        kernel,
        grid=(1,),
        in_specs=[whole(out_weight.shape)],
        out_specs=whole(shape),
        out_shape=jax.ShapeDtypeStruct(shape, BF16),
        compiler_params=params(16),
        cost_estimate=cost(0, 6 * width * D),
        name="split_out",
    )(out_weight)


def pack_out(plan, blocks):
    n, rows, width = blocks.shape

    def kernel(pos_ref, in_ref, out_ref, full_ref):
        plane = pos_ref[3]
        for i in range(n):
            full_ref[:, i * width : (i + 1) * width] = in_ref[i].astype(F32)
        mlp = full_ref[:, pl.ds(pl.multiple_of(D + plane * FH, PAIR), FH)]
        out_ref[:, :FH] = mlp.astype(BF16)
        heads = full_ref[:, pl.ds(pl.multiple_of(plane * DH, PAIR), DH)]
        out_ref[:, FH:] = heads.astype(BF16)

    return pl.pallas_call(
        kernel,
        grid=(1,),
        in_specs=[smem(), whole(blocks.shape)],
        out_specs=whole((rows, FH + DH)),
        out_shape=jax.ShapeDtypeStruct((rows, FH + DH), BF16),
        scratch_shapes=[pltpu.VMEM((rows, D + FF), F32)],
        compiler_params=params(16),
        cost_estimate=cost(rows * (D + FF), 6 * rows * D),
        name="pack_out",
    )(plan.pos, blocks)


def unpack_out(plan, own, swap):
    rows = own.shape[0]
    width = (D + FF) // plan.n

    def kernel(pos_ref, own_ref, swap_ref, out_ref, full_ref):
        first = pos_ref[3] == 0
        a, b = own_ref[...].astype(F32), swap_ref[...].astype(F32)
        for plane, part in enumerate((jnp.where(first, a, b), jnp.where(first, b, a))):
            full_ref[:, D + plane * FH : D + (plane + 1) * FH] = part[:, :FH]
            full_ref[:, plane * DH : (plane + 1) * DH] = part[:, FH:]
        for i in range(plan.n):
            out_ref[i] = full_ref[:, i * width : (i + 1) * width].astype(BF16)

    return pl.pallas_call(
        kernel,
        grid=(1,),
        in_specs=[smem(), whole(own.shape), whole(own.shape)],
        out_specs=whole((plan.n, rows, width)),
        out_shape=jax.ShapeDtypeStruct((plan.n, rows, width), BF16),
        scratch_shapes=[pltpu.VMEM((rows, D + FF), F32)],
        compiler_params=params(16),
        cost_estimate=cost(rows * (D + FF), 6 * rows * D),
        name="unpack_out",
    )(plan.pos, own, swap)


def stack(pieces):
    rows, width = pieces[0].shape

    def kernel(*refs):
        for i, ref in enumerate(refs[:-1]):
            refs[-1][i * rows : (i + 1) * rows, :] = ref[...]

    shape = (len(pieces) * rows, width)
    return pl.pallas_call(
        kernel,
        grid=(1,),
        in_specs=[whole((rows, width))] * len(pieces),
        out_specs=whole(shape),
        out_shape=jax.ShapeDtypeStruct(shape, BF16),
        compiler_params=params(8),
        cost_estimate=cost(0, 4 * shape[0] * width),
        name="stack",
    )(*pieces)


def fold(a):
    total = a[:, :PAIR]
    for i in range(1, a.shape[1] // PAIR):
        total = total + a[:, i * PAIR : (i + 1) * PAIR]
    return total


def partial_sums(plan, mlp, qkv, out, in_weight, vec_t):
    rows = in_weight.shape[0]

    def kernel(pos_ref, mlp_ref, qkv_ref, out_ref, w_ref, vec_ref, block_ref):
        plane = pos_ref[3]
        gain = vec_ref[:, :1]
        square = jnp.zeros((rows, PAIR), F32)
        dot = jnp.zeros((rows, PAIR), F32)

        def add(square, dot, hat, source, width):
            at = pl.ds(pl.multiple_of(source, PAIR), width)
            low = w_ref[:, at].astype(BF16).astype(F32)
            grad = hat * gain
            return square + fold(grad * grad), dot + fold(low * hat)

        hat = mlp_ref[:, :FH].astype(F32)
        square, dot = add(square, dot, hat, 3 * D + plane * FH, FH)
        for pair in range(PAIRS):
            for which in range(3):
                at = pair * QKV + which * PAIR
                hat = qkv_ref[:, at : at + PAIR].astype(F32)
                source = which * D + plane * DH + pair * PAIR
                square, dot = add(square, dot, hat, source, PAIR)
        value = out_ref[...].astype(F32)
        square = square + fold(value * value)
        lane = lax.broadcasted_iota(jnp.int32, (rows, VEC), 1)
        total = jnp.sum(dot, axis=1, keepdims=True)
        block_ref[:rows, :] = jnp.where(lane == 0, total, qkv_ref[:, QW:].astype(F32))
        square = jnp.sum(square, axis=0, keepdims=True) * 0.125
        block_ref[rows:, :] = jnp.broadcast_to(square, (8, PAIR))

    shape = (rows + 8, VEC)
    arrays = (mlp, qkv, out, in_weight, vec_t)
    return pl.pallas_call(
        kernel,
        grid=(1,),
        in_specs=[smem()] + [whole(a.shape) for a in arrays],
        out_specs=whole(shape),
        out_shape=jax.ShapeDtypeStruct(shape, F32),
        compiler_params=params(16),
        cost_estimate=cost(8 * rows * 6 * D, 14 * rows * 6 * D),
        name="partial_sums",
    )(plan.pos, *arrays)


def join_sums(own, swap):
    rows = own.shape[0] - 8

    def kernel(own_ref, swap_ref, vec_ref, total_ref):
        vec = own_ref[:rows, :] + swap_ref[:rows, :]
        vec_ref[...] = vec
        square = jnp.sum(vec * vec, axis=0, keepdims=True) * 0.125
        total_ref[...] = own_ref[rows:, :] + swap_ref[rows:, :] + jnp.broadcast_to(square, (8, VEC))

    return pl.pallas_call(
        kernel,
        grid=(1,),
        in_specs=[whole(own.shape)] * 2,
        out_specs=[whole((rows, VEC)), whole((8, VEC))],
        out_shape=[
            jax.ShapeDtypeStruct((rows, VEC), F32),
            jax.ShapeDtypeStruct((8, VEC), F32),
        ],
        compiler_params=params(16),
        cost_estimate=cost(4 * own.size, 12 * own.size),
        name="join_sums",
    )(own, swap)


def finish_out(blocks):
    n, rows, width = blocks.shape

    def kernel(in_ref, out_ref):
        out_ref[...] = in_ref[...].reshape(n * rows, width).astype(F32).T

    return pl.pallas_call(
        kernel,
        grid=(1,),
        in_specs=[whole(blocks.shape)],
        out_specs=whole((width, D)),
        out_shape=jax.ShapeDtypeStruct((width, D), F32),
        compiler_params=params(16),
        cost_estimate=cost(0, 6 * width * D),
        name="finish_out",
    )(blocks)


def finish_mlp(plan, own, swap, like, vec_t):
    rows = like.shape[0]

    def kernel(pos_ref, own_ref, swap_ref, vec_ref, grad_ref):
        mine = pl.program_id(0) // 2 == pos_ref[3]
        hat = jnp.where(mine, own_ref[...].astype(F32), swap_ref[...].astype(F32))
        grad_ref[...] = hat * vec_ref[:, :1]

    part = pl.BlockSpec((rows, D), lambda j: (0, j % 2))
    return pl.pallas_call(
        kernel,
        grid=(FF // D,),
        in_specs=[smem(), part, part, whole((rows, VEC))],
        out_specs=pl.BlockSpec((rows, D), lambda j: (0, 3 + j)),
        out_shape=jax.ShapeDtypeStruct(like.shape, F32),
        compiler_params=params(16),
        cost_estimate=cost(2 * rows * FF, 8 * rows * FF),
        name="finish_mlp",
    )(plan.pos, own, swap, vec_t)


def finish_qkv(plan, own, swap, vec_t, grad):
    rows = grad.shape[0]

    def kernel(pos_ref, own_ref, swap_ref, vec_ref, _, grad_ref):
        step = pl.program_id(0)
        first = pos_ref[3] == 0
        parts = []
        for pair in range(PAIRS):
            at = pl.ds(pl.multiple_of(pair * QKV + step * PAIR, PAIR), PAIR)
            parts.append([ref[:, at].astype(F32) for ref in (own_ref, swap_ref)])
        low = [jnp.where(first, a, b) for a, b in parts]
        high = [jnp.where(first, b, a) for a, b in parts]
        grad_ref[...] = jnp.concatenate(low + high, axis=1) * vec_ref[:, :1]

    return pl.pallas_call(
        kernel,
        grid=(3,),
        in_specs=[
            smem(),
            whole(own.shape),
            whole(own.shape),
            whole((rows, VEC)),
            pl.BlockSpec(memory_space=pl.ANY),
        ],
        out_specs=pl.BlockSpec((rows, D), lambda j: (0, j)),
        out_shape=jax.ShapeDtypeStruct(grad.shape, F32),
        input_output_aliases={4: 0},
        compiler_params=params(16),
        cost_estimate=cost(6 * rows * D, 24 * rows * D),
        name="finish_qkv",
    )(plan.pos, own, swap, vec_t, grad)


def prepare(plan, tokens, other_tokens, cotangent, other_cotangent, rows):
    tok = tokens.shape[0]
    kind = row_type(rows)

    def kernel(pos_ref, to_ref, tp_ref, co_ref, cp_ref, xo_ref, xp_ref, turned_ref, sum_ref, t_ref):
        for half, (from_ref, cot_ref, x_ref) in enumerate(
            ((to_ref, co_ref, xo_ref), (tp_ref, cp_ref, xp_ref))
        ):
            values = from_ref[...].astype(F32)
            centre = values - jnp.mean(values, axis=-1, keepdims=True)
            r = lax.rsqrt(jnp.mean(centre * centre, axis=-1, keepdims=True) + norm_eps)
            normal = centre * r
            x_ref[...] = normal.astype(BF16)
            cot = cot_ref[...].astype(F32)
            if half == 0:
                total = jnp.sum(cot, axis=0, keepdims=True)
                sum_ref[...] = jnp.broadcast_to(total, (8, D))
            for which, value in enumerate((normal, cot)):
                t_ref[...] = value.T.astype(kind)

                def put(at, a):
                    columns = slice(half * tok, (half + 1) * tok)
                    turned_ref[which, at : at + rows, columns] = a.astype(BF16)

                turn(plan, pos_ref, t_ref, rows, put)

    low = jax.ShapeDtypeStruct((tok, D), BF16)
    return pl.pallas_call(
        kernel,
        grid=(1,),
        in_specs=[smem()] + [whole((tok, D))] * 4,
        out_specs=[whole((tok, D))] * 2 + [whole((2, D, 2 * tok)), whole((8, D))],
        out_shape=[
            low,
            low,
            jax.ShapeDtypeStruct((2, D, 2 * tok), BF16),
            jax.ShapeDtypeStruct((8, D), F32),
        ],
        scratch_shapes=[pltpu.VMEM((D, tok), kind)],
        compiler_params=params(),
        cost_estimate=cost(40 * tok * D, 20 * tok * D),
        name="prepare",
    )(plan.pos, tokens, other_tokens, cotangent, other_cotangent)


def mlp_forward(plan, x_own, x_other, turned, pieces):
    tok = x_own.shape[0]
    rows = pieces[0].shape[0] // plan.zs
    tile = 512
    n = len(pieces)

    half_d = D // 2

    def kernel(pos_ref, xo_ref, xp_ref, ct_ref, *rest):
        refs, (mix_ref, slope_ref, g_own_ref, g_other_ref, w_ref) = rest[:n], rest[n:]
        place(plan, pos_ref, refs, rows, w_ref)
        w = w_ref[...].astype(BF16)
        for half, x_ref in enumerate((xo_ref, xp_ref)):
            v = mm(x_ref[...], w)
            v2 = v * v
            t = jnp.tanh(v * (GELU_C + (GELU_C * 0.044715) * v2))
            h = 0.5 + 0.5 * t
            g = v * h
            slope = h + 2.0 * g * (1.0 - h) * (GELU_C + (3.0 * GELU_C * 0.044715) * v2)
            mix_ref[half] = g.astype(BF16)
            slope_ref[half] = slope.astype(BF16)
        g = mm(ct_ref[0], mix_ref[...].reshape(2 * tok, tile)).astype(BF16)
        g_own_ref[...] = g[:half_d]
        g_other_ref[...] = g[half_d:]

    block = pl.BlockSpec((2, tok, tile), lambda j: (0, 0, j))
    grad = pl.BlockSpec((half_d, tile), lambda j: (0, j))
    return pl.pallas_call(
        kernel,
        grid=(FH // tile,),
        in_specs=[smem()]
        + [whole((tok, D))] * 2
        + [pl.BlockSpec((1, D, 2 * tok), lambda j: (1, 0, 0))]
        + [pl.BlockSpec((plan.zs * rows, tile), lambda j: (0, j))] * n,
        out_specs=[block, block, grad, grad],
        out_shape=[jax.ShapeDtypeStruct((2, tok, FH), BF16)] * 2
        + [jax.ShapeDtypeStruct((half_d, FH + DH), BF16)] * 2,
        scratch_shapes=[pltpu.VMEM((D, tile), row_type(rows))],
        compiler_params=params(),
        cost_estimate=cost(8 * tok * D * FH, 12 * tok * FH, 2 * tok * FH),
        name="mlp_forward",
    )(plan.pos, x_own, x_other, turned, *pieces)


def head_means(a, block_ref):
    high = a.astype(BF16)
    low = (a - high.astype(F32)).astype(BF16)
    return mm(high, block_ref[...]) + mm(low, block_ref[...])


def attention_forward(plan, x_own, x_other, pieces, ids, block, turned, g_own, g_other):
    tok = x_own.shape[0]
    rows = pieces[0].shape[0] // plan.zs
    n = len(pieces)
    half_d = D // 2

    def kernel(pos_ref, xo_ref, xp_ref, ido_ref, idp_ref, block_ref, ct_ref, _, __, *rest):
        refs, vec_refs = rest[:n], rest[n : 2 * n]
        (
            qk_ref, v_ref, n_ref, r_ref, att_ref, p_ref, gain_ref, g_own_ref, g_other_ref,
            w_ref, vs_ref, all_ref,
        ) = rest[2 * n :]
        step = pl.program_id(0)

        @pl.when(step == 0)
        def _():
            place(plan, pos_ref, vec_refs, rows, vs_ref)
            gain_ref[...] = vs_ref[...].astype(F32).T[:8]

        place(plan, pos_ref, refs, rows, w_ref)
        w = w_ref[...].astype(BF16)
        column = pl.ds(pl.multiple_of(pos_ref[3] * DH + step * PAIR, PAIR), PAIR)
        gain = jnp.concatenate(
            [gain_ref[1:2, column] * (HD ** (-0.5)), gain_ref[2:3, column]], axis=1
        )
        first = lax.broadcasted_iota(jnp.int32, (tok, PAIR), 1) < HD
        for half, x_ref in enumerate((xo_ref, xp_ref)):
            raw = mm(x_ref[...], w)
            qk = raw[:, : 2 * PAIR]
            centre = qk - head_means(qk, block_ref)
            r = lax.rsqrt(mm((centre * centre).astype(BF16), block_ref[...]) + norm_eps)
            normal = centre * r
            n_ref[half] = normal.astype(BF16)
            r_ref[half] = r.astype(BF16)
            low = (normal * gain).astype(BF16)
            qk_ref[half] = low
            q, k = low[:, :PAIR], low[:, PAIR:]
            v = raw[:, 2 * PAIR :].astype(BF16)
            v_ref[half] = v
            number = (ido_ref, idp_ref)[half][...].astype(F32)
            same = jnp.broadcast_to(number, (8, tok)).T[:, :1] == number
            att = []
            zero = jnp.zeros_like(q)
            for head in range(2):
                qh = jnp.where(first, q, zero) if head == 0 else jnp.where(first, zero, q)
                e = jnp.where(same, jnp.exp(mm(qh, k, NT)), 0.0)
                p = (e * (1.0 / jnp.sum(e, axis=1, keepdims=True))).astype(BF16)
                p_ref[half, head] = p
                att.append(mm(p, v))
            att_low = jnp.where(first, att[0], att[1]).astype(BF16)
            att_ref[half] = att_low
            at = pl.ds(pl.multiple_of(step * PAIR, PAIR), PAIR)
            all_ref[half * tok : (half + 1) * tok, at] = att_low

        @pl.when(step == PAIRS - 1)
        def _():
            g = mm(ct_ref[0], all_ref[...]).astype(BF16)
            g_own_ref[...] = g[:half_d]
            g_other_ref[...] = g[half_d:]

    pair = pl.BlockSpec((2, tok, PAIR), lambda j: (0, 0, j))
    pair2 = pl.BlockSpec((2, tok, 2 * PAIR), lambda j: (0, 0, j))
    small = jax.ShapeDtypeStruct((2, tok, DH), BF16)
    small2 = jax.ShapeDtypeStruct((2, tok, 2 * DH), BF16)
    heads = pl.BlockSpec((half_d, DH), lambda j: (0, FH // DH))
    return pl.pallas_call(
        kernel,
        grid=(PAIRS,),
        in_specs=[smem()]
        + [whole((tok, D))] * 2
        + [whole((1, tok))] * 2
        + [whole((2 * PAIR, 2 * PAIR))]
        + [pl.BlockSpec((1, D, 2 * tok), lambda j: (1, 0, 0))]
        + [pl.BlockSpec(memory_space=pl.ANY)] * 2
        + [pl.BlockSpec((plan.zs * rows, QKV), lambda j: (0, j))] * n
        + [pl.BlockSpec((plan.zs * rows, VEC), lambda j: (0, QW // VEC))] * n,
        out_specs=[pair2, pair, pair2, pair2, pair]
        + [pl.BlockSpec((2, 2, tok, tok), lambda j: (0, j, 0, 0)), whole((8, D))]
        + [heads, heads],
        out_shape=[small2, small, small2, small2, small]
        + [
            jax.ShapeDtypeStruct((2, 2 * PAIRS, tok, tok), BF16),
            jax.ShapeDtypeStruct((8, D), F32),
            jax.ShapeDtypeStruct(g_own.shape, BF16),
            jax.ShapeDtypeStruct(g_own.shape, BF16),
        ],
        input_output_aliases={7: 7, 8: 8},
        scratch_shapes=[
            pltpu.VMEM((D, QKV), row_type(rows)),
            pltpu.VMEM((D, VEC), row_type(rows)),
            pltpu.VMEM((2 * tok, DH), BF16),
        ],
        compiler_params=params(),
        cost_estimate=cost(4 * tok * D * QW, 20 * MIB, 12 * tok * tok),
        name="attention_forward",
    )(
        plan.pos, x_own, x_other, *ids, block, turned, g_own, g_other, *pieces, *pieces,
    )


TILE = 256


def token_tiles(tok):
    per = tok // TILE

    def pair(j):
        return (j // per, j % per, 0)

    def own(j):
        return jnp.minimum(j, per - 1)

    def other(j):
        return jnp.maximum(j - per, 0)

    return per, pair, own, other


def output_step(plan, att, mixed, slope, cot_own, cot_other, pieces):
    tok = cot_own.shape[0]
    rows = pieces[0].shape[0] // plan.zs
    n = len(pieces)
    per, pair, own, other = token_tiles(tok)

    def kernel(pos_ref, att_ref, mix_ref, slope_ref, co_ref, cp_ref, *rest):
        refs = rest[:n]
        out_own_ref, out_other_ref, d_att_ref, d_in_ref, w_ref = rest[n:]
        step = pl.program_id(0)

        @pl.when(step == 0)
        def _():
            place(plan, pos_ref, refs, rows, w_ref)

        w = w_ref[...].astype(BF16)
        cot = jnp.where(step < per, co_ref[...], cp_ref[...])
        for at in range(0, FH, DH):
            d = mm(cot, w[:, at : at + DH])
            slopes = slope_ref[0, :, at : at + DH].astype(F32)
            d_in_ref[0, :, at : at + DH] = (d * slopes).astype(BF16)
        d_att_ref[0] = mm(cot, w[:, FH:]).astype(BF16)
        out = mm(mix_ref[0], w[:, :FH], NT) + mm(att_ref[0], w[:, FH:], NT)

        @pl.when(step < per)
        def _():
            out_own_ref[...] = out

        @pl.when(step >= per)
        def _():
            out_other_ref[...] = out.astype(BF16)

    return pl.pallas_call(
        kernel,
        grid=(2 * per,),
        in_specs=[
            smem(),
            pl.BlockSpec((1, TILE, DH), pair),
            pl.BlockSpec((1, TILE, FH), pair),
            pl.BlockSpec((1, TILE, FH), pair),
            pl.BlockSpec((TILE, D), lambda j: (own(j), 0)),
            pl.BlockSpec((TILE, D), lambda j: (other(j), 0)),
        ]
        + [whole(pieces[0].shape)] * n,
        out_specs=[
            pl.BlockSpec((TILE, D), lambda j: (own(j), 0)),
            pl.BlockSpec((TILE, D), lambda j: (other(j), 0)),
            pl.BlockSpec((1, TILE, DH), pair),
            pl.BlockSpec((1, TILE, FH), pair),
        ],
        out_shape=[
            jax.ShapeDtypeStruct((tok, D), F32),
            jax.ShapeDtypeStruct((tok, D), BF16),
            jax.ShapeDtypeStruct((2, tok, DH), BF16),
            jax.ShapeDtypeStruct((2, tok, FH), BF16),
        ],
        scratch_shapes=[pltpu.VMEM((D, FH + DH), row_type(rows))],
        compiler_params=params(40),
        cost_estimate=cost(8 * tok * (FH + DH) * D, 20 * MIB),
        name="output_step",
    )(plan.pos, att, mixed, slope, cot_own, cot_other, *pieces)


def mlp_gradient(turned, d_inner):
    tok = d_inner.shape[1]
    half_d = D // 2
    tile = 512

    def kernel(xt_ref, d_ref, g_own_ref, g_other_ref):
        g = mm(xt_ref[0], d_ref[...].reshape(2 * tok, tile)).astype(BF16)
        g_own_ref[...] = g[:half_d]
        g_other_ref[...] = g[half_d:]

    grad = pl.BlockSpec((half_d, tile), lambda j: (0, j))
    return pl.pallas_call(
        kernel,
        grid=(FH // tile,),
        in_specs=[
            pl.BlockSpec((1, D, 2 * tok), lambda j: (0, 0, 0)),
            pl.BlockSpec((2, tok, tile), lambda j: (0, 0, j)),
        ],
        out_specs=[grad, grad],
        out_shape=[jax.ShapeDtypeStruct((half_d, FH), BF16)] * 2,
        compiler_params=params(40),
        cost_estimate=cost(4 * tok * D * FH, 8 * MIB),
        name="mlp_gradient",
    )(turned, d_inner)


def scaled_gradient(plan, d_inner, d_qkv, mlp_pieces, qkv_pieces):
    tok = d_inner.shape[1]
    rows = mlp_pieces[0].shape[0] // plan.zs
    n = len(mlp_pieces)
    per, pair, own, other = token_tiles(tok)

    def kernel(pos_ref, dm_ref, dq_ref, *rest):
        refs_m, refs_q = rest[:n], rest[n : 2 * n]
        e_own_ref, e_other_ref, wm_ref, wq_ref = rest[2 * n :]
        step = pl.program_id(0)

        @pl.when(step == 0)
        def _():
            place(plan, pos_ref, refs_m, rows, wm_ref)
            place(plan, pos_ref, refs_q, rows, wq_ref)

        e = mm(dm_ref[0], wm_ref[...].astype(BF16), NT)
        e = e + mm(dq_ref[0], wq_ref[...].astype(BF16)[:, :QW], NT)

        @pl.when(step < per)
        def _():
            e_own_ref[...] = e

        @pl.when(step >= per)
        def _():
            e_other_ref[...] = e.astype(BF16)

    return pl.pallas_call(
        kernel,
        grid=(2 * per,),
        in_specs=[
            smem(),
            pl.BlockSpec((1, TILE, FH), pair),
            pl.BlockSpec((1, TILE, QW), pair),
        ]
        + [whole(mlp_pieces[0].shape)] * n
        + [whole(qkv_pieces[0].shape)] * n,
        out_specs=[
            pl.BlockSpec((TILE, D), lambda j: (own(j), 0)),
            pl.BlockSpec((TILE, D), lambda j: (other(j), 0)),
        ],
        out_shape=[
            jax.ShapeDtypeStruct((tok, D), F32),
            jax.ShapeDtypeStruct((tok, D), BF16),
        ],
        scratch_shapes=[
            pltpu.VMEM((D, FH), row_type(rows)),
            pltpu.VMEM((D, QW + VEC), row_type(rows)),
        ],
        compiler_params=params(48),
        cost_estimate=cost(4 * tok * (FH + QW) * D, 16 * MIB),
        name="scaled_gradient",
    )(plan.pos, d_inner, d_qkv, *mlp_pieces, *qkv_pieces)


def attention_backward(plan, turned, saved, d_att, block, gains, cot_sum, rows):
    qk, v, normals, factors, probs = saved
    tok = d_att.shape[1]
    half_d = D // 2
    kind = row_type(rows)

    def kernel(pos_ref, xt_ref, qk_ref, v_ref, n_ref, r_ref, p_ref, da_ref, block_ref, gain_ref,
               cot_ref, g_own_ref, g_other_ref, d_ref, vec_ref, turn_ref):
        step = pl.program_id(0)

        @pl.when(step == 0)
        def _():
            vec_ref[...] = jnp.zeros_like(vec_ref)
            vec_ref[3:4, :] = cot_ref[:1]

        column = pl.ds(pl.multiple_of(pos_ref[3] * DH + step * PAIR, PAIR), PAIR)
        gain = jnp.concatenate(
            [gain_ref[1:2, column] * (HD ** (-0.5)), gain_ref[2:3, column]], axis=1
        )
        first = lax.broadcasted_iota(jnp.int32, (tok, PAIR), 1) < HD

        def heads(a):
            zero = jnp.zeros_like(a)
            return jnp.concatenate([jnp.where(first, a, zero), jnp.where(first, zero, a)], axis=0)

        for half in range(2):
            qb, kb, vb = qk_ref[half, :, :PAIR], qk_ref[half, :, PAIR:], v_ref[half]
            da = heads(da_ref[half])
            p_low = p_ref[half].reshape(2 * tok, tok)
            p = p_low.astype(F32)
            t = p * mm(da, vb, NT)
            ds = (t - p * jnp.sum(t, axis=1, keepdims=True)).astype(BF16)
            d_value = mm(da.T, p_low).T
            d_key = mm(heads(qb).T, ds).T
            dq = mm(ds, kb)
            d_query = jnp.where(first, dq[:tok], dq[tok:])
            d = jnp.concatenate([d_query, d_key], axis=1)
            normal = n_ref[half].astype(F32)
            sums = jnp.sum(d * normal, axis=0, keepdims=True)
            vec_ref[1:2, column] += sums[:, :PAIR] * (HD ** (-0.5))
            vec_ref[2:3, column] += sums[:, PAIR:]
            e = d * gain
            along = mm((e * normal).astype(BF16), block_ref[...])
            d_raw = r_ref[half].astype(F32) * (e - head_means(e, block_ref) - normal * along)
            d_ref[half, :, : 2 * PAIR] = d_raw.astype(BF16)
            d_ref[half, :, 2 * PAIR :] = d_value.astype(BF16)
        g = mm(xt_ref[0], d_ref[...].reshape(2 * tok, QKV)).astype(BF16)
        at = pl.ds(pl.multiple_of(step * QKV, QKV), QKV)
        g_own_ref[:, at] = g[:half_d]
        g_other_ref[:, at] = g[half_d:]

        @pl.when(step == PAIRS - 1)
        def _():
            turn_ref[...] = vec_ref[...].T.astype(kind)

            def put(at, a):
                ref = g_own_ref if at < half_d else g_other_ref
                ref[at % half_d : at % half_d + rows, QW:] = a.astype(BF16)

            turn(plan, pos_ref, turn_ref, rows, put)

    pair = pl.BlockSpec((2, tok, PAIR), lambda j: (0, 0, j))
    pair2 = pl.BlockSpec((2, tok, 2 * PAIR), lambda j: (0, 0, j))
    return pl.pallas_call(
        kernel,
        grid=(PAIRS,),
        in_specs=[smem(), pl.BlockSpec((1, D, 2 * tok), lambda j: (0, 0, 0))]
        + [pair2, pair, pair2, pair2]
        + [
            pl.BlockSpec((2, 2, tok, tok), lambda j: (0, j, 0, 0)),
            pair,
            whole((2 * PAIR, 2 * PAIR)),
            whole((8, D)),
            whole((8, D)),
        ],
        out_specs=[whole((half_d, QW + VEC))] * 2
        + [pl.BlockSpec((2, tok, QKV), lambda j: (0, 0, j))],
        out_shape=[jax.ShapeDtypeStruct((half_d, QW + VEC), BF16)] * 2
        + [jax.ShapeDtypeStruct((2, tok, QW), BF16)],
        scratch_shapes=[pltpu.VMEM((VEC, D), F32), pltpu.VMEM((D, VEC), kind)],
        compiler_params=params(48),
        cost_estimate=cost(16 * tok * D * QW, 24 * MIB),
        name="attention_backward",
    )(plan.pos, turned, qk, v, normals, factors, probs, d_att, block, gains, cot_sum)


def token_gradient(tokens, cotangent, e_own, e_recv):
    tok = tokens.shape[0]

    def kernel(t_ref, c_ref, own_ref, recv_ref, out_ref):
        rows = t_ref[...].astype(F32)
        centre = rows - jnp.mean(rows, axis=-1, keepdims=True)
        r = lax.rsqrt(jnp.mean(centre * centre, axis=-1, keepdims=True) + norm_eps)
        normal = centre * r
        e = own_ref[...] + recv_ref[...].astype(F32)
        mean = jnp.mean(e, axis=-1, keepdims=True)
        along = jnp.mean(e * normal, axis=-1, keepdims=True)
        out_ref[...] = c_ref[...].astype(F32) + r * (e - mean - normal * along)

    block = pl.BlockSpec((tok // 4, D), lambda j: (j, 0))
    return pl.pallas_call(
        kernel,
        grid=(4,),
        in_specs=[block] * 4,
        out_specs=block,
        out_shape=jax.ShapeDtypeStruct((tok, D), F32),
        compiler_params=params(16),
        cost_estimate=cost(20 * tok * D, 14 * tok * D),
        name="token_gradient",
    )(tokens, cotangent, e_own, e_recv)


def adamw(master, first, second, grad, factor):
    clipped = grad * factor
    first_new = beta_one * first + (1.0 - beta_one) * clipped
    second_new = beta_two * second + (1.0 - beta_two) * clipped * clipped
    first_hat = first_new * (1.0 / (1.0 - beta_one**ADAM_STEP))
    second_hat = second_new * (1.0 / (1.0 - beta_two**ADAM_STEP))
    update = -learning * (first_hat / (jnp.sqrt(second_hat) + epsilon) + decay_rate * master)
    return (update, first_new, second_new)


def optimize(total, vec_cols, ins, outs, vecs):
    rows, out_rows = ins[0].shape[0], outs[0].shape[0]
    steps = 3

    def kernel(total_ref, cols_ref, *refs):
        in_refs, out_refs, vec_refs, rest = refs[:4], refs[4:8], refs[8:11], refs[11:]
        vec_grad_ref, norm_ref, pad_ref = rest[0], rest[1], rest[-1]
        sums = jnp.sum(jnp.sum(total_ref[...], axis=1, keepdims=True), axis=0, keepdims=True)
        norm = jnp.sqrt(sums)
        factor = jnp.minimum(1.0, math.sqrt(PARAMS) / norm)
        for group, results in ((in_refs, rest[2:5]), (out_refs, rest[5:8])):
            for ref, value in zip(results, adamw(*[ref[...] for ref in group], factor)):
                ref[...] = value

        @pl.when(pl.program_id(0) == 0)
        def _():
            norm_ref[...] = norm
            pad_ref[...] = jnp.zeros_like(pad_ref)
            pad_ref[:rows] = cols_ref[...]
            grad = pad_ref[...].T[:4, :rows]
            vec_grad_ref[...] = grad
            values = adamw(*[ref[...] for ref in vec_refs], grad, factor)
            for ref, value in zip(rest[8:11], values):
                ref[...] = value

    in_block = pl.BlockSpec((rows, 7 * D // steps), lambda j: (0, j))
    out_block = pl.BlockSpec((out_rows // steps, D), lambda j: (j, 0))
    shapes = [jax.ShapeDtypeStruct(a.shape, F32) for a in (ins[0], outs[0], vecs[0])]
    return pl.pallas_call(
        kernel,
        grid=(steps,),
        in_specs=[whole((8, 128)), whole(vec_cols.shape)]
        + [in_block] * 4
        + [out_block] * 4
        + [whole(vecs[0].shape)] * 3,
        out_specs=[whole(vecs[0].shape), whole((1, 1))]
        + [in_block] * 3
        + [out_block] * 3
        + [whole(vecs[0].shape)] * 3,
        out_shape=[shapes[2], jax.ShapeDtypeStruct((1, 1), F32)]
        + [shapes[0]] * 3
        + [shapes[1]] * 3
        + [shapes[2]] * 3,
        scratch_shapes=[pltpu.VMEM((128, 128), F32)],
        compiler_params=params(16),
        cost_estimate=cost(20 * 7 * D * rows, 28 * 13 * D * rows),
        name="optimize",
    )(total, vec_cols, *ins, *outs, *vecs)


def local(
    tokens,
    cotangent,
    image_ids,
    in_weight,
    out_weight,
    vectors,
    in_moment,
    out_moment,
    vec_moment,
    in_second,
    out_second,
    vec_second,
):
    plan = Plan(lax.axis_size("fsdp"), lax.axis_size("dp"))
    rows = in_weight.shape[0]

    low_vec = vectors.astype(BF16).astype(F32)
    vec_t = jnp.pad(low_vec.T, ((0, 0), (0, VEC - 4)))
    mlp_piece, qkv_piece = pack_in(plan, in_weight, vec_t)
    other_tokens = plan.swap_plane(tokens)
    other_cotangent = plan.swap_plane(cotangent)
    blocks = lax.all_to_all(split_out(plan, out_weight, rows), "fsdp", 0, 0)

    def z_all(piece):
        return [plan.from_z(piece, s) for s in range(1, plan.zs)]

    def y_all(column):
        return [plan.from_y(column, t) for t in range(1, plan.ys)]

    def core_all(arrays):
        return [plan.swap_core(a) for a in arrays]

    def held(groups):
        flat = iter(fence(*[a for group in groups for a in group]))
        return [[next(flat) for _ in group] for group in groups]

    mlp_z = z_all(mlp_piece)
    mlp_z, (qkv_piece,) = held([mlp_z, [qkv_piece]])
    mlp_col = stack([mlp_piece] + mlp_z)
    mlp_y = y_all(mlp_col)
    qkv_z = z_all(qkv_piece)
    out_piece = pack_out(plan, blocks)
    x_own, x_other, turned, cot_sum = prepare(
        plan, tokens, other_tokens, cotangent, other_cotangent, rows
    )
    mlp_y, qkv_z, (mlp_col, out_piece, x_own) = held(
        [mlp_y, qkv_z, [mlp_col, out_piece, x_own]]
    )
    mlp_pieces = [mlp_col] + mlp_y + core_all([mlp_col] + mlp_y)
    qkv_col = stack([qkv_piece] + qkv_z)
    qkv_y = y_all(qkv_col)
    out_z = z_all(out_piece)
    mixed, slope, g_own, g_other = mlp_forward(plan, x_own, x_other, turned, mlp_pieces)
    qkv_y, out_z, (qkv_col, mixed, slope, g_own, g_other, ids_now) = held(
        [qkv_y, out_z, [qkv_col, mixed, slope, g_own, g_other, image_ids]]
    )
    other_ids = plan.swap_plane(ids_now)
    qkv_pieces = [qkv_col] + qkv_y + core_all([qkv_col] + qkv_y)
    out_col = stack([out_piece] + out_z)
    out_y = y_all(out_col)
    out_core = core_all([out_col])
    lane = np.arange(2 * PAIR) // HD
    block = jnp.asarray(np.where(lane[:, None] == lane[None, :], 1.0 / HD, 0.0), BF16)
    *saved, att, probs, gains, g_own, g_other = attention_forward(
        plan, x_own, x_other, qkv_pieces, (image_ids[None, :], other_ids[None, :]), block,
        turned, g_own, g_other,
    )
    saved = tuple(saved) + (probs,)
    out_y, out_core, (att, g_own, g_other) = held([out_y, out_core, [att, g_own, g_other]])
    s_out = Scatter(plan, g_own, g_other)
    s_out.by_core()
    out_core = out_core + core_all(out_y)
    s_out.recv, *out_core = fence(s_out.recv, *out_core)
    s_out.by_y()
    out_pieces = [out_col] + out_y + out_core
    out_mine, out_theirs, d_att, d_inner = output_step(
        plan, att, mixed, slope, cotangent, other_cotangent, out_pieces
    )
    g_own, g_other = mlp_gradient(turned, d_inner)
    s_mlp = Scatter(plan, g_own, g_other)
    s_mlp.by_core()
    s_out.y_got, (out_theirs, g_own) = held([s_out.y_got, [out_theirs, g_own]])
    s_out.by_z()
    out_recv = plan.swap_plane(out_theirs)
    s_mlp.recv, d_att = fence(s_mlp.recv, d_att)
    s_mlp.by_y()
    g_own, g_other, d_qkv = attention_backward(
        plan, turned, saved, d_att, block, gains, cot_sum, rows
    )
    s_out.z_got, s_mlp.y_got, (g_own, g_other, d_qkv, out_recv) = held(
        [s_out.z_got, s_mlp.y_got, [g_own, g_other, d_qkv, out_recv]]
    )
    s_qkv = Scatter(plan, g_own, g_other)
    s_qkv.by_core()
    out_sum = s_out.total()
    out_swap = plan.swap_plane(out_sum)
    parts, s_mlp.y_got, (out_sum, d_qkv) = held([s_qkv.y_parts(), s_mlp.y_got, [out_sum, d_qkv]])
    s_qkv.by_y(parts)
    s_mlp.by_z()
    e_own, e_other = scaled_gradient(plan, d_inner, d_qkv, mlp_pieces, qkv_pieces)
    out_swap, e_other, e_own = fence(out_swap, e_other, e_own)
    e_recv = plan.swap_plane(e_other)
    blocks = unpack_out(plan, plan.over_pairs(out_sum), plan.over_pairs(out_swap))
    s_qkv.y_got, s_mlp.z_got, (blocks,) = held([s_qkv.y_got, s_mlp.z_got, [blocks]])
    s_qkv.by_z()
    blocks = lax.all_to_all(blocks, "fsdp", 0, 0)
    result = (
        tokens.astype(F32) + out_mine + out_recv.astype(F32) + gains[3][None, :]
    ).astype(BF16)
    mlp_sum = s_mlp.total()
    mlp_swap = plan.swap_plane(mlp_sum)
    s_qkv.z_got, (result,) = held([s_qkv.z_got, [result]])
    qkv_sum = plan.over_pairs(s_qkv.total())
    mlp_sum, out_sum = plan.over_pairs(mlp_sum), plan.over_pairs(out_sum)
    own = partial_sums(plan, mlp_sum, qkv_sum, out_sum, in_weight, vec_t)
    swap = plan.swap_plane(own)
    input_grad = token_gradient(tokens, cotangent, e_own, e_recv)
    swap, qkv_sum, mlp_swap, input_grad = fence(swap, qkv_sum, mlp_swap, input_grad)
    vec_cols, square = join_sums(own, swap)
    qkv_swap = plan.swap_plane(qkv_sum)
    in_grad = finish_mlp(plan, mlp_sum, plan.over_pairs(mlp_swap), in_weight, vec_t)
    out_grad = finish_out(blocks)
    total, out_grad, _, in_grad = plan.total(
        square, out_grad, in_grad, lambda a: finish_qkv(plan, qkv_sum, qkv_swap, vec_t, a)
    )
    vec_grad, norm, *updates = optimize(
        total,
        vec_cols,
        (in_weight, in_moment, in_second, in_grad),
        (out_weight, out_moment, out_second, out_grad),
        (vectors, vec_moment, vec_second),
    )
    in_update, in_mean, in_square = updates[:3]
    out_update, out_mean, out_square = updates[3:6]
    vec_update, vec_mean, vec_square = updates[6:]
    return (
        result,
        input_grad,
        in_grad,
        out_grad,
        vec_grad,
        norm.reshape(()),
        in_update,
        out_update,
        vec_update,
        in_mean,
        out_mean,
        vec_mean,
        in_square,
        out_square,
        vec_square,
    )


def solution(mesh):
    in_specs = (
        P(("dp", "fsdp"), None),
        P(("dp", "fsdp"), None),
        P(("dp", "fsdp")),
        P("fsdp", None),
        P("fsdp", None),
        P(None, "fsdp"),
        P("fsdp", None),
        P("fsdp", None),
        P(None, "fsdp"),
        P("fsdp", None),
        P("fsdp", None),
        P(None, "fsdp"),
    )
    out_specs = (
        P(("dp", "fsdp"), None),
        P(("dp", "fsdp"), None),
        P("fsdp", None),
        P("fsdp", None),
        P(None, "fsdp"),
        P(),
        P("fsdp", None),
        P("fsdp", None),
        P(None, "fsdp"),
        P("fsdp", None),
        P("fsdp", None),
        P(None, "fsdp"),
        P("fsdp", None),
        P("fsdp", None),
        P(None, "fsdp"),
    )
    return jax.shard_map(local, mesh=mesh, in_specs=in_specs, out_specs=out_specs, check_vma=False)
```
